32 devices in a mesh: dp: 8 (over z, x), fsdp: 4 (over y, core).
Axes of the slice: x: 2, y: 2, z: 4, core: 2. Of those that a mesh axis runs over, the one named last changes fastest.
Arguments:
- first_half: float32 [2, 8, 1280, 1024], P(None, 'dp', 'fsdp'), may hold values from -6 to 6
- second_half: float32 [2, 8, 1280, 1024], P(None, 'dp', 'fsdp'), may hold values from -6 to 6
- grad_first: float32 [2, 8, 1280, 1024], P(None, 'dp', 'fsdp'), may hold values from -6 to 6
- grad_second: float32 [2, 8, 1280, 1024], P(None, 'dp', 'fsdp'), may hold values from -6 to 6
- query_weight: bfloat16 [1024, 1024], P(('dp', 'fsdp')), may hold values from -0.1875 to 0.1875
- value_weight: bfloat16 [1024, 1024], P(('dp', 'fsdp')), may hold values from -0.1875 to 0.1875
- output_weight: bfloat16 [1024, 1024], P(('dp', 'fsdp')), may hold values from -1.5 to 1.5
- inner_weight: bfloat16 [1024, 4096], P(('dp', 'fsdp')), may hold values from -0.1875 to 0.1875
- inner_bias: bfloat16 [4096], P(('dp', 'fsdp')), may hold values from -3 to 3
- outer_weight: bfloat16 [4096, 1024], P(('dp', 'fsdp')), may hold values from -0.09375 to 0.09375
- outer_bias: bfloat16 [1024], P(('dp', 'fsdp')), may hold values from -2 to 2
- mixer_gain: bfloat16 [1024], P(('dp', 'fsdp')), may hold values from 0.5 to 1.5
- mixer_shift: bfloat16 [1024], P(('dp', 'fsdp')), may hold values from -2 to 2
- feed_gain: bfloat16 [1024], P(('dp', 'fsdp')), may hold values from 0.5 to 1.5
- feed_shift: bfloat16 [1024], P(('dp', 'fsdp')), may hold values from -2 to 2
- parents: int32 [2, 8, 10], P(None, 'dp'), may hold values from 0 to 5, as said below
- buckets: int32 [2, 8, 4, 1280], P(None, 'dp'), may hold values from 0 to 31
- order: int32 [2, 8, 4, 1280], P(None, 'dp'), may hold values from 0 to 1279, as said below
Outputs:
- first_out: float32 [2, 8, 1280, 1024], P(None, 'dp', 'fsdp')
- second_out: float32 [2, 8, 1280, 1024], P(None, 'dp', 'fsdp')
- grad_first_in: float32 [2, 8, 1280, 1024], P(None, 'dp', 'fsdp')
- grad_second_in: float32 [2, 8, 1280, 1024], P(None, 'dp', 'fsdp')
- query_grad: float32 [1024, 1024], P(('dp', 'fsdp'))
- value_grad: float32 [1024, 1024], P(('dp', 'fsdp'))
- output_grad: float32 [1024, 1024], P(('dp', 'fsdp'))
- inner_grad: float32 [1024, 4096], P(('dp', 'fsdp'))
- inner_bias_grad: float32 [4096], P(('dp', 'fsdp'))
- outer_grad: float32 [4096, 1024], P(('dp', 'fsdp'))
- outer_bias_grad: float32 [1024], P(('dp', 'fsdp'))
- mixer_gain_grad: float32 [1024], P(('dp', 'fsdp'))
- mixer_shift_grad: float32 [1024], P(('dp', 'fsdp'))
- feed_gain_grad: float32 [1024], P(('dp', 'fsdp'))
- feed_shift_grad: float32 [1024], P(('dp', 'fsdp'))
The draws below stay inside these ranges and needn't reach their ends.
Inputs may be any that keep to these rules, and one draw needn't show every extreme that they name: In each tree the first 4 segments form a chain (segment i has parent i - 1, segment 0 is its own parent); each of the next 2 segments has a parent that is trunk segment 2 or 3; the last 4 segments have parents among the branch segments, 2 on each branch. `order`: for each tree and round, every position once, ordered by that round's bucket and, within a bucket, by position.
All inputs are finite; a program needn't handle non-finite values.
Results may differ from the reference program's by a relative error of at most 0.019.
Values may be sent and summed in bfloat16 or wider, within the bound.
No kernel may reach another device: no remote copies, remote signals or barrier semaphores. Data moves between devices by JAX's collectives and lax.ppermute only.
A program may use at most 384 MiB of HBM per device.

```python
import math
import jax
import jax.numpy as jnp
from jax import lax

D = 1024
H = 8
DH = 128
FF = 4096
CH = 64
ROUNDS = 4
NBUCK = 32
SEG = 128
TRUNK = 4
BRANCHES = 2
LEAVES = 2
MICRO = 2
TREE = 1280
N_DP = 8


def bucket_table(key):
    return jax.random.randint(jax.random.fold_in(key, 7), (MICRO, N_DP, ROUNDS, TREE), 0, NBUCK, dtype=jnp.int32)


def draw_buckets(key, part):
    return bucket_table(key)


def draw_order(key, part):
    table = bucket_table(key)
    ranked = table * TREE + jnp.arange(TREE, dtype=jnp.int32)
    return jnp.argsort(ranked, axis=-1).astype(jnp.int32)


def draw_parents(key, part):
    indices = jnp.arange(TRUNK, dtype=jnp.int32)
    trunk_rows = jnp.broadcast_to(jnp.maximum(indices - 1, 0), (MICRO, N_DP, TRUNK))
    branch_rows = jax.random.randint(jax.random.fold_in(key, 3), (MICRO, N_DP, BRANCHES), TRUNK // 2, TRUNK, dtype=jnp.int32)
    offsets = jax.random.randint(jax.random.fold_in(key, 5), (MICRO, N_DP, 1), 0, BRANCHES, dtype=jnp.int32)
    leaf_index = jnp.arange(BRANCHES * LEAVES, dtype=jnp.int32) // LEAVES
    leaf_rows = TRUNK + (leaf_index[None, None, :] + offsets) % BRANCHES
    return jnp.concatenate([trunk_rows, branch_rows, leaf_rows], axis=-1).astype(jnp.int32)


def block_scale(own_key, shape, cuts, low, top_value):
    loudness, own = 1.0, jax.random.fold_in(own_key, 6)
    for position, shards_of in cuts:
        heights = jnp.exp(jax.random.uniform(jax.random.fold_in(own, position), (shards_of,), jnp.float32, low / len(cuts), top_value / len(cuts)))
        loudness = loudness * jnp.repeat(heights, shape[position] // shards_of).reshape([-1 if axis == position else 1 for axis in range(len(shape))])
    return loudness


def bell_draw(key, extent, width, bound, shards=(), kind=jnp.bfloat16):
    values = jax.random.normal(key, extent, jnp.float32) * width
    if len(shards) > 0:
        values = block_scale(key, extent, shards, -0.22, 0.18) * values
    return jnp.clip(values, min=-bound, max=bound).astype(kind)


def setup_inputs(seed: int = 0) -> dict:
    streams_of = jax.random.split(jax.random.key(seed), 19)
    return {
        "first_half": bell_draw(streams_of[0], (MICRO, N_DP, TREE, D), 1.0, 6.0, ((1, 8), (2, 4)), jnp.float32),
        "second_half": bell_draw(streams_of[1], (MICRO, N_DP, TREE, D), 1.0, 6.0, ((1, 8), (2, 4)), jnp.float32),
        "grad_first": bell_draw(streams_of[2], (MICRO, N_DP, TREE, D), 1.0, 6.0, ((1, 8), (2, 4)), jnp.float32),
        "grad_second": bell_draw(streams_of[3], (MICRO, N_DP, TREE, D), 1.0, 6.0, ((1, 8), (2, 4)), jnp.float32),
        "query_weight": bell_draw(streams_of[4], (D, D), D ** -0.5, 0.1875, ((0, 32),)),
        "value_weight": bell_draw(streams_of[5], (D, D), D ** -0.5, 0.1875, ((0, 32),)),
        "output_weight": bell_draw(streams_of[6], (D, D), (D // 64) ** -0.5, 1.5, ((0, 32),)),
        "inner_weight": bell_draw(streams_of[7], (D, FF), D ** -0.5, 0.1875, ((0, 32),)),
        "inner_bias": bell_draw(streams_of[8], (FF,), 0.5, 3.0, ((0, 32),)),
        "outer_weight": bell_draw(streams_of[9], (FF, D), FF ** -0.5, 0.09375, ((0, 32),)),
        "outer_bias": bell_draw(streams_of[10], (D,), 0.3, 2.0, ((0, 32),)),
        "mixer_gain": jnp.clip(1.0 + 0.1 * jax.random.normal(streams_of[11], (D,), jnp.float32), 0.5, 1.5).astype(jnp.bfloat16),
        "mixer_shift": bell_draw(streams_of[12], (D,), 0.3, 2.0, ((0, 32),)),
        "feed_gain": jnp.clip(1.0 + 0.1 * jax.random.normal(streams_of[13], (D,), jnp.float32), 0.5, 1.5).astype(jnp.bfloat16),
        "feed_shift": bell_draw(streams_of[14], (D,), 0.3, 2.0, ((0, 32),)),
        "parents": draw_parents(jax.random.fold_in(streams_of[18], 71), 0),
        "buckets": draw_buckets(jax.random.fold_in(streams_of[18], 71), 0),
        "order": draw_order(jax.random.fold_in(streams_of[18], 71), 0),
    }


@jax.custom_vjp
def low(v):
    return lax.optimization_barrier(v.astype(jnp.bfloat16)).astype(jnp.float32)

@jax.custom_vjp
def low_back(v):
    return v

def low_keep(v):
    return (low(v), None)

def low_pass(kept, grad):
    return (grad,)

def back_keep(v):
    return (v, None)

def back_low(kept, grad):
    return (low(grad),)
low.defvjp(low_keep, low_pass)
low_back.defvjp(back_keep, back_low)
SELF_SCORE = -10000.0
NEG_SCORE = -1e+30
EPSILON = 1e-06
FULL_PRECISION = lax.Precision.HIGHEST

def both_ways(values):
    return low_back(low(values))

def layer_norm(values, gain_vec, shift_vec):
    center = values - lax.optimization_barrier(jnp.mean(values, axis=-1, keepdims=True))
    factor = lax.rsqrt(lax.optimization_barrier(jnp.mean(center * center, axis=-1, keepdims=True)) + EPSILON)
    return center * factor * gain_vec + shift_vec

def key_norm(rows_in, head_count):
    heads_view = rows_in.reshape(rows_in.shape[:-1] + (head_count, rows_in.shape[-1] // head_count))
    factor = lax.rsqrt(lax.optimization_barrier(jnp.mean(heads_view * heads_view, axis=-1, keepdims=True)) + EPSILON)
    return (heads_view * factor / math.sqrt(heads_view.shape[-1])).reshape(rows_in.shape)

def fast_gelu(values):
    return jax.nn.gelu(values, approximate=True)

def ancestry(parent_row):
    segments = parent_row.shape[0]
    indices = jnp.arange(segments, dtype=jnp.int32)
    step_map = (parent_row[:, None] == indices[None, :]).astype(jnp.float32)
    reached = jnp.minimum(jnp.eye(segments, dtype=jnp.float32) + step_map, 1.0)
    for _ in range(segments.bit_length()):
        reached = jnp.minimum(jnp.dot(reached, reached, precision=FULL_PRECISION), 1.0)
    return reached

def tree_attention(query_key, value_rows, unit_keys, parent_row, bucket_rows, order_rows):
    tree_len = query_key.shape[0]
    blocks = tree_len // CH
    ancestors = ancestry(parent_row)

    def scored(ranking, bucket):
        inverse = jnp.zeros((tree_len,), jnp.int32).at[ranking].set(jnp.arange(tree_len, dtype=jnp.int32))
        tokens = ranking.reshape(blocks, CH)
        token_window = jnp.concatenate([jnp.roll(tokens, 1, axis=0), tokens], axis=1)
        labels = bucket[ranking].reshape(blocks, CH)
        label_window = jnp.concatenate([jnp.roll(labels, 1, axis=0), labels], axis=1)
        queries = query_key[ranking].reshape(blocks, CH, H, DH)
        keys_sorted = unit_keys[ranking].reshape(blocks, CH, H, DH)
        key_window = jnp.concatenate([jnp.roll(keys_sorted, 1, axis=0), keys_sorted], axis=1)
        values_sorted = value_rows[ranking].reshape(blocks, CH, H, DH)
        value_window = jnp.concatenate([jnp.roll(values_sorted, 1, axis=0), values_sorted], axis=1)
        has_prev = jnp.arange(blocks) > 0
        in_range = jnp.concatenate([jnp.broadcast_to(has_prev[:, None], (blocks, CH)), jnp.ones((blocks, CH), bool)], axis=1)
        linked = ancestors[(tokens // SEG)[:, :, None], (token_window // SEG)[:, None, :]] > 0.5
        usable = in_range[:, None, :] & (label_window[:, None, :] == labels[:, :, None]) & (token_window[:, None, :] <= tokens[:, :, None]) & linked
        itself = token_window[:, None, :] == tokens[:, :, None]
        scores = low_back(jnp.einsum('bqhd,bkhd->bhqk', queries, key_window, precision=FULL_PRECISION))
        masked = jnp.where(itself[:, None], SELF_SCORE, jnp.where(usable[:, None], scores, NEG_SCORE))
        block_lse = jax.nn.logsumexp(masked, axis=-1)
        token_lse = jnp.moveaxis(block_lse, 1, 0).reshape(H, tree_len)[:, inverse]
        return (masked, value_window, token_lse, inverse)
    masked, value_window, token_lse, inverse = jax.vmap(scored)(order_rows, bucket_rows)
    overall = jax.nn.logsumexp(token_lse, axis=0)

    def spread(masked_round, value_round, ranking, inverse_round):
        query_total = jnp.moveaxis(overall[:, ranking].reshape(H, blocks, CH), 0, 1)
        chances = low(jnp.exp(masked_round - query_total[..., None]))
        result_rows = jnp.einsum('bhqk,bkhd->bqhd', chances, value_round, precision=FULL_PRECISION).reshape(tree_len, H * DH)
        return result_rows[inverse_round]
    return lax.optimization_barrier(jnp.sum(jax.vmap(spread)(masked, value_window, order_rows, inverse), axis=0))

def forward(first_in, second_in, params, parent_row, bucket_rows, order_rows):
    query_w, value_w, output_w, inner_w, inner_b, outer_w, outer_b, mixer_g, mixer_s, feed_g, feed_s = params
    mixed_low = low(layer_norm(second_in, mixer_g, mixer_s))
    query_key = both_ways(jnp.dot(mixed_low, query_w, precision=FULL_PRECISION))
    value_rows = both_ways(jnp.dot(mixed_low, value_w, precision=FULL_PRECISION))
    unit_keys = low(key_norm(query_key, H))
    attended = tree_attention(query_key, value_rows, unit_keys, parent_row, bucket_rows, order_rows)
    attended_low = both_ways(attended)
    first_out = first_in + low_back(jnp.dot(attended_low, output_w, precision=FULL_PRECISION))
    feed_low = low(layer_norm(first_out, feed_g, feed_s))
    inner_pre = low_back(jnp.dot(feed_low, inner_w, precision=FULL_PRECISION) + inner_b)
    active = low(fast_gelu(inner_pre))
    second_out = second_in + low_back(jnp.dot(active, outer_w, precision=FULL_PRECISION) + outer_b)
    return (first_out, second_out)

def reference(first_half, second_half, grad_first, grad_second, query_weight, value_weight, output_weight, inner_weight, inner_bias, outer_weight, outer_bias, mixer_gain, mixer_shift, feed_gain, feed_shift, parents, buckets, order):
    weights = tuple((member.astype(jnp.float32) for member in (query_weight, value_weight, output_weight, inner_weight, inner_bias, outer_weight, outer_bias, mixer_gain, mixer_shift, feed_gain, feed_shift)))
    tree_count = MICRO * N_DP

    def flatten_trees(array):
        return array.reshape((tree_count,) + array.shape[2:])

    def one_tree(summed, tree_item):
        first_rows, second_rows, grad_a, grad_b, parent_row, bucket_rows, order_rows = tree_item

        def run_tree(first_in, second_in, params):
            return forward(first_in, second_in, params, parent_row, bucket_rows, order_rows)
        pair, pullback = jax.vjp(run_tree, first_rows, second_rows, weights)
        grad_in_a, grad_in_b, grad_params = pullback((grad_a, grad_b))
        summed = jax.tree.map(jnp.add, summed, grad_params)
        return (summed, (pair[0], pair[1], grad_in_a, grad_in_b))
    zeros_start = tuple((jnp.zeros_like(member) for member in weights))
    items = (flatten_trees(first_half.astype(jnp.float32)), flatten_trees(second_half.astype(jnp.float32)), flatten_trees(grad_first.astype(jnp.float32)), flatten_trees(grad_second.astype(jnp.float32)), flatten_trees(parents), flatten_trees(buckets), flatten_trees(order))
    summed, stacked = lax.scan(one_tree, zeros_start, items)
    full_shape = first_half.shape
    return (stacked[0].reshape(full_shape), stacked[1].reshape(full_shape), stacked[2].reshape(full_shape), stacked[3].reshape(full_shape), summed[0], summed[1], summed[2], summed[3], summed[4], summed[5], summed[6], summed[7], summed[8], summed[9], summed[10])
```

```python
import functools
import math

import jax
import jax.numpy as jnp
from jax import lax
from jax.experimental import pallas as pl
from jax.experimental.pallas import tpu as pltpu
from jax.sharding import PartitionSpec as P

H = 8
DH = 128
CH = 64
SEG = 128
TRUNK = 4
BRANCHES = 2
NBUCK = 32
SELF_SCORE = -10000.0
NEG_SCORE = -1e30
EPSILON = 1e-06
BF = jnp.bfloat16
F32 = jnp.float32
AXES = ("dp", "fsdp")
GELU_A = math.sqrt(2.0 / math.pi)
GELU_B = 0.044715


def norm_stats(values):
    center = values - jnp.mean(values, axis=-1, keepdims=True)
    factor = lax.rsqrt(jnp.mean(center * center, axis=-1, keepdims=True) + EPSILON)
    return center * factor, factor


def norm_back(unit, factor, gain_vec, grad):
    scaled = grad * gain_vec
    inner = jnp.mean(scaled * unit, axis=-1, keepdims=True)
    return factor * (scaled - jnp.mean(scaled, axis=-1, keepdims=True) - unit * inner)


def position_codes(bucket_rows):
    rounds, tree_len = bucket_rows.shape
    buckets_t = bucket_rows.T
    lanes = jnp.arange(rounds * NBUCK, dtype=jnp.int32)
    member = (jnp.repeat(buckets_t, NBUCK, axis=1) == (lanes % NBUCK)[None, :]).astype(F32)
    rows = jnp.arange(tree_len, dtype=jnp.int32)
    lower = (rows[:, None] >= rows[None, :]).astype(BF)
    ranks = jnp.dot(lower, member.astype(BF), preferred_element_type=F32)
    totals = ranks[-1]
    before = ((lanes[:, None] // NBUCK == lanes[None, :] // NBUCK) & (lanes[:, None] < lanes[None, :])).astype(F32)
    offsets = jnp.sum(totals[:, None] * before, axis=0)
    places = jnp.sum((member * (ranks - 1.0 + offsets[None, :])).reshape(tree_len, rounds, NBUCK), axis=-1)
    return buckets_t.astype(F32) * tree_len + jnp.floor((places + 0.5) / CH)


def seg_parts(seg, info_ref):
    parts = []
    prefix = min(seg, TRUNK) * SEG
    if prefix:
        parts.append((0, prefix, 0, False))
    if seg >= TRUNK + BRANCHES:
        start = pl.multiple_of(info_ref[seg] * SEG, SEG)
        parts.append((start, SEG, TRUNK * SEG, False))
    parts.append((seg * SEG, SEG, (TRUNK + 1) * SEG, True))
    return parts


def unit_rows(rows_f32):
    factor = lax.rsqrt(jnp.mean(rows_f32 * rows_f32, axis=-1, keepdims=True) + EPSILON)
    return rows_f32 * factor * (1.0 / math.sqrt(DH)), factor


def own_diagonal():
    row = lax.broadcasted_iota(jnp.int32, (SEG, SEG), 0)
    col = lax.broadcasted_iota(jnp.int32, (SEG, SEG), 1)
    return row == col


def attention_forward_kernel(segments, rounds, info_ref, q_ref, v_ref, cq_ref, ck_ref, out_ref, total_ref, count_ref, unit_ref):
    head = pl.program_id(0)

    @pl.when(head == 0)
    def _():
        row = lax.broadcasted_iota(jnp.int32, (SEG, SEG), 0)
        col = lax.broadcasted_iota(jnp.int32, (SEG, SEG), 1)
        total_ref[...] = jnp.zeros_like(total_ref)
        for seg in range(segments):
            query = cq_ref[seg * SEG:(seg + 1) * SEG, :]
            for start, size, column, own in seg_parts(seg, info_ref):
                for piece in range(size // SEG):
                    first = start + piece * SEG
                    key = ck_ref[:, pl.ds(first, SEG)]
                    counted = jnp.zeros((SEG, SEG), F32)
                    for turn in range(rounds):
                        gap = query[:, turn:turn + 1] - key[turn:turn + 1, :]
                        counted = counted + jnp.where(jnp.abs(gap - 0.5) < 0.75, 1.0, 0.0)
                    if own:
                        counted = jnp.where(row >= col, counted, 0.0)
                    elif column == 0 and seg >= TRUNK:
                        counted = counted * jnp.where(info_ref[segments + seg] >= piece, 1.0, 0.0)
                    begin = column + piece * SEG
                    count_ref[seg * SEG:(seg + 1) * SEG, begin:begin + SEG] = counted.astype(BF)

    unit_ref[...] = unit_rows(q_ref[...].astype(F32))[0].astype(BF)
    diagonal = own_diagonal()
    lane = lax.broadcasted_iota(jnp.int32, (SEG, 128), 1)
    for seg in range(segments):
        rows = slice(seg * SEG, (seg + 1) * SEG)
        query = q_ref[rows, :]
        scored = []
        top = None
        for start, size, column, own in seg_parts(seg, info_ref):
            keys = pl.ds(start, size)
            scores = lax.dot_general(query, unit_ref[keys, :], (((1,), (1,)), ((), ())), preferred_element_type=F32)
            counted = count_ref[rows, column:column + size].astype(F32)
            if own:
                scores = jnp.where(diagonal, SELF_SCORE, scores)
            scores = jnp.where(counted > 0.0, scores, NEG_SCORE)
            best = jnp.max(scores, axis=-1, keepdims=True)
            top = best if top is None else jnp.maximum(top, best)
            scored.append((keys, scores, counted))
        amount = jnp.zeros((SEG, 1), F32)
        result = jnp.zeros((SEG, DH), F32)
        for keys, scores, counted in scored:
            weight = counted * jnp.exp(scores - top)
            amount = amount + jnp.sum(weight, axis=-1, keepdims=True)
            result = result + jnp.dot(weight.astype(BF), v_ref[keys, :], preferred_element_type=F32)
        out_ref[rows, :] = (result / amount).astype(BF)
        total = top + jnp.log(amount)
        total_ref[rows, :] = jnp.where(lane == head, total, total_ref[rows, :])


def attention_backward_kernel(segments, info_ref, q_ref, v_ref, out_ref, grad_ref, total_ref, count_ref, dq_ref, dv_ref, unit_ref, chance_ref, slope_ref, key_acc, value_acc, query_acc):
    head = pl.program_id(0)
    trunk = TRUNK * SEG
    whole = q_ref[...].astype(F32)
    unit, factor = unit_rows(whole)
    unit_ref[...] = unit.astype(BF)

    @pl.when(head == 0)
    def _():
        chance_ref[0:trunk, 0:trunk] = jnp.zeros((trunk, trunk), BF)
        slope_ref[0:trunk, 0:trunk] = jnp.zeros((trunk, trunk), BF)

    diagonal = own_diagonal()
    lane = lax.broadcasted_iota(jnp.int32, (SEG, 128), 1)
    for seg in range(segments):
        rows = slice(seg * SEG, (seg + 1) * SEG)
        query = q_ref[rows, :]
        grad = grad_ref[rows, :]
        total = jnp.sum(jnp.where(lane == head, total_ref[rows, :], 0.0), axis=-1, keepdims=True)
        delta = jnp.sum(grad.astype(F32) * out_ref[rows, :].astype(F32), axis=-1, keepdims=True)
        query_grad = jnp.zeros((SEG, DH), F32)
        for start, size, column, own in seg_parts(seg, info_ref):
            keys = pl.ds(start, size)
            scores = lax.dot_general(query, unit_ref[keys, :], (((1,), (1,)), ((), ())), preferred_element_type=F32)
            counted = count_ref[rows, column:column + size].astype(F32)
            if own:
                scores = jnp.where(diagonal, SELF_SCORE, scores)
            scores = jnp.where(counted > 0.0, scores, NEG_SCORE)
            chance = counted * jnp.exp(scores - total)
            reach = lax.dot_general(grad, v_ref[keys, :], (((1,), (1,)), ((), ())), preferred_element_type=F32)
            slope = chance * (reach - delta)
            if own:
                slope = jnp.where(diagonal, 0.0, slope)
            slope = slope.astype(BF)
            chance_ref[rows, column:column + size] = chance.astype(BF)
            slope_ref[rows, column:column + size] = slope
            query_grad = query_grad + jnp.dot(slope, unit_ref[keys, :], preferred_element_type=F32)
        query_acc[rows, :] = query_grad

    for weight_ref, side_ref, acc in ((chance_ref, grad_ref, value_acc), (slope_ref, q_ref, key_acc)):
        acc[0:trunk, :] = lax.dot_general(weight_ref[:, 0:trunk], side_ref[...], (((0,), (0,)), ((), ())), preferred_element_type=F32)
        for seg in range(segments):
            rows = slice(seg * SEG, (seg + 1) * SEG)
            leaf = seg >= TRUNK + BRANCHES
            begin = trunk if leaf else trunk + SEG
            added = lax.dot_general(weight_ref[rows, begin:trunk + 2 * SEG], side_ref[rows, :], (((0,), (0,)), ((), ())), preferred_element_type=F32)
            if leaf:
                above = pl.ds(pl.multiple_of(info_ref[seg] * SEG, SEG), SEG)
                acc[above, :] += added[0:SEG]
                added = added[SEG:]
            acc[rows, :] = added if seg >= TRUNK else acc[rows, :] + added

    key_grad = key_acc[...]
    along = jnp.mean(key_grad * whole, axis=-1, keepdims=True) * (factor * factor)
    dq_ref[...] = (query_acc[...] + (factor * (1.0 / math.sqrt(DH))) * (key_grad - whole * along)).astype(BF)
    dv_ref[...] = value_acc[...].astype(BF)


def attention_calls(tree_len, local_heads, rounds, segments):
    head_spec = pl.BlockSpec((tree_len, DH), lambda h, info: (0, h))
    side = pl.BlockSpec((tree_len, 128), lambda h, info: (0, 0))
    count_spec = pl.BlockSpec((tree_len, (TRUNK + 2) * SEG), lambda h, info: (0, 0))
    wide = local_heads * DH
    forward = pl.pallas_call(
        functools.partial(attention_forward_kernel, segments, rounds),
        grid_spec=pltpu.PrefetchScalarGridSpec(
            num_scalar_prefetch=1,
            grid=(local_heads,),
            in_specs=[head_spec, head_spec, side, pl.BlockSpec((8, tree_len), lambda h, info: (0, 0))],
            out_specs=[head_spec, side, count_spec],
            scratch_shapes=[pltpu.VMEM((tree_len, DH), BF)],
        ),
        out_shape=[
            jax.ShapeDtypeStruct((tree_len, wide), BF),
            jax.ShapeDtypeStruct((tree_len, 128), F32),
            jax.ShapeDtypeStruct((tree_len, (TRUNK + 2) * SEG), BF),
        ],
        compiler_params=pltpu.CompilerParams(vmem_limit_bytes=40 << 20),
        name="attention_forward",
    )
    backward = pl.pallas_call(
        functools.partial(attention_backward_kernel, segments),
        grid_spec=pltpu.PrefetchScalarGridSpec(
            num_scalar_prefetch=1,
            grid=(local_heads,),
            in_specs=[head_spec, head_spec, head_spec, head_spec, side, count_spec],
            out_specs=[head_spec, head_spec],
            scratch_shapes=[pltpu.VMEM((tree_len, DH), BF)]
            + [pltpu.VMEM((tree_len, (TRUNK + 2) * SEG), BF)] * 2
            + [pltpu.VMEM((tree_len, DH), F32)] * 3,
        ),
        out_shape=[jax.ShapeDtypeStruct((tree_len, wide), BF)] * 2,
        compiler_params=pltpu.CompilerParams(vmem_limit_bytes=40 << 20),
        name="attention_backward",
    )
    return forward, backward


def feed_kernel(feed_ref, grad_ref, inner_ref, bias_ref, outer_ref, out_ref, back_ref, inner_grad_ref, outer_grad_ref, bias_grad_ref):
    step = pl.program_id(0)

    @pl.when(step == 0)
    def _():
        out_ref[...] = jnp.zeros_like(out_ref)
        back_ref[...] = jnp.zeros_like(back_ref)

    feed = feed_ref[...]
    grad = grad_ref[...]
    weight = inner_ref[...]
    value = jnp.dot(feed, weight, preferred_element_type=F32) + bias_ref[...]
    square = value * value
    bend = jnp.tanh(GELU_A * (value + GELU_B * (square * value)))
    half = 0.5 * (1.0 + bend)
    active = (value * half).astype(BF)
    slope = half + 0.5 * value * (1.0 - bend * bend) * (GELU_A * (1.0 + 3.0 * GELU_B * square))
    out_ref[...] += jnp.dot(active, outer_ref[...], preferred_element_type=F32)
    outer_grad_ref[...] = lax.dot_general(active, grad, (((0,), (0,)), ((), ())), preferred_element_type=F32).astype(BF)
    pulled = lax.dot_general(grad, outer_ref[...], (((1,), (1,)), ((), ())), preferred_element_type=F32)
    inner_low = (pulled * slope).astype(BF)
    bias_grad_ref[...] = jnp.sum(inner_low.astype(F32), axis=0, keepdims=True)
    inner_grad_ref[...] = lax.dot_general(feed, inner_low, (((0,), (0,)), ((), ())), preferred_element_type=F32).astype(BF)
    back_ref[...] += lax.dot_general(inner_low, weight, (((1,), (1,)), ((), ())), preferred_element_type=F32)


def feed_call(rows, features, hidden, tile):
    fixed = pl.BlockSpec((rows, features), lambda j: (0, 0))
    return pl.pallas_call(
        feed_kernel,
        grid=(hidden // tile,),
        in_specs=[
            fixed,
            fixed,
            pl.BlockSpec((features, tile), lambda j: (0, j)),
            pl.BlockSpec((1, tile), lambda j: (0, j)),
            pl.BlockSpec((tile, features), lambda j: (j, 0)),
        ],
        out_specs=[
            fixed,
            fixed,
            pl.BlockSpec((features, tile), lambda j: (0, j)),
            pl.BlockSpec((tile, features), lambda j: (j, 0)),
            pl.BlockSpec((1, tile), lambda j: (0, j)),
        ],
        out_shape=[
            jax.ShapeDtypeStruct((rows, features), F32),
            jax.ShapeDtypeStruct((rows, features), F32),
            jax.ShapeDtypeStruct((features, hidden), BF),
            jax.ShapeDtypeStruct((hidden, features), BF),
            jax.ShapeDtypeStruct((1, hidden), F32),
        ],
        compiler_params=pltpu.CompilerParams(vmem_limit_bytes=60 << 20),
        name="feed_forward_backward",
    )


def pick(flag, when_true, when_false):
    return jnp.where(flag, when_true, when_false)


class PairPlan:
    def __init__(self):
        me = lax.axis_index("fsdp")
        self.upper = me // 2 == 1
        self.odd = me % 2 == 1
        self.tree = me // 2
        self.head_group = me % 2

    def near(self, value):
        return lax.ppermute(value, "fsdp", [(i, i ^ 1) for i in range(4)])

    def far(self, value):
        return lax.ppermute(value, "fsdp", [(i, i ^ 2) for i in range(4)])

    def rows_to_tree(self, rows):
        mine = pick(self.upper, rows[1], rows[0])
        got = self.far(pick(self.upper, rows[0], rows[1]))
        pair = jnp.stack([pick(self.upper, got, mine), pick(self.upper, mine, got)])
        other = self.near(pair)
        whole = jnp.stack([pick(self.odd, other, pair), pick(self.odd, pair, other)], axis=1)
        return whole.reshape((-1, rows.shape[2]))

    def heads_to_rows(self, heads):
        blocks = heads.reshape(2, 2, -1, heads.shape[1])
        keep = pick(self.odd, blocks[:, 1], blocks[:, 0])
        got = self.near(pick(self.odd, blocks[:, 0], blocks[:, 1]))
        full = jnp.concatenate([pick(self.odd, got, keep), pick(self.odd, keep, got)], axis=-1)
        return self.swap_trees(full)

    def swap_trees(self, full):
        mine = pick(self.upper, full[1], full[0])
        got = self.far(pick(self.upper, full[0], full[1]))
        return jnp.stack([pick(self.upper, got, mine), pick(self.upper, mine, got)])

    def rows_to_heads(self, rows):
        wide = rows.shape[2] // 2
        mine = pick(self.upper, rows[1], rows[0])
        got = self.far(pick(self.upper, rows[0], rows[1]))
        pair = jnp.stack([pick(self.upper, got, mine), pick(self.upper, mine, got)])
        keep = pick(self.odd, pair[..., wide:], pair[..., :wide])
        other = self.near(pick(self.odd, pair[..., :wide], pair[..., wide:]))
        whole = jnp.stack([pick(self.odd, other, keep), pick(self.odd, keep, other)], axis=1)
        return whole.reshape((-1, wide))

    def partial_to_rows(self, partial):
        blocks = partial.reshape(2, 2, -1, partial.shape[1])
        keep = pick(self.odd, blocks[:, 1], blocks[:, 0])
        got = self.near(pick(self.odd, blocks[:, 0], blocks[:, 1]).astype(BF))
        return self.swap_trees((keep + got.astype(F32)).astype(BF)).astype(F32)


class GroupPlan:
    def __init__(self, size, trees):
        me = lax.axis_index("fsdp")
        self.size = size
        self.trees = trees
        self.group = size // trees
        self.tree = me // self.group
        self.head_group = me % self.group
        self.me = me

    def rows_to_tree(self, rows):
        every = lax.all_gather(rows, "fsdp", axis=1, tiled=True)
        return lax.dynamic_index_in_dim(every, self.tree, 0, False)

    def heads_to_rows(self, heads):
        count = heads.shape[0] // self.size
        every = lax.all_gather(heads, "fsdp", axis=0, tiled=False)
        mine = lax.dynamic_slice_in_dim(every, self.me * count, count, 1)
        mine = mine.reshape(self.trees, self.group, count, heads.shape[1])
        return jnp.moveaxis(mine, 1, 2).reshape(self.trees, count, -1)

    def rows_to_heads(self, rows):
        wide = rows.shape[2] // self.group
        whole = self.rows_to_tree(rows)
        return lax.dynamic_slice_in_dim(whole, self.head_group * wide, wide, 1)

    def partial_to_rows(self, partial):
        every = jnp.zeros((self.trees,) + partial.shape, F32)
        every = lax.dynamic_update_index_in_dim(every, partial, self.tree, 0)
        return lax.psum_scatter(every, "fsdp", scatter_dimension=1, tiled=True)


def per_device(
    first_half,
    second_half,
    grad_first,
    grad_second,
    query_weight,
    value_weight,
    output_weight,
    inner_weight,
    inner_bias,
    outer_weight,
    outer_bias,
    mixer_gain,
    mixer_shift,
    feed_gain,
    feed_shift,
    parents,
    buckets,
    order,
    *,
    dp_size,
    fsdp_size,
):
    trees = first_half.shape[0]
    row_count = first_half.shape[2]
    features = first_half.shape[3]
    hidden = inner_weight.shape[1]
    rounds = buckets.shape[2]
    tree_len = buckets.shape[3]
    segments = parents.shape[2]
    all_rows = trees * row_count
    devices = dp_size * fsdp_size
    plan = PairPlan() if (fsdp_size, trees) == (4, 2) else GroupPlan(fsdp_size, trees)
    local_heads = H // (fsdp_size // trees)
    wide = local_heads * DH

    first = first_half[:, 0]
    second = second_half[:, 0]
    grad_a = grad_first[:, 0]
    grad_b = grad_second[:, 0]

    def gather(shard):
        return lax.all_gather(shard, AXES, axis=0, tiled=True)

    small_sizes = [v.shape[0] for v in (inner_bias, outer_bias, mixer_gain, mixer_shift, feed_gain, feed_shift)]
    small = lax.all_gather(
        jnp.concatenate([inner_bias, outer_bias, mixer_gain, mixer_shift, feed_gain, feed_shift])[None], AXES, axis=0, tiled=True
    ).astype(F32)
    vectors = []
    begin = 0
    for size in small_sizes:
        vectors.append(small[:, begin:begin + size].reshape(-1))
        begin += size
    bias_inner, bias_outer, gain_mix, shift_mix, gain_feed, shift_feed = vectors

    query_full = gather(query_weight)
    value_full = gather(value_weight)
    output_full = gather(output_weight)
    inner_full = gather(inner_weight)
    outer_full = gather(outer_weight)

    mix_unit, mix_factor = norm_stats(second)
    mixed_low = (mix_unit * gain_mix + shift_mix).astype(BF)
    mixed_tree = plan.rows_to_tree(mixed_low)
    parent_row = lax.dynamic_index_in_dim(parents[:, 0], plan.tree, 0, False)
    bucket_rows = lax.dynamic_index_in_dim(buckets[:, 0], plan.tree, 0, False)
    branch = parent_row[jnp.clip(parent_row, 0, segments - 1)]
    trunk_end = jnp.where(jnp.arange(segments) >= TRUNK + BRANCHES, branch, parent_row)
    info = jnp.concatenate([parent_row, trunk_end])
    codes = position_codes(bucket_rows)
    codes_q = jnp.pad(codes, ((0, 0), (0, 128 - rounds)))
    codes_k = jnp.pad(codes.T, ((0, 8 - rounds), (0, 0)))
    query_cols = lax.dynamic_slice_in_dim(query_full, plan.head_group * wide, wide, 1)
    value_cols = lax.dynamic_slice_in_dim(value_full, plan.head_group * wide, wide, 1)
    query_key = jnp.dot(mixed_tree, query_cols, preferred_element_type=F32).astype(BF)
    value_rows = jnp.dot(mixed_tree, value_cols, preferred_element_type=F32).astype(BF)
    attend, attend_back = attention_calls(tree_len, local_heads, rounds, segments)
    attended, totals, counts = attend(info, query_key, value_rows, codes_q, codes_k)
    attended_low = plan.heads_to_rows(attended)

    first_out = first + jnp.dot(attended_low.reshape(all_rows, features), output_full, preferred_element_type=F32).reshape(first.shape)
    feed_unit, feed_factor = norm_stats(first_out)
    feed_low = (feed_unit * gain_feed + shift_feed).astype(BF).reshape(all_rows, features)
    outer_low = grad_b.astype(BF).reshape(all_rows, features)
    fed, grad_feed, inner_grad, outer_grad, inner_bias_sum = feed_call(all_rows, features, hidden, 512)(
        feed_low, outer_low, inner_full, bias_inner[None], outer_full
    )
    second_out = second + fed.reshape(second.shape) + bias_outer
    outer_bias_sum = jnp.sum(outer_low.astype(F32), axis=0)
    grad_feed = grad_feed.reshape(first.shape)
    feed_gain_sum = jnp.sum(grad_feed * feed_unit, axis=(0, 1))
    feed_shift_sum = jnp.sum(grad_feed, axis=(0, 1))
    grad_first_in = grad_a + norm_back(feed_unit, feed_factor, gain_feed, grad_feed)
    branch_low = grad_first_in.astype(BF).reshape(all_rows, features)

    output_grad = lax.dot_general(
        attended_low.reshape(all_rows, features), branch_low, (((0,), (0,)), ((), ())), preferred_element_type=F32
    ).astype(BF)
    grad_attended = lax.dot_general(branch_low, output_full, (((1,), (1,)), ((), ())), preferred_element_type=F32).astype(BF)
    grad_heads = plan.rows_to_heads(grad_attended.reshape(trees, row_count, features))
    query_low, value_low = attend_back(info, query_key, value_rows, attended, grad_heads, totals, counts)
    query_grad = lax.dot_general(mixed_tree, query_low, (((0,), (0,)), ((), ())), preferred_element_type=F32).astype(BF)
    value_grad = lax.dot_general(mixed_tree, value_low, (((0,), (0,)), ((), ())), preferred_element_type=F32).astype(BF)
    partial = lax.dot_general(query_low, query_cols, (((1,), (1,)), ((), ())), preferred_element_type=F32) + lax.dot_general(
        value_low, value_cols, (((1,), (1,)), ((), ())), preferred_element_type=F32
    )
    grad_mixed = plan.partial_to_rows(partial)
    mix_gain_sum = jnp.sum(grad_mixed * mix_unit, axis=(0, 1))
    mix_shift_sum = jnp.sum(grad_mixed, axis=(0, 1))
    grad_second_in = grad_b + norm_back(mix_unit, mix_factor, gain_mix, grad_mixed)

    def scatter(total):
        return lax.psum_scatter(total, AXES, scatter_dimension=0, tiled=True).astype(F32)

    def spread(cols):
        return lax.dynamic_update_slice_in_dim(jnp.zeros((features, features), BF), cols, plan.head_group * wide, 1)

    small_sums = [inner_bias_sum[0], outer_bias_sum, mix_gain_sum, mix_shift_sum, feed_gain_sum, feed_shift_sum]
    packed = jnp.concatenate([v.reshape(devices, -1) for v in small_sums], axis=1)
    packed = lax.psum_scatter(packed, AXES, scatter_dimension=0, tiled=True)[0]
    pieces = []
    begin = 0
    for size in small_sizes:
        pieces.append(packed[begin:begin + size])
        begin += size
    return (
        first_out[:, None],
        second_out[:, None],
        grad_first_in[:, None],
        grad_second_in[:, None],
        scatter(spread(query_grad)),
        scatter(spread(value_grad)),
        scatter(output_grad),
        scatter(inner_grad),
        pieces[0],
        scatter(outer_grad),
        pieces[1],
        pieces[2],
        pieces[3],
        pieces[4],
        pieces[5],
    )


def solution(mesh):
    rows = P(None, "dp", "fsdp", None)
    matrix = P(AXES, None)
    vector = P(AXES)
    weights = (matrix, matrix, matrix, matrix, vector, matrix, vector, vector, vector, vector, vector)
    return jax.shard_map(
        functools.partial(per_device, dp_size=mesh.shape["dp"], fsdp_size=mesh.shape["fsdp"]),
        mesh=mesh,
        in_specs=(rows,) * 4 + weights + (P(None, "dp", None), P(None, "dp", None, None), P(None, "dp", None, None)),
        out_specs=(rows,) * 4 + weights,
        check_vma=False,
    )
```

```python
import functools
import math

import jax
import jax.numpy as jnp
from jax import lax
from jax.experimental import pallas as pl
from jax.experimental.pallas import tpu as pltpu
from jax.sharding import PartitionSpec as P

H = 8
DH = 128
CH = 64
SEG = 128
TRUNK = 4
BRANCHES = 2
NBUCK = 32
SELF_SCORE = -10000.0
NEG_SCORE = -1e30
EPSILON = 1e-06
BF = jnp.bfloat16
F32 = jnp.float32
AXES = ("dp", "fsdp")
GELU_A = math.sqrt(2.0 / math.pi)
GELU_B = 0.044715


def norm_stats(values):
    center = values - jnp.mean(values, axis=-1, keepdims=True)
    factor = lax.rsqrt(jnp.mean(center * center, axis=-1, keepdims=True) + EPSILON)
    return center * factor, factor


def norm_back(unit, factor, gain_vec, grad):
    scaled = grad * gain_vec
    inner = jnp.mean(scaled * unit, axis=-1, keepdims=True)
    return factor * (scaled - jnp.mean(scaled, axis=-1, keepdims=True) - unit * inner)


def position_codes(bucket_rows):
    rounds, tree_len = bucket_rows.shape
    buckets_t = bucket_rows.T
    lanes = jnp.arange(rounds * NBUCK, dtype=jnp.int32)
    member = (jnp.repeat(buckets_t, NBUCK, axis=1) == (lanes % NBUCK)[None, :]).astype(F32)
    rows = jnp.arange(tree_len, dtype=jnp.int32)
    lower = (rows[:, None] >= rows[None, :]).astype(BF)
    ranks = jnp.dot(lower, member.astype(BF), preferred_element_type=F32)
    totals = ranks[-1]
    before = ((lanes[:, None] // NBUCK == lanes[None, :] // NBUCK) & (lanes[:, None] < lanes[None, :])).astype(F32)
    offsets = jnp.sum(totals[:, None] * before, axis=0)
    places = jnp.sum((member * (ranks - 1.0 + offsets[None, :])).reshape(tree_len, rounds, NBUCK), axis=-1)
    return buckets_t.astype(F32) * tree_len + jnp.floor((places + 0.5) / CH)


def seg_parts(seg, info_ref):
    parts = []
    prefix = min(seg, TRUNK) * SEG
    if prefix:
        parts.append((0, prefix, 0, False))
    if seg >= TRUNK + BRANCHES:
        start = pl.multiple_of(info_ref[seg] * SEG, SEG)
        parts.append((start, SEG, TRUNK * SEG, False))
    parts.append((seg * SEG, SEG, (TRUNK + 1) * SEG, True))
    return parts


def unit_rows(rows_f32):
    factor = lax.rsqrt(jnp.mean(rows_f32 * rows_f32, axis=-1, keepdims=True) + EPSILON)
    return rows_f32 * factor * (1.0 / math.sqrt(DH)), factor


def own_diagonal():
    row = lax.broadcasted_iota(jnp.int32, (SEG, SEG), 0)
    col = lax.broadcasted_iota(jnp.int32, (SEG, SEG), 1)
    return row == col


def attention_forward_kernel(segments, rounds, info_ref, q_ref, v_ref, cq_ref, ck_ref, out_ref, total_ref, count_ref, unit_ref):
    head = pl.program_id(0)

    @pl.when(head == 0)
    def _():
        row = lax.broadcasted_iota(jnp.int32, (SEG, SEG), 0)
        col = lax.broadcasted_iota(jnp.int32, (SEG, SEG), 1)
        total_ref[...] = jnp.zeros_like(total_ref)
        for seg in range(segments):
            query = cq_ref[seg * SEG:(seg + 1) * SEG, :]
            for start, size, column, own in seg_parts(seg, info_ref):
                for piece in range(size // SEG):
                    first = start + piece * SEG
                    key = ck_ref[:, pl.ds(first, SEG)]
                    counted = jnp.zeros((SEG, SEG), F32)
                    for turn in range(rounds):
                        gap = query[:, turn:turn + 1] - key[turn:turn + 1, :]
                        counted = counted + jnp.where(jnp.abs(gap - 0.5) < 0.75, 1.0, 0.0)
                    if own:
                        counted = jnp.where(row >= col, counted, 0.0)
                    elif column == 0 and seg >= TRUNK:
                        counted = counted * jnp.where(info_ref[segments + seg] >= piece, 1.0, 0.0)
                    begin = column + piece * SEG
                    count_ref[seg * SEG:(seg + 1) * SEG, begin:begin + SEG] = counted.astype(BF)

    unit_ref[...] = unit_rows(q_ref[...].astype(F32))[0].astype(BF)
    diagonal = own_diagonal()
    lane = lax.broadcasted_iota(jnp.int32, (SEG, 128), 1)
    for seg in range(segments):
        rows = slice(seg * SEG, (seg + 1) * SEG)
        query = q_ref[rows, :]
        scored = []
        top = None
        for start, size, column, own in seg_parts(seg, info_ref):
            keys = pl.ds(start, size)
            scores = lax.dot_general(query, unit_ref[keys, :], (((1,), (1,)), ((), ())), preferred_element_type=F32)
            counted = count_ref[rows, column:column + size].astype(F32)
            if own:
                scores = jnp.where(diagonal, SELF_SCORE, scores)
            scores = jnp.where(counted > 0.0, scores, NEG_SCORE)
            best = jnp.max(scores, axis=-1, keepdims=True)
            top = best if top is None else jnp.maximum(top, best)
            scored.append((keys, scores, counted))
        amount = jnp.zeros((SEG, 1), F32)
        result = jnp.zeros((SEG, DH), F32)
        for keys, scores, counted in scored:
            weight = counted * jnp.exp(scores - top)
            amount = amount + jnp.sum(weight, axis=-1, keepdims=True)
            result = result + jnp.dot(weight.astype(BF), v_ref[keys, :], preferred_element_type=F32)
        out_ref[rows, :] = (result / amount).astype(BF)
        total = top + jnp.log(amount)
        total_ref[rows, :] = jnp.where(lane == head, total, total_ref[rows, :])


def attention_backward_kernel(segments, info_ref, q_ref, v_ref, out_ref, grad_ref, total_ref, count_ref, dq_ref, dv_ref, unit_ref, chance_ref, slope_ref, key_acc, value_acc, query_acc):
    head = pl.program_id(0)
    trunk = TRUNK * SEG
    whole = q_ref[...].astype(F32)
    unit, factor = unit_rows(whole)
    unit_ref[...] = unit.astype(BF)

    @pl.when(head == 0)
    def _():
        chance_ref[0:trunk, 0:trunk] = jnp.zeros((trunk, trunk), BF)
        slope_ref[0:trunk, 0:trunk] = jnp.zeros((trunk, trunk), BF)

    diagonal = own_diagonal()
    lane = lax.broadcasted_iota(jnp.int32, (SEG, 128), 1)
    for seg in range(segments):
        rows = slice(seg * SEG, (seg + 1) * SEG)
        query = q_ref[rows, :]
        grad = grad_ref[rows, :]
        total = jnp.sum(jnp.where(lane == head, total_ref[rows, :], 0.0), axis=-1, keepdims=True)
        delta = jnp.sum(grad.astype(F32) * out_ref[rows, :].astype(F32), axis=-1, keepdims=True)
        query_grad = jnp.zeros((SEG, DH), F32)
        for start, size, column, own in seg_parts(seg, info_ref):
            keys = pl.ds(start, size)
            scores = lax.dot_general(query, unit_ref[keys, :], (((1,), (1,)), ((), ())), preferred_element_type=F32)
            counted = count_ref[rows, column:column + size].astype(F32)
            if own:
                scores = jnp.where(diagonal, SELF_SCORE, scores)
            scores = jnp.where(counted > 0.0, scores, NEG_SCORE)
            chance = counted * jnp.exp(scores - total)
            reach = lax.dot_general(grad, v_ref[keys, :], (((1,), (1,)), ((), ())), preferred_element_type=F32)
            slope = chance * (reach - delta)
            if own:
                slope = jnp.where(diagonal, 0.0, slope)
            slope = slope.astype(BF)
            chance_ref[rows, column:column + size] = chance.astype(BF)
            slope_ref[rows, column:column + size] = slope
            query_grad = query_grad + jnp.dot(slope, unit_ref[keys, :], preferred_element_type=F32)
        query_acc[rows, :] = query_grad

    for weight_ref, side_ref, acc in ((chance_ref, grad_ref, value_acc), (slope_ref, q_ref, key_acc)):
        acc[0:trunk, :] = lax.dot_general(weight_ref[:, 0:trunk], side_ref[...], (((0,), (0,)), ((), ())), preferred_element_type=F32)
        for seg in range(segments):
            rows = slice(seg * SEG, (seg + 1) * SEG)
            leaf = seg >= TRUNK + BRANCHES
            begin = trunk if leaf else trunk + SEG
            added = lax.dot_general(weight_ref[rows, begin:trunk + 2 * SEG], side_ref[rows, :], (((0,), (0,)), ((), ())), preferred_element_type=F32)
            if leaf:
                above = pl.ds(pl.multiple_of(info_ref[seg] * SEG, SEG), SEG)
                acc[above, :] += added[0:SEG]
                added = added[SEG:]
            acc[rows, :] = added if seg >= TRUNK else acc[rows, :] + added

    key_grad = key_acc[...]
    along = jnp.mean(key_grad * whole, axis=-1, keepdims=True) * (factor * factor)
    dq_ref[...] = (query_acc[...] + (factor * (1.0 / math.sqrt(DH))) * (key_grad - whole * along)).astype(BF)
    dv_ref[...] = value_acc[...].astype(BF)


def attention_calls(tree_len, local_heads, rounds, segments):
    head_spec = pl.BlockSpec((tree_len, DH), lambda h, info: (0, h))
    side = pl.BlockSpec((tree_len, 128), lambda h, info: (0, 0))
    count_spec = pl.BlockSpec((tree_len, (TRUNK + 2) * SEG), lambda h, info: (0, 0))
    wide = local_heads * DH
    forward = pl.pallas_call(
        functools.partial(attention_forward_kernel, segments, rounds),
        grid_spec=pltpu.PrefetchScalarGridSpec(
            num_scalar_prefetch=1,
            grid=(local_heads,),
            in_specs=[head_spec, head_spec, side, pl.BlockSpec((8, tree_len), lambda h, info: (0, 0))],
            out_specs=[head_spec, side, count_spec],
            scratch_shapes=[pltpu.VMEM((tree_len, DH), BF)],
        ),
        out_shape=[
            jax.ShapeDtypeStruct((tree_len, wide), BF),
            jax.ShapeDtypeStruct((tree_len, 128), F32),
            jax.ShapeDtypeStruct((tree_len, (TRUNK + 2) * SEG), BF),
        ],
        compiler_params=pltpu.CompilerParams(vmem_limit_bytes=40 << 20),
        name="attention_forward",
    )
    backward = pl.pallas_call(
        functools.partial(attention_backward_kernel, segments),
        grid_spec=pltpu.PrefetchScalarGridSpec(
            num_scalar_prefetch=1,
            grid=(local_heads,),
            in_specs=[head_spec, head_spec, head_spec, head_spec, side, count_spec],
            out_specs=[head_spec, head_spec],
            scratch_shapes=[pltpu.VMEM((tree_len, DH), BF)]
            + [pltpu.VMEM((tree_len, (TRUNK + 2) * SEG), BF)] * 2
            + [pltpu.VMEM((tree_len, DH), F32)] * 3,
        ),
        out_shape=[jax.ShapeDtypeStruct((tree_len, wide), BF)] * 2,
        compiler_params=pltpu.CompilerParams(vmem_limit_bytes=40 << 20),
        name="attention_backward",
    )
    return forward, backward


def row_block(where_fn, coords_ref, span):
    return pl.ds(pl.multiple_of(where_fn(coords_ref) * span, span), span)


def piece_view(refs, piece):
    view = refs[piece[0]].at[piece[1]] if piece[1] else refs[piece[0]]
    return view if piece[2] is None else view.at[pl.ds(piece[2], piece[3])]


def load_pieces(coords_ref, refs, pieces, target, sems, first):
    copies = []
    for number, piece in enumerate(pieces):
        span = piece[3]
        copies.append(pltpu.make_async_copy(piece_view(refs, piece), target.at[row_block(piece[4], coords_ref, span)], sems.at[first + number]))
    return copies


def store_pieces(coords_ref, source, refs, pieces, sems, first):
    copies = []
    for number, piece in enumerate(pieces):
        span = piece[3]
        copies.append(pltpu.make_async_copy(source.at[row_block(piece[4], coords_ref, span)], piece_view(refs, piece), sems.at[first + number]))
    return copies


def project_kernel(q_pieces, v_pieces, q_count, v_count, coords_ref, mixed_ref, *refs):
    q_refs, v_refs = refs[:q_count], refs[q_count:q_count + v_count]
    q_out, v_out, q_weight, v_weight, sems = refs[q_count + v_count:]
    to_q = load_pieces(coords_ref, q_refs, q_pieces, q_weight, sems, 0)
    to_v = load_pieces(coords_ref, v_refs, v_pieces, v_weight, sems, len(q_pieces))
    for copy in to_q + to_v:
        copy.start()
    for copy in to_q:
        copy.wait()
    q_out[...] = jnp.dot(mixed_ref[...], q_weight[...], preferred_element_type=F32).astype(BF)
    for copy in to_v:
        copy.wait()
    v_out[...] = jnp.dot(mixed_ref[...], v_weight[...], preferred_element_type=F32).astype(BF)


VM = pl.BlockSpec(memory_space=pltpu.VMEM)
ANYWHERE = pl.BlockSpec(memory_space=pl.ANY)


def kernel_call(body, ins, outs, scratch, name, limit, grid=(), semantics=None):
    return pl.pallas_call(
        body,
        grid_spec=pltpu.PrefetchScalarGridSpec(num_scalar_prefetch=1, grid=grid, in_specs=ins, out_specs=outs[0], scratch_shapes=scratch),
        out_shape=outs[1],
        compiler_params=pltpu.CompilerParams(vmem_limit_bytes=limit << 20),
        name=name,
    )


def project(coords, mixed_tree, q_side, v_side, wide):
    q_arrays, q_pieces = q_side
    v_arrays, v_pieces = v_side
    rows, features = mixed_tree.shape
    body = functools.partial(project_kernel, q_pieces, v_pieces, len(q_arrays), len(v_arrays))
    return kernel_call(
        body,
        [VM] + [ANYWHERE] * (len(q_arrays) + len(v_arrays)),
        ([VM, VM], [jax.ShapeDtypeStruct((rows, wide), BF)] * 2),
        [pltpu.VMEM((features, wide), BF)] * 2 + [pltpu.SemaphoreType.DMA((len(q_pieces) + len(v_pieces),))],
        "project",
        40,
    )(coords, mixed_tree, *q_arrays, *v_arrays)


def project_back_kernel(q_pieces, v_pieces, q_count, v_count, q_outs, v_outs, q_made, v_made, coords_ref, mixed_ref, dq_ref, dv_ref, *refs):
    q_refs, v_refs = refs[:q_count], refs[q_count:q_count + v_count]
    rest = refs[q_count + v_count:]
    partial_ref = rest[0]
    q_grads, v_grads = rest[1:1 + q_made], rest[1 + q_made:1 + q_made + v_made]
    q_weight, v_weight, q_sum, v_sum, sems = rest[1 + q_made + v_made:]
    to_q = load_pieces(coords_ref, q_refs, q_pieces, q_weight, sems, 0)
    to_v = load_pieces(coords_ref, v_refs, v_pieces, v_weight, sems, len(q_pieces))
    for copy in to_q + to_v:
        copy.start()
    used = len(q_pieces) + len(v_pieces)
    turned = (((0,), (0,)), ((), ()))
    crossed = (((1,), (1,)), ((), ()))
    q_sum[...] = lax.dot_general(mixed_ref[...], dq_ref[...], turned, preferred_element_type=F32).astype(BF)
    from_q = store_pieces(coords_ref, q_sum, q_grads, q_outs, sems, used)
    for copy in from_q:
        copy.start()
    v_sum[...] = lax.dot_general(mixed_ref[...], dv_ref[...], turned, preferred_element_type=F32).astype(BF)
    from_v = store_pieces(coords_ref, v_sum, v_grads, v_outs, sems, used + len(q_outs))
    for copy in from_v:
        copy.start()
    for copy in to_q + to_v:
        copy.wait()
    partial_ref[...] = (
        lax.dot_general(dq_ref[...], q_weight[...], crossed, preferred_element_type=F32)
        + lax.dot_general(dv_ref[...], v_weight[...], crossed, preferred_element_type=F32)
    ).astype(BF)
    for copy in from_q + from_v:
        copy.wait()


def project_back(coords, mixed_tree, dq, dv, q_side, v_side, q_form, v_form):
    q_arrays, q_pieces = q_side
    v_arrays, v_pieces = v_side
    q_shapes, q_outs = q_form
    v_shapes, v_outs = v_form
    rows, features = mixed_tree.shape
    wide = dq.shape[1]
    body = functools.partial(
        project_back_kernel, q_pieces, v_pieces, len(q_arrays), len(v_arrays), q_outs, v_outs, len(q_shapes), len(v_shapes)
    )
    made = kernel_call(
        body,
        [VM] * 3 + [ANYWHERE] * (len(q_arrays) + len(v_arrays)),
        (
            [VM] + [ANYWHERE] * (len(q_shapes) + len(v_shapes)),
            [jax.ShapeDtypeStruct((rows, features), BF)] + [jax.ShapeDtypeStruct(s, BF) for s in q_shapes + v_shapes],
        ),
        [pltpu.VMEM((features, wide), BF)] * 4
        + [pltpu.SemaphoreType.DMA((len(q_pieces) + len(v_pieces) + len(q_outs) + len(v_outs),))],
        "project_back",
        50,
    )(coords, mixed_tree, dq, dv, *q_arrays, *v_arrays)
    return made[0], made[1:1 + len(q_shapes)], made[1 + len(q_shapes):]


def normalised(values):
    center = values - jnp.mean(values, axis=-1, keepdims=True)
    factor = lax.rsqrt(jnp.mean(center * center, axis=-1, keepdims=True) + EPSILON)
    return center * factor, factor


def out_kernel(pieces, count, coords_ref, att_ref, first_ref, gain_ref, shift_ref, *refs):
    o_refs = refs[:count]
    first_out, feed_out, weight, sems = refs[count:]
    copies = load_pieces(coords_ref, o_refs, pieces, weight, sems, 0)
    for copy in copies:
        copy.start()
    for copy in copies:
        copy.wait()
    made = first_ref[...] + jnp.dot(att_ref[...], weight[...], preferred_element_type=F32)
    first_out[...] = made
    feed_out[...] = (normalised(made)[0] * gain_ref[...] + shift_ref[...]).astype(BF)


def out_project(coords, att, first, gain, shift, side):
    arrays, pieces = side
    rows, features = first.shape
    return kernel_call(
        functools.partial(out_kernel, pieces, len(arrays)),
        [VM] * 4 + [ANYWHERE] * len(arrays),
        ([VM, VM], [jax.ShapeDtypeStruct((rows, features), F32), jax.ShapeDtypeStruct((rows, features), BF)]),
        [pltpu.VMEM((features, features), BF), pltpu.SemaphoreType.DMA((len(pieces),))],
        "out_project",
        50,
    )(coords, att, first, gain, shift, *arrays)


def out_back_kernel(pieces, count, outs, made, coords_ref, back_ref, first_ref, grad_ref, att_ref, gain_ref, *refs):
    o_refs = refs[:count]
    rest = refs[count:]
    grad_in, grad_att, gain_sum, shift_sum = rest[:4]
    grads = rest[4:4 + made]
    weight, total, sems = rest[4 + made:]
    copies = load_pieces(coords_ref, o_refs, pieces, weight, sems, 0)
    for copy in copies:
        copy.start()
    back = back_ref[...]
    unit, factor = normalised(first_ref[...])
    gain_sum[...] = jnp.sum(back * unit, axis=0, keepdims=True)
    shift_sum[...] = jnp.sum(back, axis=0, keepdims=True)
    scaled = back * gain_ref[...]
    inner = jnp.mean(scaled * unit, axis=-1, keepdims=True)
    value = grad_ref[...] + factor * (scaled - jnp.mean(scaled, axis=-1, keepdims=True) - unit * inner)
    grad_in[...] = value
    low = value.astype(BF)
    total[...] = lax.dot_general(att_ref[...], low, (((0,), (0,)), ((), ())), preferred_element_type=F32).astype(BF)
    stores = store_pieces(coords_ref, total, grads, outs, sems, len(pieces))
    for copy in stores:
        copy.start()
    for copy in copies:
        copy.wait()
    grad_att[...] = lax.dot_general(low, weight[...], (((1,), (1,)), ((), ())), preferred_element_type=F32).astype(BF)
    for copy in stores:
        copy.wait()


def out_back(coords, back, first_out, grad, att, gain, side, form):
    arrays, pieces = side
    shapes, outs = form
    rows, features = back.shape
    full = jax.ShapeDtypeStruct((rows, features), F32)
    line = jax.ShapeDtypeStruct((1, features), F32)
    made = kernel_call(
        functools.partial(out_back_kernel, pieces, len(arrays), outs, len(shapes)),
        [VM] * 5 + [ANYWHERE] * len(arrays),
        (
            [VM] * 4 + [ANYWHERE] * len(shapes),
            [full, jax.ShapeDtypeStruct((rows, features), BF), line, line] + [jax.ShapeDtypeStruct(s, BF) for s in shapes],
        ),
        [pltpu.VMEM((features, features), BF)] * 2 + [pltpu.SemaphoreType.DMA((len(pieces) + len(outs),))],
        "out_back",
        60,
    )(coords, back, first_out, grad, att, gain, *arrays)
    return made[:4], made[4:]


def feed_kernel(plan, counts, coords_ref, feed_ref, grad_ref, bias_ref, *refs):
    i_pieces, i_outs, steps, step_outs = plan
    i_count, u_count, i_made, u_made = counts
    i_refs, u_refs = refs[:i_count], refs[i_count:i_count + u_count]
    rest = refs[i_count + u_count:]
    out_ref, back_ref, bias_sum = rest[:3]
    i_grads, u_grads = rest[3:3 + i_made], rest[3 + i_made:3 + i_made + u_made]
    weight, weight_sum, outer, outer_sum, i_sems, u_sems, iout_sems, uout_sems = rest[3 + i_made + u_made:]
    step = pl.program_id(0)
    slot = lax.rem(step, 2)
    tile = outer.shape[1]
    count = len(steps)

    def u_load(number):
        return load_pieces(coords_ref, u_refs, steps[number][1], outer.at[number % 2], u_sems.at[number % 2], 0)

    def u_store(number):
        return store_pieces(coords_ref, outer_sum.at[number % 2], u_grads, step_outs[number], uout_sems.at[number % 2], 0)

    @pl.when(step == 0)
    def _():
        copies = load_pieces(coords_ref, i_refs, i_pieces, weight, i_sems, 0)
        for copy in copies + u_load(0):
            copy.start()
        out_ref[...] = jnp.zeros_like(out_ref)
        back_ref[...] = jnp.zeros_like(back_ref)
        for copy in copies:
            copy.wait()

    block = jnp.int32(0)
    for number in range(count):
        block = jnp.where(step == number, steps[number][0](coords_ref), block)

        @pl.when(step == number)
        def _(number=number):
            if number + 1 < count:
                for copy in u_load(number + 1):
                    copy.start()
            if number >= 2:
                for copy in u_store(number - 2):
                    copy.wait()
            for copy in u_load(number):
                copy.wait()

    columns = pl.ds(pl.multiple_of(block * tile, tile), tile)
    feed = feed_ref[...]
    grad = grad_ref[...]
    inner = weight[:, columns]
    value = jnp.dot(feed, inner, preferred_element_type=F32) + bias_ref[:, columns]
    square = value * value
    bend = jnp.tanh(GELU_A * (value + GELU_B * (square * value)))
    half = 0.5 * (1.0 + bend)
    active = (value * half).astype(BF)
    slope = half + 0.5 * value * (1.0 - bend * bend) * (GELU_A * (1.0 + 3.0 * GELU_B * square))
    out_ref[...] += jnp.dot(active, outer[slot], preferred_element_type=F32)
    outer_sum[slot] = lax.dot_general(active, grad, (((0,), (0,)), ((), ())), preferred_element_type=F32).astype(BF)
    pulled = lax.dot_general(grad, outer[slot], (((1,), (1,)), ((), ())), preferred_element_type=F32)
    inner_low = (pulled * slope).astype(BF)
    bias_sum[:, columns] = jnp.sum(inner_low.astype(F32), axis=0, keepdims=True)
    weight_sum[:, columns] = lax.dot_general(feed, inner_low, (((0,), (0,)), ((), ())), preferred_element_type=F32).astype(BF)
    back_ref[...] += lax.dot_general(inner_low, inner, (((1,), (1,)), ((), ())), preferred_element_type=F32)

    for number in range(count):

        @pl.when(step == number)
        def _(number=number):
            for copy in u_store(number):
                copy.start()
            if number == count - 1:
                copies = store_pieces(coords_ref, weight_sum, i_grads, i_outs, iout_sems, 0)
                for copy in copies:
                    copy.start()
                if count > 1:
                    for copy in u_store(number - 1):
                        copy.wait()
                for copy in u_store(number):
                    copy.wait()
                for copy in copies:
                    copy.wait()


def feed_call(coords, feed, grad, bias, i_side, u_side, i_form, u_form):
    i_arrays, i_pieces = i_side
    u_arrays, steps = u_side
    i_shapes, i_outs = i_form
    u_shapes, step_outs = u_form
    rows, features = feed.shape
    hidden = bias.shape[1]
    tile = hidden // len(steps)
    most = max(len(pieces) for _, pieces in steps)
    made = kernel_call(
        functools.partial(feed_kernel, (i_pieces, i_outs, steps, step_outs), (len(i_arrays), len(u_arrays), len(i_shapes), len(u_shapes))),
        [VM] * 3 + [ANYWHERE] * (len(i_arrays) + len(u_arrays)),
        (
            [VM] * 3 + [ANYWHERE] * (len(i_shapes) + len(u_shapes)),
            [jax.ShapeDtypeStruct((rows, features), F32)] * 2
            + [jax.ShapeDtypeStruct((1, hidden), F32)]
            + [jax.ShapeDtypeStruct(s, BF) for s in i_shapes + u_shapes],
        ),
        [
            pltpu.VMEM((features, hidden), BF),
            pltpu.VMEM((features, hidden), BF),
            pltpu.VMEM((2, tile, features), BF),
            pltpu.VMEM((2, tile, features), BF),
            pltpu.SemaphoreType.DMA((len(i_pieces),)),
            pltpu.SemaphoreType.DMA((2, most)),
            pltpu.SemaphoreType.DMA((len(i_outs),)),
            pltpu.SemaphoreType.DMA((2, most)),
        ],
        "feed_forward_backward",
        60,
        grid=(len(steps),),
    )(coords, feed, grad, bias, *i_arrays, *u_arrays)
    return made[0], made[1], made[2], made[3:3 + len(i_shapes)], made[3 + len(i_shapes):]


def pick(flag, when_true, when_false):
    return jnp.where(flag, when_true, when_false)


class PairPlan:
    def __init__(self):
        me = lax.axis_index("fsdp")
        self.upper = me // 2 == 1
        self.odd = me % 2 == 1
        self.tree = me // 2
        self.head_group = me % 2

    def near(self, value):
        return lax.ppermute(value, "fsdp", [(i, i ^ 1) for i in range(4)])

    def far(self, value):
        return lax.ppermute(value, "fsdp", [(i, i ^ 2) for i in range(4)])

    def rows_to_tree(self, rows):
        mine = pick(self.upper, rows[1], rows[0])
        got = self.far(pick(self.upper, rows[0], rows[1]))
        pair = jnp.stack([pick(self.upper, got, mine), pick(self.upper, mine, got)])
        other = self.near(pair)
        whole = jnp.stack([pick(self.odd, other, pair), pick(self.odd, pair, other)], axis=1)
        return whole.reshape((-1, rows.shape[2]))

    def heads_to_rows(self, heads):
        blocks = heads.reshape(2, 2, -1, heads.shape[1])
        keep = pick(self.odd, blocks[:, 1], blocks[:, 0])
        got = self.near(pick(self.odd, blocks[:, 0], blocks[:, 1]))
        full = jnp.concatenate([pick(self.odd, got, keep), pick(self.odd, keep, got)], axis=-1)
        return self.swap_trees(full)

    def swap_trees(self, full):
        mine = pick(self.upper, full[1], full[0])
        got = self.far(pick(self.upper, full[0], full[1]))
        return jnp.stack([pick(self.upper, got, mine), pick(self.upper, mine, got)])

    def rows_to_heads(self, rows):
        wide = rows.shape[2] // 2
        mine = pick(self.upper, rows[1], rows[0])
        got = self.far(pick(self.upper, rows[0], rows[1]))
        pair = jnp.stack([pick(self.upper, got, mine), pick(self.upper, mine, got)])
        keep = pick(self.odd, pair[..., wide:], pair[..., :wide])
        other = self.near(pick(self.odd, pair[..., :wide], pair[..., wide:]))
        whole = jnp.stack([pick(self.odd, other, keep), pick(self.odd, keep, other)], axis=1)
        return whole.reshape((-1, wide))

    def partial_to_rows(self, partial):
        blocks = partial.reshape(2, 2, -1, partial.shape[1])
        keep = pick(self.odd, blocks[:, 1], blocks[:, 0])
        got = self.near(pick(self.odd, blocks[:, 0], blocks[:, 1]).astype(BF))
        return self.swap_trees((keep.astype(F32) + got.astype(F32)).astype(BF)).astype(F32)


class GroupPlan:
    def __init__(self, size, trees):
        me = lax.axis_index("fsdp")
        self.size = size
        self.trees = trees
        self.group = size // trees
        self.tree = me // self.group
        self.head_group = me % self.group
        self.me = me

    def rows_to_tree(self, rows):
        every = lax.all_gather(rows, "fsdp", axis=1, tiled=True)
        return lax.dynamic_index_in_dim(every, self.tree, 0, False)

    def heads_to_rows(self, heads):
        count = heads.shape[0] // self.size
        every = lax.all_gather(heads, "fsdp", axis=0, tiled=False)
        mine = lax.dynamic_slice_in_dim(every, self.me * count, count, 1)
        mine = mine.reshape(self.trees, self.group, count, heads.shape[1])
        return jnp.moveaxis(mine, 1, 2).reshape(self.trees, count, -1)

    def rows_to_heads(self, rows):
        wide = rows.shape[2] // self.group
        whole = self.rows_to_tree(rows)
        return lax.dynamic_slice_in_dim(whole, self.head_group * wide, wide, 1)

    def partial_to_rows(self, partial):
        every = jnp.zeros((self.trees,) + partial.shape, F32)
        every = lax.dynamic_update_index_in_dim(every, partial.astype(F32), self.tree, 0)
        return lax.psum_scatter(every, "fsdp", scatter_dimension=1, tiled=True)


def low(value):
    return value.astype(BF)


def wide_of(value):
    return value.astype(F32)


def swap_pairs(size, bit):
    return [(i, i ^ bit) for i in range(size)]


class LinkMoves:
    def __init__(self):
        dp, fsdp = lax.axis_index("dp"), lax.axis_index("fsdp")
        self.bits = [fsdp % 2, fsdp // 2, dp % 2, dp // 2 % 2, dp // 4]
        self.coords = jnp.stack([dp // 2, dp % 2, fsdp // 2, fsdp % 2]).astype(jnp.int32)
        self.odd = fsdp % 2 == 1

    def core(self, value):
        return lax.ppermute(value, "fsdp", swap_pairs(4, 1))

    def over_y(self, value):
        return lax.ppermute(value, "fsdp", swap_pairs(4, 2))

    def over_x(self, value):
        return lax.ppermute(value, "dp", swap_pairs(8, 1))

    def up_z(self, value):
        return lax.ppermute(value, "dp", [(i, (i + 2) % 8) for i in range(8)])

    def bit_move(self, bit, value):
        if bit < 2:
            return lax.ppermute(value, "fsdp", swap_pairs(4, 1 << bit))
        return lax.ppermute(value, "dp", swap_pairs(8, 1 << (bit - 2)))

    def ring(self, value):
        made = [value]
        for _ in range(3):
            made.append(self.up_z(made[-1]))
        return made

    def ring_sum(self, blocks):
        total = blocks[1]
        for k in (2, 3, 0):
            total = wide_of(self.up_z(low(total))) + blocks[k]
        return total

    def gather_small(self, shard):
        made = shard
        for bit in range(5):
            got = self.bit_move(bit, made)
            one = self.bits[bit] == 1
            made = pick(one, jnp.concatenate([got, made]), jnp.concatenate([made, got]))
        return made

    def scatter_small(self, total):
        made = total
        for bit in (4, 3, 2, 1, 0):
            half = made.shape[0] // 2
            one = self.bits[bit] == 1
            keep = pick(one, made[half:], made[:half])
            made = keep + self.bit_move(bit, pick(one, made[:half], made[half:]))
        return made

    @staticmethod
    def place32(k, rx, ry, rc):
        return lambda co: ((((co[0] + 4 - k) & 3) * 2 + (co[1] ^ rx)) * 2 + (co[2] ^ ry)) * 2 + (co[3] ^ rc)

    @staticmethod
    def place16(k, rx, ry):
        return lambda co: (((co[0] + 4 - k) & 3) * 2 + (co[1] ^ rx)) * 2 + (co[2] ^ ry)

    @staticmethod
    def place8(k, rx):
        return lambda co: ((co[0] + 4 - k) & 3) * 2 + (co[1] ^ rx)

    @staticmethod
    def place4(ry, rc):
        return lambda co: (co[2] ^ ry) * 2 + (co[3] ^ rc)

    def gather_heads(self, query, value):
        count, features = query.shape
        half = features // 2
        both = jnp.stack([query, value])
        keep = pick(self.odd, both[:, :, half:], both[:, :, :half])
        got = self.core(pick(self.odd, both[:, :, :half], both[:, :, half:]))
        chip = pick(self.odd, jnp.concatenate([got, keep], axis=1), jnp.concatenate([keep, got], axis=1))
        made = self.ring(chip)
        sides = []
        for which, first, second in ((0, self.over_y, self.over_x), (1, self.over_x, self.over_y)):
            near = jnp.stack([m[which] for m in made])
            near = jnp.stack([near, first(near)])
            arrays = [near, second(near)]
            pieces = []
            for outer in range(2):
                for inner in range(2):
                    for k in range(4):
                        rx, ry = (outer, inner) if which == 0 else (inner, outer)
                        pieces.append((outer, (inner, k), None, 2 * count, self.place16(k, rx, ry)))
            sides.append((arrays, pieces))
        return sides

    def heads_form(self, count, half):
        shapes = [(2, 4, 2 * count, half)] * 2
        forms = []
        for which in range(2):
            pieces = []
            for outer in range(2):
                for inner in range(2):
                    for k in range(4):
                        rx, ry = (outer, inner) if which == 0 else (inner, outer)
                        pieces.append((outer, (inner, k), None, 2 * count, self.place16(k, rx, ry)))
            forms.append((shapes, pieces))
        return forms

    def sum_heads(self, query, value):
        totals = []
        for parts, first, second in ((query, self.over_x, self.over_y), (value, self.over_y, self.over_x)):
            made = wide_of(parts[0]) + wide_of(first(parts[1]))
            made = made[0] + wide_of(second(low(made[1])))
            totals.append(self.ring_sum([made[k] for k in range(4)]))
        both = jnp.stack(totals)
        count = both.shape[1] // 2
        keep = pick(self.odd, both[:, count:], both[:, :count])
        got = wide_of(self.core(low(pick(self.odd, both[:, :count], both[:, count:]))))
        full = pick(self.odd, jnp.concatenate([got, keep], axis=2), jnp.concatenate([keep, got], axis=2))
        return full[0], full[1]

    def gather_inner(self, shard):
        near = jnp.stack([shard, self.over_y(shard)])
        plane = jnp.stack([near, self.over_x(near)])
        made = self.ring(plane)
        arrays = made + [self.core(m) for m in made]
        count = shard.shape[0]
        pieces = [
            (rc * 4 + k, (rx, ry), None, count, self.place32(k, rx, ry, rc))
            for rc in range(2)
            for k in range(4)
            for rx in range(2)
            for ry in range(2)
        ]
        return arrays, pieces

    def inner_form(self, count, hidden):
        pieces = [
            (rc * 4 + k, (rx, ry), None, count, self.place32(k, rx, ry, rc))
            for rc in range(2)
            for k in range(4)
            for rx in range(2)
            for ry in range(2)
        ]
        return [(2, 2, count, hidden)] * 8, pieces

    def sum_inner(self, parts):
        shares = [None] * 4
        for k in (1, 2, 3, 0):
            shares[k] = wide_of(parts[k]) + wide_of(self.core(parts[4 + k]))
        made = self.ring_sum(shares)
        made = made[0] + wide_of(self.over_x(low(made[1])))
        return made[0] + wide_of(self.over_y(low(made[1])))

    def gather_outer(self, outer, output):
        count, extra = outer.shape[0], output.shape[0]
        made = jnp.stack(self.ring(jnp.concatenate([outer, output])))
        near = jnp.stack([made, self.over_y(made)])
        across = self.over_x(near)
        arrays = [near, across, self.core(near), self.core(across)]
        steps = []
        for rx in range(2):
            for k in range(4):
                pieces = [(rc * 2 + rx, (ry, k), 0, count, self.place4(ry, rc)) for ry in range(2) for rc in range(2)]
                steps.append((self.place8(k, rx), pieces))
        output_pieces = [
            (rc * 2 + rx, (ry, k), count, extra, self.place32(k, rx, ry, rc))
            for rc in range(2)
            for rx in range(2)
            for ry in range(2)
            for k in range(4)
        ]
        return (arrays, steps), (arrays, output_pieces)

    def outer_form(self, count, features):
        steps = []
        for rx in range(2):
            for k in range(4):
                steps.append([(rc * 2 + rx, (ry, k), None, count, self.place4(ry, rc)) for ry in range(2) for rc in range(2)])
        return [(2, 4, count, features)] * 4, steps

    def output_form(self, count, features):
        pieces = [
            (rc * 2 + rx, (ry, k), None, count, self.place32(k, rx, ry, rc))
            for rc in range(2)
            for rx in range(2)
            for ry in range(2)
            for k in range(4)
        ]
        return [(2, 4, count, features)] * 4, pieces

    def sum_outer(self, outer, output):
        halves = []
        for parts in (outer, output):
            sent = low(wide_of(parts[1]) + wide_of(self.core(parts[3])))
            halves.append(wide_of(parts[0]) + wide_of(self.core(parts[2])) + wide_of(self.over_x(sent)))
        made = jnp.concatenate([low(h[1]) for h in halves], axis=1)
        made = wide_of(self.over_y(made)) + jnp.concatenate([h[0] for h in halves], axis=1)
        total = self.ring_sum([made[k] for k in range(4)])
        count = outer[0].shape[2]
        return total[:count], total[count:]


class PlainMoves:
    def __init__(self, plan, wide):
        self.plan = plan
        self.wide = wide
        self.coords = jnp.zeros((4,), jnp.int32)

    @staticmethod
    def start(co):
        return co[0] * 0

    def gather(self, shard):
        return lax.all_gather(shard, AXES, axis=0, tiled=True)

    def scatter(self, total):
        return lax.psum_scatter(total, AXES, scatter_dimension=0, tiled=True)

    def whole(self, rows):
        return [(0, (), None, rows, self.start)]

    def gather_small(self, shard):
        return self.gather(shard)

    def scatter_small(self, total):
        return self.scatter(total)

    def gather_heads(self, query, value):
        sides = []
        for shard in (query, value):
            cols = lax.dynamic_slice_in_dim(self.gather(shard), self.plan.head_group * self.wide, self.wide, 1)
            sides.append(([cols], self.whole(cols.shape[0])))
        return sides

    def heads_form(self, count, half):
        features = H * DH
        return [([(features, self.wide)], self.whole(features))] * 2

    def sum_heads(self, query, value):
        made = []
        for cols in (query[0], value[0]):
            full = jnp.zeros((cols.shape[0], H * DH), F32)
            made.append(self.scatter(lax.dynamic_update_slice_in_dim(full, wide_of(cols), self.plan.head_group * self.wide, 1)))
        return made

    def gather_inner(self, shard):
        full = self.gather(shard)
        self.features, self.hidden = full.shape
        return [full], self.whole(full.shape[0])

    def inner_form(self, count, hidden):
        return [(self.features, hidden)], self.whole(self.features)

    def sum_inner(self, parts):
        return self.scatter(wide_of(parts[0]))

    def gather_outer(self, outer, output):
        self.steps = self.hidden // 512
        full = self.gather(outer).reshape(self.steps, -1, outer.shape[1])
        steps = [((lambda co, s=s: co[0] * 0 + s), [(0, (s,), None, full.shape[1], self.start)]) for s in range(self.steps)]
        other = self.gather(output)
        return ([full], steps), ([other], self.whole(other.shape[0]))

    def outer_form(self, count, features):
        tile = self.hidden // self.steps
        return [(self.steps, tile, features)], [[(0, (s,), None, tile, self.start)] for s in range(self.steps)]

    def output_form(self, count, features):
        return [(H * DH, features)], self.whole(H * DH)

    def sum_outer(self, outer, output):
        return self.scatter(wide_of(outer[0]).reshape(self.hidden, -1)), self.scatter(wide_of(output[0]))


def per_device(
    first_half,
    second_half,
    grad_first,
    grad_second,
    query_weight,
    value_weight,
    output_weight,
    inner_weight,
    inner_bias,
    outer_weight,
    outer_bias,
    mixer_gain,
    mixer_shift,
    feed_gain,
    feed_shift,
    parents,
    buckets,
    order,
    *,
    dp_size,
    fsdp_size,
):
    trees = first_half.shape[0]
    row_count = first_half.shape[2]
    features = first_half.shape[3]
    hidden = inner_weight.shape[1]
    rounds = buckets.shape[2]
    tree_len = buckets.shape[3]
    segments = parents.shape[2]
    all_rows = trees * row_count
    devices = dp_size * fsdp_size
    local_heads = H // (fsdp_size // trees)
    wide = local_heads * DH
    linked = (dp_size, fsdp_size, trees) == (8, 4, 2)
    plan = PairPlan() if linked else GroupPlan(fsdp_size, trees)
    moves = LinkMoves() if linked else PlainMoves(plan, wide)
    coords = moves.coords

    first = first_half[:, 0]
    second = second_half[:, 0]
    grad_b = grad_second[:, 0]

    def flat(value):
        return value.reshape(all_rows, features)

    small_parts = (inner_bias, outer_bias, mixer_gain, mixer_shift, feed_gain, feed_shift)
    small_sizes = [v.shape[0] for v in small_parts]
    small = wide_of(moves.gather_small(jnp.concatenate(small_parts)[None]))
    vectors = []
    begin = 0
    for size in small_sizes:
        vectors.append(small[:, begin:begin + size].reshape(1, -1))
        begin += size
    bias_inner, bias_outer, gain_mix, shift_mix, gain_feed, shift_feed = vectors

    q_side, v_side = moves.gather_heads(query_weight, value_weight)
    i_side = moves.gather_inner(inner_weight)
    u_side, o_side = moves.gather_outer(outer_weight, output_weight)

    mix_unit, mix_factor = norm_stats(second)
    mixed_tree = plan.rows_to_tree(low(mix_unit * gain_mix + shift_mix))
    parent_row = lax.dynamic_index_in_dim(parents[:, 0], plan.tree, 0, False)
    bucket_rows = lax.dynamic_index_in_dim(buckets[:, 0], plan.tree, 0, False)
    branch = parent_row[jnp.clip(parent_row, 0, segments - 1)]
    trunk_end = jnp.where(jnp.arange(segments) >= TRUNK + BRANCHES, branch, parent_row)
    info = jnp.concatenate([parent_row, trunk_end])
    codes = position_codes(bucket_rows)
    codes_q = jnp.pad(codes, ((0, 0), (0, 128 - rounds)))
    codes_k = jnp.pad(codes.T, ((0, 8 - rounds), (0, 0)))
    query_key, value_rows = project(coords, mixed_tree, q_side, v_side, wide)
    attend, attend_back = attention_calls(tree_len, local_heads, rounds, segments)
    attended, totals, counts = attend(info, query_key, value_rows, codes_q, codes_k)
    attended_low = flat(plan.heads_to_rows(attended))

    first_out, feed_low = out_project(coords, attended_low, flat(first), gain_feed, shift_feed, o_side)
    outer_low = flat(low(grad_b))
    i_form = moves.inner_form(inner_weight.shape[0], hidden)
    u_form = moves.outer_form(outer_weight.shape[0], features)
    fed, grad_feed, inner_bias_sum, inner_parts, outer_parts = feed_call(coords, feed_low, outer_low, bias_inner, i_side, u_side, i_form, u_form)
    second_out = second + fed.reshape(second.shape) + bias_outer
    outer_bias_sum = jnp.sum(wide_of(outer_low), axis=0)
    (grad_first_in, grad_attended, feed_gain_sum, feed_shift_sum), output_parts = out_back(
        coords,
        grad_feed,
        first_out,
        flat(grad_first),
        attended_low,
        gain_feed,
        o_side,
        moves.output_form(output_weight.shape[0], features),
    )

    grad_heads = plan.rows_to_heads(grad_attended.reshape(trees, row_count, features))
    query_low, value_low = attend_back(info, query_key, value_rows, attended, grad_heads, totals, counts)
    q_form, v_form = moves.heads_form(query_weight.shape[0], wide)
    partial, query_parts, value_parts = project_back(coords, mixed_tree, query_low, value_low, q_side, v_side, q_form, v_form)
    grad_mixed = plan.partial_to_rows(partial)
    mix_gain_sum = jnp.sum(grad_mixed * mix_unit, axis=(0, 1))
    mix_shift_sum = jnp.sum(grad_mixed, axis=(0, 1))
    grad_second_in = grad_b + norm_back(mix_unit, mix_factor, gain_mix, grad_mixed)

    inner_grad = moves.sum_inner(inner_parts)
    outer_grad, output_grad = moves.sum_outer(outer_parts, output_parts)
    query_grad, value_grad = moves.sum_heads(query_parts, value_parts)
    small_sums = [inner_bias_sum, outer_bias_sum, mix_gain_sum, mix_shift_sum, feed_gain_sum, feed_shift_sum]
    packed = moves.scatter_small(jnp.concatenate([v.reshape(devices, -1) for v in small_sums], axis=1))[0]
    pieces = []
    begin = 0
    for size in small_sizes:
        pieces.append(packed[begin:begin + size])
        begin += size
    return (
        first_out.reshape(first_half.shape),
        second_out[:, None],
        grad_first_in.reshape(first_half.shape),
        grad_second_in[:, None],
        query_grad,
        value_grad,
        output_grad,
        inner_grad,
        pieces[0],
        outer_grad,
        pieces[1],
        pieces[2],
        pieces[3],
        pieces[4],
        pieces[5],
    )


def solution(mesh):
    rows = P(None, "dp", "fsdp", None)
    matrix = P(AXES, None)
    vector = P(AXES)
    weights = (matrix, matrix, matrix, matrix, vector, matrix, vector, vector, vector, vector, vector)
    return jax.shard_map(
        functools.partial(per_device, dp_size=mesh.shape["dp"], fsdp_size=mesh.shape["fsdp"]),
        mesh=mesh,
        in_specs=(rows,) * 4 + weights + (P(None, "dp", None), P(None, "dp", None, None), P(None, "dp", None, None)),
        out_specs=(rows,) * 4 + weights,
        check_vma=False,
    )
```

```python
import functools
import math

import jax
import jax.numpy as jnp
from jax import lax
from jax.experimental import pallas as pl
from jax.experimental.pallas import tpu as pltpu
from jax.sharding import PartitionSpec as P

H = 8
DH = 128
CH = 64
SEG = 128
TRUNK = 4
BRANCHES = 2
NBUCK = 32
SELF_SCORE = -10000.0
NEG_SCORE = -1e30
EPSILON = 1e-06
BF = jnp.bfloat16
F32 = jnp.float32
AXES = ("dp", "fsdp")
GELU_A = math.sqrt(2.0 / math.pi)
GELU_B = 0.044715


def norm_stats(values):
    center = values - jnp.mean(values, axis=-1, keepdims=True)
    factor = lax.rsqrt(jnp.mean(center * center, axis=-1, keepdims=True) + EPSILON)
    return center * factor, factor


def norm_back(unit, factor, gain_vec, grad):
    scaled = grad * gain_vec
    inner = jnp.mean(scaled * unit, axis=-1, keepdims=True)
    return factor * (scaled - jnp.mean(scaled, axis=-1, keepdims=True) - unit * inner)


def position_codes(bucket_rows):
    rounds, tree_len = bucket_rows.shape
    buckets_t = bucket_rows.T
    lanes = jnp.arange(rounds * NBUCK, dtype=jnp.int32)
    member = (jnp.repeat(buckets_t, NBUCK, axis=1) == (lanes % NBUCK)[None, :]).astype(F32)
    rows = jnp.arange(tree_len, dtype=jnp.int32)
    lower = (rows[:, None] >= rows[None, :]).astype(BF)
    ranks = jnp.dot(lower, member.astype(BF), preferred_element_type=F32)
    totals = ranks[-1]
    before = ((lanes[:, None] // NBUCK == lanes[None, :] // NBUCK) & (lanes[:, None] < lanes[None, :])).astype(F32)
    offsets = jnp.sum(totals[:, None] * before, axis=0)
    places = jnp.sum((member * (ranks - 1.0 + offsets[None, :])).reshape(tree_len, rounds, NBUCK), axis=-1)
    return buckets_t.astype(F32) * tree_len + jnp.floor((places + 0.5) / CH)


def seg_parts(seg, info_ref):
    parts = []
    prefix = min(seg, TRUNK) * SEG
    if prefix:
        parts.append((0, prefix, 0, False))
    if seg >= TRUNK + BRANCHES:
        start = pl.multiple_of(info_ref[seg] * SEG, SEG)
        parts.append((start, SEG, TRUNK * SEG, False))
    parts.append((seg * SEG, SEG, (TRUNK + 1) * SEG, True))
    return parts


def unit_rows(rows_f32):
    factor = lax.rsqrt(jnp.mean(rows_f32 * rows_f32, axis=-1, keepdims=True) + EPSILON)
    return rows_f32 * factor * (1.0 / math.sqrt(DH)), factor


def own_diagonal():
    row = lax.broadcasted_iota(jnp.int32, (SEG, SEG), 0)
    col = lax.broadcasted_iota(jnp.int32, (SEG, SEG), 1)
    return row == col


def attention_forward_kernel(segments, rounds, info_ref, q_ref, v_ref, cq_ref, ck_ref, out_ref, total_ref, count_ref, unit_ref):
    head = pl.program_id(0)

    @pl.when(head == 0)
    def _():
        row = lax.broadcasted_iota(jnp.int32, (SEG, SEG), 0)
        col = lax.broadcasted_iota(jnp.int32, (SEG, SEG), 1)
        total_ref[...] = jnp.zeros_like(total_ref)
        for seg in range(segments):
            query = cq_ref[seg * SEG:(seg + 1) * SEG, :]
            for start, size, column, own in seg_parts(seg, info_ref):
                for piece in range(size // SEG):
                    first = start + piece * SEG
                    key = ck_ref[:, pl.ds(first, SEG)]
                    counted = jnp.zeros((SEG, SEG), F32)
                    for turn in range(rounds):
                        gap = query[:, turn:turn + 1] - key[turn:turn + 1, :]
                        counted = counted + jnp.where(jnp.abs(gap - 0.5) < 0.75, 1.0, 0.0)
                    if own:
                        counted = jnp.where(row >= col, counted, 0.0)
                    elif column == 0 and seg >= TRUNK:
                        counted = counted * jnp.where(info_ref[segments + seg] >= piece, 1.0, 0.0)
                    begin = column + piece * SEG
                    count_ref[seg * SEG:(seg + 1) * SEG, begin:begin + SEG] = counted.astype(BF)

    unit_ref[...] = unit_rows(q_ref[...].astype(F32))[0].astype(BF)
    diagonal = own_diagonal()
    lane = lax.broadcasted_iota(jnp.int32, (SEG, 128), 1)
    for seg in range(segments):
        rows = slice(seg * SEG, (seg + 1) * SEG)
        query = q_ref[rows, :]
        scored = []
        top = None
        for start, size, column, own in seg_parts(seg, info_ref):
            keys = pl.ds(start, size)
            scores = lax.dot_general(query, unit_ref[keys, :], (((1,), (1,)), ((), ())), preferred_element_type=F32)
            counted = count_ref[rows, column:column + size].astype(F32)
            if own:
                scores = jnp.where(diagonal, SELF_SCORE, scores)
            scores = jnp.where(counted > 0.0, scores, NEG_SCORE)
            best = jnp.max(scores, axis=-1, keepdims=True)
            top = best if top is None else jnp.maximum(top, best)
            scored.append((keys, scores, counted))
        amount = jnp.zeros((SEG, 1), F32)
        result = jnp.zeros((SEG, DH), F32)
        for keys, scores, counted in scored:
            weight = counted * jnp.exp(scores - top)
            amount = amount + jnp.sum(weight, axis=-1, keepdims=True)
            result = result + jnp.dot(weight.astype(BF), v_ref[keys, :], preferred_element_type=F32)
        out_ref[rows, :] = (result / amount).astype(BF)
        total = top + jnp.log(amount)
        total_ref[rows, :] = jnp.where(lane == head, total, total_ref[rows, :])


def attention_backward_kernel(segments, info_ref, q_ref, v_ref, out_ref, grad_ref, total_ref, count_ref, dq_ref, dv_ref, unit_ref, chance_ref, slope_ref, key_acc, value_acc, query_acc):
    head = pl.program_id(0)
    trunk = TRUNK * SEG
    whole = q_ref[...].astype(F32)
    unit, factor = unit_rows(whole)
    unit_ref[...] = unit.astype(BF)

    @pl.when(head == 0)
    def _():
        chance_ref[0:trunk, 0:trunk] = jnp.zeros((trunk, trunk), BF)
        slope_ref[0:trunk, 0:trunk] = jnp.zeros((trunk, trunk), BF)

    diagonal = own_diagonal()
    lane = lax.broadcasted_iota(jnp.int32, (SEG, 128), 1)
    for seg in range(segments):
        rows = slice(seg * SEG, (seg + 1) * SEG)
        query = q_ref[rows, :]
        grad = grad_ref[rows, :]
        total = jnp.sum(jnp.where(lane == head, total_ref[rows, :], 0.0), axis=-1, keepdims=True)
        delta = jnp.sum(grad.astype(F32) * out_ref[rows, :].astype(F32), axis=-1, keepdims=True)
        query_grad = jnp.zeros((SEG, DH), F32)
        for start, size, column, own in seg_parts(seg, info_ref):
            keys = pl.ds(start, size)
            scores = lax.dot_general(query, unit_ref[keys, :], (((1,), (1,)), ((), ())), preferred_element_type=F32)
            counted = count_ref[rows, column:column + size].astype(F32)
            if own:
                scores = jnp.where(diagonal, SELF_SCORE, scores)
            scores = jnp.where(counted > 0.0, scores, NEG_SCORE)
            chance = counted * jnp.exp(scores - total)
            reach = lax.dot_general(grad, v_ref[keys, :], (((1,), (1,)), ((), ())), preferred_element_type=F32)
            slope = chance * (reach - delta)
            if own:
                slope = jnp.where(diagonal, 0.0, slope)
            slope = slope.astype(BF)
            chance_ref[rows, column:column + size] = chance.astype(BF)
            slope_ref[rows, column:column + size] = slope
            query_grad = query_grad + jnp.dot(slope, unit_ref[keys, :], preferred_element_type=F32)
        query_acc[rows, :] = query_grad

    for weight_ref, side_ref, acc in ((chance_ref, grad_ref, value_acc), (slope_ref, q_ref, key_acc)):
        acc[0:trunk, :] = lax.dot_general(weight_ref[:, 0:trunk], side_ref[...], (((0,), (0,)), ((), ())), preferred_element_type=F32)
        for seg in range(segments):
            rows = slice(seg * SEG, (seg + 1) * SEG)
            leaf = seg >= TRUNK + BRANCHES
            begin = trunk if leaf else trunk + SEG
            added = lax.dot_general(weight_ref[rows, begin:trunk + 2 * SEG], side_ref[rows, :], (((0,), (0,)), ((), ())), preferred_element_type=F32)
            if leaf:
                above = pl.ds(pl.multiple_of(info_ref[seg] * SEG, SEG), SEG)
                acc[above, :] += added[0:SEG]
                added = added[SEG:]
            acc[rows, :] = added if seg >= TRUNK else acc[rows, :] + added

    key_grad = key_acc[...]
    along = jnp.mean(key_grad * whole, axis=-1, keepdims=True) * (factor * factor)
    dq_ref[...] = (query_acc[...] + (factor * (1.0 / math.sqrt(DH))) * (key_grad - whole * along)).astype(BF)
    dv_ref[...] = value_acc[...].astype(BF)


def attention_calls(tree_len, local_heads, rounds, segments):
    head_spec = pl.BlockSpec((tree_len, DH), lambda h, info: (0, h))
    side = pl.BlockSpec((tree_len, 128), lambda h, info: (0, 0))
    count_spec = pl.BlockSpec((tree_len, (TRUNK + 2) * SEG), lambda h, info: (0, 0))
    wide = local_heads * DH
    forward = pl.pallas_call(
        functools.partial(attention_forward_kernel, segments, rounds),
        grid_spec=pltpu.PrefetchScalarGridSpec(
            num_scalar_prefetch=1,
            grid=(local_heads,),
            in_specs=[head_spec, head_spec, side, pl.BlockSpec((8, tree_len), lambda h, info: (0, 0))],
            out_specs=[head_spec, side, count_spec],
            scratch_shapes=[pltpu.VMEM((tree_len, DH), BF)],
        ),
        out_shape=[
            jax.ShapeDtypeStruct((tree_len, wide), BF),
            jax.ShapeDtypeStruct((tree_len, 128), F32),
            jax.ShapeDtypeStruct((tree_len, (TRUNK + 2) * SEG), BF),
        ],
        compiler_params=pltpu.CompilerParams(vmem_limit_bytes=40 << 20),
        cost_estimate=cost(18),
        name="attention_forward",
    )
    backward = pl.pallas_call(
        functools.partial(attention_backward_kernel, segments),
        grid_spec=pltpu.PrefetchScalarGridSpec(
            num_scalar_prefetch=1,
            grid=(local_heads,),
            in_specs=[head_spec, head_spec, head_spec, head_spec, side, count_spec],
            out_specs=[head_spec, head_spec],
            scratch_shapes=[pltpu.VMEM((tree_len, DH), BF)]
            + [pltpu.VMEM((tree_len, (TRUNK + 2) * SEG), BF)] * 2
            + [pltpu.VMEM((tree_len, DH), F32)] * 3,
        ),
        out_shape=[jax.ShapeDtypeStruct((tree_len, wide), BF)] * 2,
        compiler_params=pltpu.CompilerParams(vmem_limit_bytes=40 << 20),
        cost_estimate=cost(21),
        name="attention_backward",
    )
    return forward, backward


def row_block(where_fn, coords_ref, span):
    return pl.ds(pl.multiple_of(where_fn(coords_ref) * span, span), span)


def piece_view(refs, piece):
    view = refs[piece[0]].at[piece[1]] if piece[1] else refs[piece[0]]
    if piece[2] is None:
        return view
    return view.at[pl.ds(piece[2][0], piece[3]), pl.ds(piece[2][1], piece[5][1])]


def whole_view(whole, coords_ref, piece):
    rows = row_block(piece[4], coords_ref, piece[3])
    first = piece[5][0]
    if callable(first):
        first = pl.multiple_of(first(coords_ref) * piece[5][1], piece[5][1])
    return whole.at[rows, pl.ds(first, piece[5][1])]


def load_pieces(coords_ref, refs, pieces, target, sems, first):
    return [
        pltpu.make_async_copy(piece_view(refs, piece), whole_view(target, coords_ref, piece), sems.at[first + number])
        for number, piece in enumerate(pieces)
    ]


def store_pieces(coords_ref, source, refs, pieces, sems, first):
    return [
        pltpu.make_async_copy(whole_view(source, coords_ref, piece), piece_view(refs, piece), sems.at[first + number])
        for number, piece in enumerate(pieces)
    ]


def project_kernel(q_pieces, v_pieces, q_count, v_count, coords_ref, mixed_ref, *refs):
    q_refs, v_refs = refs[:q_count], refs[q_count:q_count + v_count]
    q_out, v_out, q_weight, v_weight, sems = refs[q_count + v_count:]
    to_q = load_pieces(coords_ref, q_refs, q_pieces, q_weight, sems, 0)
    to_v = load_pieces(coords_ref, v_refs, v_pieces, v_weight, sems, len(q_pieces))
    for copy in to_q + to_v:
        copy.start()
    for copy in to_q:
        copy.wait()
    q_out[...] = jnp.dot(mixed_ref[...], q_weight[...], preferred_element_type=F32).astype(BF)
    for copy in to_v:
        copy.wait()
    v_out[...] = jnp.dot(mixed_ref[...], v_weight[...], preferred_element_type=F32).astype(BF)


VM = pl.BlockSpec(memory_space=pltpu.VMEM)
ANYWHERE = pl.BlockSpec(memory_space=pl.ANY)


def cost(micros):
    return pl.CostEstimate(flops=int(micros * 1e9), transcendentals=0, bytes_accessed=0)


def kernel_call(body, ins, outs, scratch, name, limit, micros, grid=()):
    return pl.pallas_call(
        body,
        grid_spec=pltpu.PrefetchScalarGridSpec(num_scalar_prefetch=1, grid=grid, in_specs=ins, out_specs=outs[0], scratch_shapes=scratch),
        out_shape=outs[1],
        compiler_params=pltpu.CompilerParams(vmem_limit_bytes=limit << 20),
        cost_estimate=cost(micros),
        name=name,
    )


def project(coords, mixed_tree, q_side, v_side, wide):
    q_arrays, q_pieces = q_side
    v_arrays, v_pieces = v_side
    rows, features = mixed_tree.shape
    body = functools.partial(project_kernel, q_pieces, v_pieces, len(q_arrays), len(v_arrays))
    return kernel_call(
        body,
        [VM] + [ANYWHERE] * (len(q_arrays) + len(v_arrays)),
        ([VM, VM], [jax.ShapeDtypeStruct((rows, wide), BF)] * 2),
        [pltpu.VMEM((features, wide), BF)] * 2 + [pltpu.SemaphoreType.DMA((len(q_pieces) + len(v_pieces),))],
        "project",
        40,
        7,
    )(coords, mixed_tree, *q_arrays, *v_arrays)


def project_back_kernel(q_pieces, v_pieces, q_count, v_count, q_outs, v_outs, q_made, v_made, coords_ref, mixed_ref, unit_ref, dq_ref, dv_ref, *refs):
    q_refs, v_refs = refs[:q_count], refs[q_count:q_count + v_count]
    rest = refs[q_count + v_count:]
    partial_ref, gain_sum, shift_sum = rest[:3]
    rest = rest[3:]
    q_grads, v_grads = rest[:q_made], rest[q_made:q_made + v_made]
    q_weight, v_weight, q_sum, v_sum, sems = rest[q_made + v_made:]
    to_q = load_pieces(coords_ref, q_refs, q_pieces, q_weight, sems, 0)
    to_v = load_pieces(coords_ref, v_refs, v_pieces, v_weight, sems, len(q_pieces))
    for copy in to_q + to_v:
        copy.start()
    used = len(q_pieces) + len(v_pieces)
    turned = (((0,), (0,)), ((), ()))
    crossed = (((1,), (1,)), ((), ()))
    q_sum[...] = lax.dot_general(mixed_ref[...], dq_ref[...], turned, preferred_element_type=F32).astype(BF)
    from_q = store_pieces(coords_ref, q_sum, q_grads, q_outs, sems, used)
    for copy in from_q:
        copy.start()
    v_sum[...] = lax.dot_general(mixed_ref[...], dv_ref[...], turned, preferred_element_type=F32).astype(BF)
    from_v = store_pieces(coords_ref, v_sum, v_grads, v_outs, sems, used + len(q_outs))
    for copy in from_v:
        copy.start()
    for copy in to_q + to_v:
        copy.wait()
    partial = lax.dot_general(dq_ref[...], q_weight[...], crossed, preferred_element_type=F32) + lax.dot_general(
        dv_ref[...], v_weight[...], crossed, preferred_element_type=F32
    )
    partial_ref[...] = partial.astype(BF)
    gain_sum[...] = jnp.sum(partial * unit_ref[...].astype(F32), axis=0, keepdims=True)
    shift_sum[...] = jnp.sum(partial, axis=0, keepdims=True)
    for copy in from_q + from_v:
        copy.wait()


def project_back(coords, mixed_tree, unit_tree, dq, dv, q_side, v_side, q_form, v_form):
    q_arrays, q_pieces = q_side
    v_arrays, v_pieces = v_side
    q_shapes, q_outs = q_form
    v_shapes, v_outs = v_form
    rows, features = mixed_tree.shape
    wide = dq.shape[1]
    body = functools.partial(
        project_back_kernel, q_pieces, v_pieces, len(q_arrays), len(v_arrays), q_outs, v_outs, len(q_shapes), len(v_shapes)
    )
    made = kernel_call(
        body,
        [VM] * 4 + [ANYWHERE] * (len(q_arrays) + len(v_arrays)),
        (
            [VM] * 3 + [ANYWHERE] * (len(q_shapes) + len(v_shapes)),
            [jax.ShapeDtypeStruct((rows, features), BF)]
            + [jax.ShapeDtypeStruct((1, features), F32)] * 2
            + [jax.ShapeDtypeStruct(s, BF) for s in q_shapes + v_shapes],
        ),
        [pltpu.VMEM((features, wide), BF)] * 4
        + [pltpu.SemaphoreType.DMA((len(q_pieces) + len(v_pieces) + len(q_outs) + len(v_outs),))],
        "project_back",
        50,
        18,
    )(coords, mixed_tree, unit_tree, dq, dv, *q_arrays, *v_arrays)
    return made[:3], made[3:3 + len(q_shapes)], made[3 + len(q_shapes):]


def normalised(values):
    center = values - jnp.mean(values, axis=-1, keepdims=True)
    factor = lax.rsqrt(jnp.mean(center * center, axis=-1, keepdims=True) + EPSILON)
    return center * factor, factor


def out_kernel(pieces, count, coords_ref, att_ref, first_ref, gain_ref, shift_ref, *refs):
    o_refs = refs[:count]
    first_out, feed_out, weight, sems = refs[count:]
    copies = load_pieces(coords_ref, o_refs, pieces, weight, sems, 0)
    for copy in copies:
        copy.start()
    for copy in copies:
        copy.wait()
    made = first_ref[...] + jnp.dot(att_ref[...], weight[...], preferred_element_type=F32)
    first_out[...] = made
    feed_out[...] = (normalised(made)[0] * gain_ref[...] + shift_ref[...]).astype(BF)


def out_project(coords, att, first, gain, shift, side):
    arrays, pieces = side
    rows, features = first.shape
    return kernel_call(
        functools.partial(out_kernel, pieces, len(arrays)),
        [VM] * 4 + [ANYWHERE] * len(arrays),
        ([VM, VM], [jax.ShapeDtypeStruct((rows, features), F32), jax.ShapeDtypeStruct((rows, features), BF)]),
        [pltpu.VMEM((features, features), BF), pltpu.SemaphoreType.DMA((len(pieces),))],
        "out_project",
        50,
        8,
    )(coords, att, first, gain, shift, *arrays)


def out_back_kernel(pieces, count, outs, made, coords_ref, back_ref, first_ref, grad_ref, att_ref, gain_ref, *refs):
    o_refs = refs[:count]
    rest = refs[count:]
    grad_in, grad_att, gain_sum, shift_sum = rest[:4]
    grads = rest[4:4 + made]
    weight, total, sems = rest[4 + made:]
    copies = load_pieces(coords_ref, o_refs, pieces, weight, sems, 0)
    for copy in copies:
        copy.start()
    back = back_ref[...]
    unit, factor = normalised(first_ref[...])
    gain_sum[...] = jnp.sum(back * unit, axis=0, keepdims=True)
    shift_sum[...] = jnp.sum(back, axis=0, keepdims=True)
    scaled = back * gain_ref[...]
    inner = jnp.mean(scaled * unit, axis=-1, keepdims=True)
    value = grad_ref[...] + factor * (scaled - jnp.mean(scaled, axis=-1, keepdims=True) - unit * inner)
    grad_in[...] = value
    low = value.astype(BF)
    total[...] = lax.dot_general(att_ref[...], low, (((0,), (0,)), ((), ())), preferred_element_type=F32).astype(BF)
    stores = store_pieces(coords_ref, total, grads, outs, sems, len(pieces))
    for copy in stores:
        copy.start()
    for copy in copies:
        copy.wait()
    grad_att[...] = lax.dot_general(low, weight[...], (((1,), (1,)), ((), ())), preferred_element_type=F32).astype(BF)
    for copy in stores:
        copy.wait()


def out_back(coords, back, first_out, grad, att, gain, side, form):
    arrays, pieces = side
    shapes, outs = form
    rows, features = back.shape
    full = jax.ShapeDtypeStruct((rows, features), F32)
    line = jax.ShapeDtypeStruct((1, features), F32)
    made = kernel_call(
        functools.partial(out_back_kernel, pieces, len(arrays), outs, len(shapes)),
        [VM] * 5 + [ANYWHERE] * len(arrays),
        (
            [VM] * 4 + [ANYWHERE] * len(shapes),
            [full, jax.ShapeDtypeStruct((rows, features), BF), line, line] + [jax.ShapeDtypeStruct(s, BF) for s in shapes],
        ),
        [pltpu.VMEM((features, features), BF)] * 2 + [pltpu.SemaphoreType.DMA((len(pieces) + len(outs),))],
        "out_back",
        60,
        12,
    )(coords, back, first_out, grad, att, gain, *arrays)
    return made[:4], made[4:]


def feed_in_kernel(plan, counts, coords_ref, feed_ref, grad_ref, bias_ref, *refs):
    pieces, step_outs, block_of = plan
    i_count, made = counts
    i_refs = refs[:i_count]
    active_ref, slope_ref = refs[i_count:i_count + 2]
    grads = refs[i_count + 2:i_count + 2 + made]
    weight, outer_sum, in_sems, out_sems = refs[i_count + 2 + made:]
    step = pl.program_id(0)
    slot = lax.rem(step, 2)
    tile = outer_sum.shape[1]
    count = len(step_outs)

    def store(number):
        return store_pieces(coords_ref, outer_sum.at[number % 2], grads, step_outs[number], out_sems.at[number % 2], 0)

    @pl.when(step == 0)
    def _():
        copies = load_pieces(coords_ref, i_refs, pieces, weight, in_sems, 0)
        for copy in copies:
            copy.start()
        for copy in copies:
            copy.wait()

    for number in range(2, count):

        @pl.when(step == number)
        def _(number=number):
            for copy in store(number - 2):
                copy.wait()

    columns = pl.ds(pl.multiple_of(block_of(step, coords_ref) * tile, tile), tile)
    value = jnp.dot(feed_ref[...], weight[:, columns], preferred_element_type=F32) + bias_ref[:, columns]
    square = value * value
    bend = jnp.tanh(GELU_A * (value + GELU_B * (square * value)))
    half = 0.5 * (1.0 + bend)
    active = (value * half).astype(BF)
    active_ref[...] = active
    slope_ref[...] = (half + 0.5 * value * (1.0 - bend * bend) * (GELU_A * (1.0 + 3.0 * GELU_B * square))).astype(BF)
    outer_sum[slot] = lax.dot_general(active, grad_ref[...], (((0,), (0,)), ((), ())), preferred_element_type=F32).astype(BF)

    for number in range(count):

        @pl.when(step == number)
        def _(number=number):
            for copy in store(number):
                copy.start()
            if number == count - 1:
                for last in range(max(0, number - 1), count):
                    for copy in store(last):
                        copy.wait()


def feed_in(coords, feed, grad, bias, side, form, block_of):
    arrays, pieces = side
    shapes, step_outs = form
    rows, features = feed.shape
    hidden = bias.shape[1]
    tile = hidden // len(step_outs)
    most = max(len(outs) for outs in step_outs)
    block = pl.BlockSpec((rows, tile), lambda j, co: (0, block_of(j, co)))
    made = kernel_call(
        functools.partial(feed_in_kernel, (pieces, step_outs, block_of), (len(arrays), len(shapes))),
        [VM] * 3 + [ANYWHERE] * len(arrays),
        (
            [block, block] + [ANYWHERE] * len(shapes),
            [jax.ShapeDtypeStruct((rows, hidden), BF)] * 2 + [jax.ShapeDtypeStruct(s, BF) for s in shapes],
        ),
        [
            pltpu.VMEM((features, hidden), BF),
            pltpu.VMEM((2, tile, features), BF),
            pltpu.SemaphoreType.DMA((len(pieces),)),
            pltpu.SemaphoreType.DMA((2, most)),
        ],
        "feed_in",
        60,
        29,
        grid=(len(step_outs),),
    )(coords, feed, grad, bias, *arrays)
    return made[0], made[1], made[2:]


def feed_out_kernel(plan, counts, coords_ref, feed_ref, grad_ref, base_ref, bias_ref, active_ref, slope_ref, *refs):
    i_pieces, i_outs, steps, block_of = plan
    i_count, u_count, made = counts
    i_refs, u_refs = refs[:i_count], refs[i_count:i_count + u_count]
    rest = refs[i_count + u_count:]
    out_ref, back_ref, bias_sum = rest[:3]
    grads = rest[3:3 + made]
    weight, weight_sum, outer, i_sems, u_sems, out_sems = rest[3 + made:]
    step = pl.program_id(0)
    slot = lax.rem(step, 2)
    tile = outer.shape[1]
    count = len(steps)

    def u_load(number):
        return load_pieces(coords_ref, u_refs, steps[number], outer.at[number % 2], u_sems.at[number % 2], 0)

    @pl.when(step == 0)
    def _():
        copies = load_pieces(coords_ref, i_refs, i_pieces, weight, i_sems, 0)
        for copy in u_load(0) + copies:
            copy.start()
        out_ref[...] = base_ref[...] + bias_ref[...]
        back_ref[...] = jnp.zeros_like(back_ref)
        for copy in copies:
            copy.wait()

    for number in range(count):

        @pl.when(step == number)
        def _(number=number):
            if number + 1 < count:
                for copy in u_load(number + 1):
                    copy.start()
            for copy in u_load(number):
                copy.wait()

    columns = pl.ds(pl.multiple_of(block_of(step, coords_ref) * tile, tile), tile)
    grad = grad_ref[...]
    out_ref[...] += jnp.dot(active_ref[...], outer[slot], preferred_element_type=F32)
    pulled = lax.dot_general(grad, outer[slot], (((1,), (1,)), ((), ())), preferred_element_type=F32)
    inner_low = (pulled * slope_ref[...].astype(F32)).astype(BF)
    bias_sum[:, columns] = jnp.sum(inner_low.astype(F32), axis=0, keepdims=True)
    weight_sum[:, columns] = lax.dot_general(feed_ref[...], inner_low, (((0,), (0,)), ((), ())), preferred_element_type=F32).astype(BF)
    back_ref[...] += lax.dot_general(inner_low, weight[:, columns], (((1,), (1,)), ((), ())), preferred_element_type=F32)

    @pl.when(step == count - 1)
    def _():
        copies = store_pieces(coords_ref, weight_sum, grads, i_outs, out_sems, 0)
        for copy in copies:
            copy.start()
        for copy in copies:
            copy.wait()


def feed_out(coords, feed, grad, base, bias, active, slope, i_side, u_side, i_form, block_of):
    i_arrays, i_pieces = i_side
    u_arrays, steps = u_side
    shapes, i_outs = i_form
    rows, features = feed.shape
    hidden = active.shape[1]
    tile = hidden // len(steps)
    most = max(len(pieces) for pieces in steps)
    block = pl.BlockSpec((rows, tile), lambda j, co: (0, block_of(j, co)))
    made = kernel_call(
        functools.partial(feed_out_kernel, (i_pieces, i_outs, steps, block_of), (len(i_arrays), len(u_arrays), len(shapes))),
        [VM] * 4 + [block, block] + [ANYWHERE] * (len(i_arrays) + len(u_arrays)),
        (
            [VM] * 3 + [ANYWHERE] * len(shapes),
            [jax.ShapeDtypeStruct((rows, features), F32)] * 2
            + [jax.ShapeDtypeStruct((1, hidden), F32)]
            + [jax.ShapeDtypeStruct(s, BF) for s in shapes],
        ),
        [
            pltpu.VMEM((features, hidden), BF),
            pltpu.VMEM((features, hidden), BF),
            pltpu.VMEM((2, tile, features), BF),
            pltpu.SemaphoreType.DMA((len(i_pieces),)),
            pltpu.SemaphoreType.DMA((2, most)),
            pltpu.SemaphoreType.DMA((len(i_outs),)),
        ],
        "feed_out",
        60,
        40,
        grid=(len(steps),),
    )(coords, feed, grad, base, bias, active, slope, *i_arrays, *u_arrays)
    return made[0], made[1], made[2], made[3:]


def pick(flag, when_true, when_false):
    return jnp.where(flag, when_true, when_false)


def after(value, *earlier):
    return lax.optimization_barrier((value,) + earlier)[0]


class PairPlan:
    def __init__(self):
        me = lax.axis_index("fsdp")
        self.upper = me // 2 == 1
        self.odd = me % 2 == 1
        self.tree = me // 2
        self.head_group = me % 2
        self.far_made = []

    def near(self, value):
        return lax.ppermute(value, "fsdp", [(i, i ^ 1) for i in range(4)])

    def far(self, value):
        made = lax.ppermute(value, "fsdp", [(i, i ^ 2) for i in range(4)])
        self.far_made = [made]
        return made

    def rows_to_tree(self, rows):
        mine = pick(self.upper, rows[1], rows[0])
        got = self.far(pick(self.upper, rows[0], rows[1]))
        pair = jnp.stack([pick(self.upper, got, mine), pick(self.upper, mine, got)])
        other = self.near(pair)
        whole = jnp.stack([pick(self.odd, other, pair), pick(self.odd, pair, other)], axis=1)
        return whole.reshape((-1, rows.shape[2]))

    def heads_to_rows(self, heads):
        blocks = heads.reshape(2, 2, -1, heads.shape[1])
        keep = pick(self.odd, blocks[:, 1], blocks[:, 0])
        got = self.near(pick(self.odd, blocks[:, 0], blocks[:, 1]))
        full = jnp.concatenate([pick(self.odd, got, keep), pick(self.odd, keep, got)], axis=-1)
        return self.swap_trees(full)

    def swap_trees(self, full):
        mine = pick(self.upper, full[1], full[0])
        got = self.far(pick(self.upper, full[0], full[1]))
        return jnp.stack([pick(self.upper, got, mine), pick(self.upper, mine, got)])

    def rows_to_heads(self, rows):
        wide = rows.shape[2] // 2
        mine = pick(self.upper, rows[1], rows[0])
        got = self.far(pick(self.upper, rows[0], rows[1]))
        pair = jnp.stack([pick(self.upper, got, mine), pick(self.upper, mine, got)])
        keep = pick(self.odd, pair[..., wide:], pair[..., :wide])
        other = self.near(pick(self.odd, pair[..., :wide], pair[..., wide:]))
        whole = jnp.stack([pick(self.odd, other, keep), pick(self.odd, keep, other)], axis=1)
        return whole.reshape((-1, wide))

    def partial_to_rows(self, partial, *earlier):
        blocks = partial.reshape(2, 2, -1, partial.shape[1])
        keep = pick(self.odd, blocks[:, 1], blocks[:, 0])
        got = self.near(pick(self.odd, blocks[:, 0], blocks[:, 1]).astype(BF))
        return self.swap_trees(after((keep.astype(F32) + got.astype(F32)).astype(BF), *earlier)).astype(F32)


class GroupPlan:
    def __init__(self, size, trees):
        me = lax.axis_index("fsdp")
        self.size = size
        self.trees = trees
        self.group = size // trees
        self.tree = me // self.group
        self.head_group = me % self.group
        self.me = me
        self.far_made = []

    def rows_to_tree(self, rows):
        every = lax.all_gather(rows, "fsdp", axis=1, tiled=True)
        return lax.dynamic_index_in_dim(every, self.tree, 0, False)

    def heads_to_rows(self, heads):
        count = heads.shape[0] // self.size
        every = lax.all_gather(heads, "fsdp", axis=0, tiled=False)
        mine = lax.dynamic_slice_in_dim(every, self.me * count, count, 1)
        mine = mine.reshape(self.trees, self.group, count, heads.shape[1])
        return jnp.moveaxis(mine, 1, 2).reshape(self.trees, count, -1)

    def rows_to_heads(self, rows):
        wide = rows.shape[2] // self.group
        whole = self.rows_to_tree(rows)
        return lax.dynamic_slice_in_dim(whole, self.head_group * wide, wide, 1)

    def partial_to_rows(self, partial, *earlier):
        every = jnp.zeros((self.trees,) + partial.shape, F32)
        every = lax.dynamic_update_index_in_dim(every, partial.astype(F32), self.tree, 0)
        return lax.psum_scatter(every, "fsdp", scatter_dimension=1, tiled=True)


def low(value):
    return value.astype(BF)


def wide_of(value):
    return value.astype(F32)


def swap_pairs(size, bit):
    return [(i, i ^ bit) for i in range(size)]


class LinkMoves:
    def __init__(self, plan):
        self.plan = plan
        dp, fsdp = lax.axis_index("dp"), lax.axis_index("fsdp")
        self.bits = [fsdp % 2, fsdp // 2, dp % 2, dp // 2 % 2, dp // 4]
        self.coords = jnp.stack([dp // 2, dp % 2, fsdp // 2, fsdp % 2]).astype(jnp.int32)
        self.odd = fsdp % 2 == 1

    def core(self, value):
        return lax.ppermute(value, "fsdp", swap_pairs(4, 1))

    def over_y(self, value):
        return lax.ppermute(value, "fsdp", swap_pairs(4, 2))

    def over_x(self, value):
        return lax.ppermute(value, "dp", swap_pairs(8, 1))

    def up_z(self, value):
        return lax.ppermute(value, "dp", [(i, (i + 2) % 8) for i in range(8)])

    def bit_move(self, bit, value):
        if bit < 2:
            return lax.ppermute(value, "fsdp", swap_pairs(4, 1 << bit))
        return lax.ppermute(value, "dp", swap_pairs(8, 1 << (bit - 2)))

    def ring(self, value):
        made = [value]
        for _ in range(3):
            made.append(self.up_z(made[-1]))
        return made

    def ring_sum(self, blocks):
        total = blocks[1]
        for k in (2, 3, 0):
            total = wide_of(self.up_z(low(total))) + blocks[k]
        return total

    def small_step(self, bit, made):
        got = self.bit_move(bit, made)
        one = self.bits[bit] == 1
        return pick(one, jnp.concatenate([got, made]), jnp.concatenate([made, got]))

    def scatter_small(self, total):
        made = after(total, *self.heads_first)
        for bit in (4, 3, 2, 1, 0):
            half = made.shape[0] // 2
            one = self.bits[bit] == 1
            keep = pick(one, made[half:], made[:half])
            made = keep + self.bit_move(bit, pick(one, made[:half], made[half:]))
        return made

    @staticmethod
    def place32(k, rx, ry, rc):
        return lambda co: ((((co[0] + 4 - k) & 3) * 2 + (co[1] ^ rx)) * 2 + (co[2] ^ ry)) * 2 + (co[3] ^ rc)

    @staticmethod
    def place16(k, rx, ry):
        return lambda co: (((co[0] + 4 - k) & 3) * 2 + (co[1] ^ rx)) * 2 + (co[2] ^ ry)

    @staticmethod
    def place4(ry, rc):
        return lambda co: (co[2] ^ ry) * 2 + (co[3] ^ rc)

    @staticmethod
    def block_of(step, co):
        return ((co[0] + 4 - (step >> 1)) & 3) * 2 + (co[1] ^ (step & 1))

    def heads_pieces(self, which, rows, half):
        pieces = []
        for outer in range(2):
            for inner in range(2):
                for k in range(4):
                    rx, ry = (outer, inner) if which == 0 else (inner, outer)
                    pieces.append((outer, (inner, k), None, rows, self.place16(k, rx, ry), (0, half)))
        return pieces

    def gather_first(self, small, query, value, output, rows_of):
        count, features = query.shape
        half = features // 2
        both = jnp.stack([query, value, output])
        keep = pick(self.odd, both[:, :, half:], both[:, :, :half])
        got = self.core(pick(self.odd, both[:, :, :half], both[:, :, half:]))
        chip = pick(self.odd, jnp.concatenate([got, keep], axis=1), jnp.concatenate([keep, got], axis=1))
        made = [chip, self.up_z(chip)]
        small = self.small_step(1, after(self.small_step(0, small), chip))
        self.small_early = [small]
        tree = rows_of(small)
        made.append(self.up_z(after(made[1], small)))
        small = self.small_step(2, after(small, made[1]))
        made.append(self.up_z(after(made[2], small, *self.plan.far_made)))
        small = self.small_step(4, after(self.small_step(3, small), made[2]))
        self.heads_ring = made[3]
        sides = []
        for which, first, second in ((0, self.over_y, self.over_x), (1, self.over_x, self.over_y)):
            near = jnp.stack([m[which] for m in made])
            near = jnp.stack([near, first(near)])
            sides.append(([near, second(after(near, *self.plan.far_made))], self.heads_pieces(which, 2 * count, half)))
        self.heads_last = [sides[0][0][1], sides[1][0][1]]
        self.output_near = jnp.stack([m[2] for m in made])
        self.output_got = self.over_y(after(self.output_near, *self.heads_last))
        self.output_pieces_in = self.output_parts(2 * count, half)
        return small, sides, tree

    def output_plane(self, made):
        near = jnp.stack([self.output_near, after(self.output_got, made)])
        arrays = [near, self.over_x(near)]
        self.output_last = [arrays[1]]
        arrays += [self.core(m) for m in arrays]
        return arrays, self.output_pieces_in

    def output_parts(self, rows, half):
        pieces = []
        for rc in range(2):
            for rx in range(2):
                for ry in range(2):
                    for k in range(4):
                        columns = ((lambda co, rc=rc: co[3] ^ rc), half)
                        pieces.append((rc * 2 + rx, (ry, k), None, rows, self.place16(k, rx, ry), columns))
        return pieces

    def heads_form(self, count, half):
        shapes = [(2, 4, 2 * count, half)] * 2
        return [(shapes, self.heads_pieces(which, 2 * count, half)) for which in range(2)]

    def sum_heads(self, query, value, *earlier):
        totals = []
        self.heads_first = []
        self.heads_sum = []
        for parts, first, second in ((query, self.over_x, self.over_y), (value, self.over_y, self.over_x)):
            got = first(after(parts[1], *earlier))
            self.heads_first.append(got)
            made = wide_of(parts[0]) + wide_of(got)
            got = second(low(made[1]))
            self.heads_sum.append(got)
            totals.append(made[0] + wide_of(got))
        self.heads_total = jnp.stack(totals, axis=1)

    def sum_heads_last(self, *earlier):
        made = self.heads_total
        total = made[1]
        for k in (2, 3, 0):
            if k == 0:
                total = after(total, *earlier)
            total = wide_of(self.up_z(low(total))) + made[k]
        both = total
        count = both.shape[1] // 2
        keep = pick(self.odd, both[:, count:], both[:, :count])
        got = wide_of(self.core(low(pick(self.odd, both[:, :count], both[:, count:]))))
        full = pick(self.odd, jnp.concatenate([got, keep], axis=2), jnp.concatenate([keep, got], axis=2))
        return full[0], full[1]


    def inner_cut(self, hidden):
        return hidden * 11 // 16

    def inner_pieces(self, count, hidden):
        cut = self.inner_cut(hidden)
        pieces = []
        for part in range(2):
            for rc in range(2):
                for outer in range(2):
                    for inner in range(2):
                        for k in range(4):
                            rx, ry = (outer, inner) if part == 0 else (inner, outer)
                            columns = (0, cut) if part == 0 else (cut, hidden - cut)
                            pieces.append((rc * 4 + part * 2 + outer, (inner, k), None, count, self.place32(k, rx, ry, rc), columns))
        return pieces

    def output_pieces(self, count, features):
        pieces = []
        for rc in range(2):
            for ry in range(2):
                for rx in range(2):
                    for k in range(4):
                        pieces.append((rc * 2 + ry, (rx, k), None, count, self.place32(k, rx, ry, rc), (0, features)))
        return pieces

    def gather_inner(self, inner):
        count, hidden = inner.shape
        cut = self.inner_cut(hidden)
        made = [after(inner, self.heads_ring)]
        made.append(self.up_z(made[0]))
        made.append(self.up_z(made[1]))
        made.append(self.up_z(after(made[2], *self.heads_last)))
        self.inner_ring = [made[3]]
        self.inner_made = made

    def inner_plane(self, made):
        blocks = self.inner_made[:3] + [after(self.inner_made[3], made)]
        self.inner_ring = blocks[3:]
        hidden = blocks[0].shape[1]
        cut = self.inner_cut(hidden)
        self.inner_near = []
        self.inner_first = []
        for part, first in ((0, self.over_y), (1, self.over_x)):
            near = jnp.stack([m[:, :cut] if part == 0 else m[:, cut:] for m in blocks])
            self.inner_first.append(first(near))
            self.inner_near.append(near)

    def inner_across(self, *earlier):
        near = [jnp.stack(pair) for pair in zip(self.inner_near, self.inner_first)]
        self.inner_arrays = [near[0], self.over_x(near[0]), near[1], self.over_y(after(near[1], *earlier))]

    def inner_finish(self, made):
        arrays = list(self.inner_arrays)
        arrays[1] = after(arrays[1], made)
        arrays[3] = after(arrays[3], made)
        count = arrays[0].shape[2]
        hidden = arrays[0].shape[3] + arrays[2].shape[3]
        return arrays + [self.core(m) for m in arrays], self.inner_pieces(count, hidden)

    def inner_form(self, count, hidden):
        cut = self.inner_cut(hidden)
        shapes = ([(2, 4, count, cut)] * 2 + [(2, 4, count, hidden - cut)] * 2) * 2
        return shapes, self.inner_pieces(count, hidden)

    def output_form(self, count, features):
        return [(2, 4, count, features)] * 4, self.output_pieces(count, features)

    def sum_inner_cores(self, inner):
        self.inner_cores = [self.core(part) for part in inner[4:]]
        return self.inner_cores

    def sum_inner(self, inner, output, *earlier):
        hidden = inner[0].shape[3] + inner[2].shape[3]
        first = [wide_of(inner[which]) + wide_of(self.inner_cores[which]) for which in range(2)]
        first_got = self.over_x(low(first[1]))
        first_keep = first[0] + wide_of(first_got)
        halves = []
        for which in (1, 0):
            both = [wide_of(inner[2 + which]) + wide_of(self.inner_cores[2 + which])]
            both.append(wide_of(output[which]) + wide_of(self.core(output[2 + which])))
            halves.append(both)
        second_got = self.over_y(after(jnp.concatenate([low(half) for half in halves[0]], axis=3), *earlier))
        second_keep = jnp.concatenate(halves[1], axis=3) + wide_of(second_got)
        self.inner_sum_first = [first_got, second_got]
        self.inner_sum_sent = [low(first_keep[1]), low(second_keep[1])]
        first_last = self.over_y(self.inner_sum_sent[0])
        second_last = self.over_x(self.inner_sum_sent[1])
        self.inner_sum_last = [first_last, second_last]
        made = jnp.concatenate([first_keep[0] + wide_of(first_last), second_keep[0] + wide_of(second_last)], axis=2)
        total = self.ring_sum([made[k] for k in range(4)])
        return total[:, :hidden], total[:, hidden:]


    def outer_steps(self, count, features):
        steps = []
        for k in range(4):
            for rx in range(2):
                steps.append(
                    [(rc * 4 + k, (rx, ry), None, count, self.place4(ry, rc), (0, features)) for ry in range(2) for rc in range(2)]
                )
        return steps

    def gather_outer(self, outer):
        near = jnp.stack([outer, self.over_x(outer)])
        self.outer_near = near
        self.outer_got_y = self.over_y(after(near, *self.heads_last))

    def outer_plane(self, made):
        plane = jnp.stack([self.outer_near, after(self.outer_got_y, made)], axis=1)
        self.outer_ring = [plane, self.up_z(after(plane, *self.inner_ring))]

    def outer_next(self, made):
        self.outer_ring[-1] = after(self.outer_ring[-1], made)
        self.outer_ring.append(self.up_z(self.outer_ring[-1]))

    def outer_finish(self):
        arrays = self.outer_ring + [self.core(m) for m in self.outer_ring]
        return arrays, self.outer_steps(*arrays[0].shape[2:])

    def outer_form(self, count, features):
        return [(2, 2, count, features)] * 8, self.outer_steps(count, features)

    def sum_outer_first(self, parts):
        self.shares = [None] * 4
        cores = []
        for k in (1, 2, 3, 0):
            cores.append(self.core(parts[4 + k]))
            self.shares[k] = wide_of(parts[k]) + wide_of(cores[-1])
        self.outer_got = self.up_z(low(self.shares[1]))
        return [self.outer_got] + cores

    def sum_outer_step(self, k, *earlier):
        if earlier:
            self.outer_got = after(self.outer_got, *earlier)
        total = low(wide_of(self.outer_got) + self.shares[k])
        self.outer_got = self.up_z(total)
        return [self.outer_got]

    def sum_outer_x(self, *earlier):
        total = wide_of(after(self.outer_got, *earlier)) + self.shares[0]
        got = self.over_x(low(total[1]))
        self.outer_total = total[0] + wide_of(got)
        return [got]

    def sum_outer_last(self, *earlier):
        return self.outer_total[0] + wide_of(self.over_y(after(low(self.outer_total[1]), *earlier)))


class PlainMoves:
    def __init__(self, plan, wide):
        self.plan = plan
        self.wide = wide
        self.coords = jnp.zeros((4,), jnp.int32)
        self.small_early = self.inner_ring = self.inner_first = self.inner_sum_first = self.inner_sum_last = self.heads_sum = []
        self.output_last = self.inner_sum_sent = []

    @staticmethod
    def start(co):
        return co[0] * 0

    def gather(self, shard):
        return lax.all_gather(shard, AXES, axis=0, tiled=True)

    def scatter(self, total):
        return lax.psum_scatter(total, AXES, scatter_dimension=0, tiled=True)

    def whole(self, rows, columns):
        return [(0, (), None, rows, self.start, (0, columns))]

    @staticmethod
    def block_of(step, co):
        return step

    def scatter_small(self, total):
        return self.scatter(total)

    def gather_first(self, small, query, value, output, rows_of):
        sides = []
        for shard in (query, value):
            cols = lax.dynamic_slice_in_dim(self.gather(shard), self.plan.head_group * self.wide, self.wide, 1)
            sides.append(([cols], self.whole(*cols.shape)))
        self.output_full = self.gather(output)
        small = self.gather(small)
        return small, sides, rows_of(small)

    def heads_form(self, count, half):
        features = H * DH
        return [([(features, self.wide)], self.whole(features, self.wide))] * 2

    def sum_heads(self, query, value, *earlier):
        self.heads_parts = (query[0], value[0])

    def sum_heads_last(self, *earlier):
        made = []
        for cols in self.heads_parts:
            full = jnp.zeros((cols.shape[0], H * DH), F32)
            made.append(self.scatter(lax.dynamic_update_slice_in_dim(full, wide_of(cols), self.plan.head_group * self.wide, 1)))
        return made

    def gather_inner(self, inner):
        self.inner_full = self.gather(inner)
        self.features, self.hidden = self.inner_full.shape

    def inner_plane(self, made):
        pass

    def inner_across(self, *earlier):
        pass

    def inner_finish(self, made):
        return [self.inner_full], self.whole(*self.inner_full.shape)

    def output_plane(self, made):
        return [self.output_full], self.whole(*self.output_full.shape)

    def inner_form(self, count, hidden):
        return [(self.features, hidden)], self.whole(self.features, hidden)

    def output_form(self, count, features):
        return [(H * DH, features)], self.whole(H * DH, features)

    def sum_inner_cores(self, inner):
        return []

    def sum_inner(self, inner, output, *earlier):
        return self.scatter(wide_of(inner[0])), self.scatter(wide_of(output[0]))

    def outer_steps(self, features):
        return [[(0, (s,), None, 512, self.start, (0, features))] for s in range(self.hidden // 512)]

    def gather_outer(self, outer):
        self.outer_full = self.gather(outer)

    def outer_plane(self, made):
        pass

    def outer_next(self, made):
        pass

    def outer_finish(self):
        features = self.outer_full.shape[1]
        return [self.outer_full.reshape(-1, 512, features)], self.outer_steps(features)

    def outer_form(self, count, features):
        return [(self.hidden // 512, 512, features)], self.outer_steps(features)

    def sum_outer_first(self, parts):
        self.outer_total = wide_of(parts[0]).reshape(self.hidden, -1)
        return []

    def sum_outer_step(self, k, *earlier):
        return []

    def sum_outer_x(self, *earlier):
        return []

    def sum_outer_last(self, *earlier):
        return self.scatter(self.outer_total)


def join_vectors(parts):
    total = sum(part.shape[0] for part in parts)
    made, begin = 0.0, 0
    for part in parts:
        made = made + jnp.pad(wide_of(part), (begin, total - begin - part.shape[0]))
        begin += part.shape[0]
    return low(made)


def per_device(
    first_half,
    second_half,
    grad_first,
    grad_second,
    query_weight,
    value_weight,
    output_weight,
    inner_weight,
    inner_bias,
    outer_weight,
    outer_bias,
    mixer_gain,
    mixer_shift,
    feed_gain,
    feed_shift,
    parents,
    buckets,
    order,
    *,
    dp_size,
    fsdp_size,
):
    trees = first_half.shape[0]
    row_count = first_half.shape[2]
    features = first_half.shape[3]
    hidden = inner_weight.shape[1]
    rounds = buckets.shape[2]
    tree_len = buckets.shape[3]
    segments = parents.shape[2]
    all_rows = trees * row_count
    devices = dp_size * fsdp_size
    local_heads = H // (fsdp_size // trees)
    wide = local_heads * DH
    linked = (dp_size, fsdp_size, trees) == (8, 4, 2)
    plan = PairPlan() if linked else GroupPlan(fsdp_size, trees)
    moves = LinkMoves(plan) if linked else PlainMoves(plan, wide)
    coords = moves.coords

    first = first_half[:, 0]
    second = second_half[:, 0]
    grad_b = grad_second[:, 0]

    def flat(value):
        return value.reshape(all_rows, features)

    small_parts = (inner_bias, outer_bias, mixer_gain, mixer_shift, feed_gain, feed_shift)
    small_sizes = [v.shape[0] for v in small_parts]
    mix_unit, mix_factor = norm_stats(second)
    small, (q_side, v_side), unit_tree = moves.gather_first(
        join_vectors(small_parts)[None],
        query_weight,
        value_weight,
        output_weight,
        lambda early: plan.rows_to_tree(after(low(mix_unit), early)),
    )
    small = wide_of(small)
    vectors = []
    begin = 0
    for size in small_sizes:
        vectors.append(small[:, begin:begin + size].reshape(1, -1))
        begin += size
    bias_inner, bias_outer, gain_mix, shift_mix, gain_feed, shift_feed = vectors

    moves.gather_inner(inner_weight)
    moves.gather_outer(outer_weight)

    mixed_tree = low(wide_of(unit_tree) * gain_mix + shift_mix)
    parent_row = lax.dynamic_index_in_dim(after(parents, *moves.small_early)[:, 0], plan.tree, 0, False)
    bucket_rows = lax.dynamic_index_in_dim(after(buckets, *moves.small_early)[:, 0], plan.tree, 0, False)
    branch = parent_row[jnp.clip(parent_row, 0, segments - 1)]
    trunk_end = jnp.where(jnp.arange(segments) >= TRUNK + BRANCHES, branch, parent_row)
    info = jnp.concatenate([parent_row, trunk_end])
    codes = position_codes(bucket_rows)
    codes_q = jnp.pad(codes, ((0, 0), (0, 128 - rounds)))
    codes_k = jnp.pad(codes.T, ((0, 8 - rounds), (0, 0)))
    query_key, value_rows = project(coords, mixed_tree, q_side, v_side, wide)
    attend, attend_back = attention_calls(tree_len, local_heads, rounds, segments)
    moves.inner_plane(query_key)
    o_side = moves.output_plane(query_key)
    moves.outer_plane(query_key)
    attended, totals, counts = attend(info, query_key, value_rows, codes_q, codes_k)
    moves.outer_next(attended)
    attended_low = flat(plan.heads_to_rows(after(attended, *moves.inner_first, *moves.output_last)))
    moves.inner_across(*plan.far_made)

    first_out, feed_low = out_project(coords, attended_low, flat(first), gain_feed, shift_feed, o_side)
    i_side = moves.inner_finish(feed_low)
    moves.outer_next(feed_low)
    outer_low = flat(low(grad_b))
    active, slope, outer_parts = feed_in(
        coords, feed_low, outer_low, bias_inner, i_side, moves.outer_form(*outer_weight.shape), moves.block_of
    )
    outer_ring = moves.sum_outer_first(outer_parts)
    second_out, grad_feed, inner_bias_sum, inner_parts = feed_out(
        coords,
        feed_low,
        outer_low,
        flat(second),
        bias_outer,
        active,
        slope,
        i_side,
        moves.outer_finish(),
        moves.inner_form(*inner_weight.shape),
        moves.block_of,
    )
    outer_bias_sum = jnp.sum(wide_of(outer_low), axis=0)
    (grad_first_in, grad_attended, feed_gain_sum, feed_shift_sum), output_parts = out_back(
        coords,
        after(grad_feed, *outer_ring),
        first_out,
        flat(grad_first),
        attended_low,
        gain_feed,
        o_side,
        moves.output_form(output_weight.shape[0], features),
    )


    outer_ring = moves.sum_outer_step(2, grad_feed)
    grad_attended = after(grad_attended, *moves.sum_inner_cores(inner_parts))
    grad_heads = plan.rows_to_heads(grad_attended.reshape(trees, row_count, features))
    inner_grad, output_grad = moves.sum_inner(inner_parts, output_parts, *plan.far_made)
    query_low, value_low = attend_back(info, query_key, value_rows, attended, grad_heads, totals, counts)
    outer_ring = moves.sum_outer_step(3, query_low)
    q_form, v_form = moves.heads_form(query_weight.shape[0], wide)
    (partial, mix_gain_sum, mix_shift_sum), query_parts, value_parts = project_back(
        coords,
        mixed_tree,
        unit_tree,
        after(query_low, *moves.inner_sum_first, *moves.inner_sum_sent),
        value_low,
        q_side,
        v_side,
        q_form,
        v_form,
    )
    moves.sum_heads(query_parts, value_parts, *moves.inner_sum_last)
    moves.sum_outer_x(*moves.heads_sum)
    grad_mixed = plan.partial_to_rows(partial, *moves.heads_sum[:1])
    query_grad, value_grad = moves.sum_heads_last(*plan.far_made)
    outer_grad = moves.sum_outer_last()
    grad_second_in = grad_b + norm_back(mix_unit, mix_factor, gain_mix, grad_mixed)

    small_sums = [inner_bias_sum, outer_bias_sum, mix_gain_sum, mix_shift_sum, feed_gain_sum, feed_shift_sum]
    packed = moves.scatter_small(jnp.concatenate([v.reshape(devices, -1) for v in small_sums], axis=1))[0]
    pieces = []
    begin = 0
    for size in small_sizes:
        pieces.append(packed[begin:begin + size])
        begin += size
    return (
        first_out.reshape(first_half.shape),
        second_out.reshape(first_half.shape),
        grad_first_in.reshape(first_half.shape),
        grad_second_in[:, None],
        query_grad,
        value_grad,
        output_grad,
        inner_grad,
        pieces[0],
        outer_grad,
        pieces[1],
        pieces[2],
        pieces[3],
        pieces[4],
        pieces[5],
    )


def solution(mesh):
    rows = P(None, "dp", "fsdp", None)
    matrix = P(AXES, None)
    vector = P(AXES)
    weights = (matrix, matrix, matrix, matrix, vector, matrix, vector, vector, vector, vector, vector)
    return jax.shard_map(
        functools.partial(per_device, dp_size=mesh.shape["dp"], fsdp_size=mesh.shape["fsdp"]),
        mesh=mesh,
        in_specs=(rows,) * 4 + weights + (P(None, "dp", None), P(None, "dp", None, None), P(None, "dp", None, None)),
        out_specs=(rows,) * 4 + weights,
        check_vma=False,
    )
```

```python
import functools
import math

import jax
import jax.numpy as jnp
from jax import lax
from jax.experimental import pallas as pl
from jax.experimental.pallas import tpu as pltpu
from jax.sharding import PartitionSpec as P

H = 8
DH = 128
CH = 64
SEG = 128
TRUNK = 4
BRANCHES = 2
NBUCK = 32
SELF_SCORE = -10000.0
NEG_SCORE = -1e30
EPSILON = 1e-06
BF = jnp.bfloat16
F32 = jnp.float32
AXES = ("dp", "fsdp")
GELU_A = math.sqrt(2.0 / math.pi)
GELU_B = 0.044715


def norm_stats(values):
    center = values - jnp.mean(values, axis=-1, keepdims=True)
    factor = lax.rsqrt(jnp.mean(center * center, axis=-1, keepdims=True) + EPSILON)
    return center * factor, factor


def norm_back(unit, factor, gain_vec, grad):
    scaled = grad * gain_vec
    inner = jnp.mean(scaled * unit, axis=-1, keepdims=True)
    return factor * (scaled - jnp.mean(scaled, axis=-1, keepdims=True) - unit * inner)


def position_codes(bucket_rows):
    rounds, tree_len = bucket_rows.shape
    buckets_t = bucket_rows.T
    lanes = jnp.arange(rounds * NBUCK, dtype=jnp.int32)
    member = (jnp.repeat(buckets_t, NBUCK, axis=1) == (lanes % NBUCK)[None, :]).astype(F32)
    rows = jnp.arange(tree_len, dtype=jnp.int32)
    lower = (rows[:, None] >= rows[None, :]).astype(BF)
    ranks = jnp.dot(lower, member.astype(BF), preferred_element_type=F32)
    totals = ranks[-1]
    before = ((lanes[:, None] // NBUCK == lanes[None, :] // NBUCK) & (lanes[:, None] < lanes[None, :])).astype(F32)
    offsets = jnp.sum(totals[:, None] * before, axis=0)
    places = jnp.sum((member * (ranks - 1.0 + offsets[None, :])).reshape(tree_len, rounds, NBUCK), axis=-1)
    return buckets_t.astype(F32) * tree_len + jnp.floor((places + 0.5) / CH)


def seg_parts(seg, info_ref):
    parts = []
    prefix = min(seg, TRUNK) * SEG
    if prefix:
        parts.append((0, prefix, 0, False))
    if seg >= TRUNK + BRANCHES:
        start = pl.multiple_of(info_ref[seg] * SEG, SEG)
        parts.append((start, SEG, TRUNK * SEG, False))
    parts.append((seg * SEG, SEG, (TRUNK + 1) * SEG, True))
    return parts


def unit_rows(rows_f32):
    factor = lax.rsqrt(jnp.mean(rows_f32 * rows_f32, axis=-1, keepdims=True) + EPSILON)
    return rows_f32 * factor * (1.0 / math.sqrt(DH)), factor


def own_diagonal():
    row = lax.broadcasted_iota(jnp.int32, (SEG, SEG), 0)
    col = lax.broadcasted_iota(jnp.int32, (SEG, SEG), 1)
    return row == col


def attention_forward_kernel(segments, rounds, info_ref, q_ref, v_ref, cq_ref, ck_ref, out_ref, total_ref, count_ref, unit_ref):
    head = pl.program_id(0)

    @pl.when(head == 0)
    def _():
        row = lax.broadcasted_iota(jnp.int32, (SEG, SEG), 0)
        col = lax.broadcasted_iota(jnp.int32, (SEG, SEG), 1)
        total_ref[...] = jnp.zeros_like(total_ref)
        for seg in range(segments):
            query = cq_ref[seg * SEG:(seg + 1) * SEG, :]
            for start, size, column, own in seg_parts(seg, info_ref):
                for piece in range(size // SEG):
                    first = start + piece * SEG
                    key = ck_ref[:, pl.ds(first, SEG)]
                    counted = jnp.zeros((SEG, SEG), F32)
                    for turn in range(rounds):
                        gap = query[:, turn:turn + 1] - key[turn:turn + 1, :]
                        counted = counted + jnp.where(jnp.abs(gap - 0.5) < 0.75, 1.0, 0.0)
                    if own:
                        counted = jnp.where(row >= col, counted, 0.0)
                    elif column == 0 and seg >= TRUNK:
                        counted = counted * jnp.where(info_ref[segments + seg] >= piece, 1.0, 0.0)
                    begin = column + piece * SEG
                    count_ref[seg * SEG:(seg + 1) * SEG, begin:begin + SEG] = counted.astype(BF)

    unit_ref[...] = unit_rows(q_ref[...].astype(F32))[0].astype(BF)
    diagonal = own_diagonal()
    lane = lax.broadcasted_iota(jnp.int32, (SEG, 128), 1)
    for seg in range(segments):
        rows = slice(seg * SEG, (seg + 1) * SEG)
        query = q_ref[rows, :]
        scored = []
        top = None
        for start, size, column, own in seg_parts(seg, info_ref):
            keys = pl.ds(start, size)
            scores = lax.dot_general(query, unit_ref[keys, :], (((1,), (1,)), ((), ())), preferred_element_type=F32)
            counted = count_ref[rows, column:column + size].astype(F32)
            if own:
                scores = jnp.where(diagonal, SELF_SCORE, scores)
            scores = jnp.where(counted > 0.0, scores, NEG_SCORE)
            best = jnp.max(scores, axis=-1, keepdims=True)
            top = best if top is None else jnp.maximum(top, best)
            scored.append((keys, scores, counted))
        amount = jnp.zeros((SEG, 1), F32)
        result = jnp.zeros((SEG, DH), F32)
        for keys, scores, counted in scored:
            weight = counted * jnp.exp(scores - top)
            amount = amount + jnp.sum(weight, axis=-1, keepdims=True)
            result = result + jnp.dot(weight.astype(BF), v_ref[keys, :], preferred_element_type=F32)
        out_ref[rows, :] = (result / amount).astype(BF)
        total = top + jnp.log(amount)
        total_ref[rows, :] = jnp.where(lane == head, total, total_ref[rows, :])


def attention_backward_kernel(segments, info_ref, q_ref, v_ref, out_ref, grad_ref, total_ref, count_ref, dq_ref, dv_ref, unit_ref, chance_ref, slope_ref, key_acc, value_acc, query_acc):
    head = pl.program_id(0)
    trunk = TRUNK * SEG
    whole = q_ref[...].astype(F32)
    unit, factor = unit_rows(whole)
    unit_ref[...] = unit.astype(BF)

    @pl.when(head == 0)
    def _():
        chance_ref[0:trunk, 0:trunk] = jnp.zeros((trunk, trunk), BF)
        slope_ref[0:trunk, 0:trunk] = jnp.zeros((trunk, trunk), BF)

    diagonal = own_diagonal()
    lane = lax.broadcasted_iota(jnp.int32, (SEG, 128), 1)
    for seg in range(segments):
        rows = slice(seg * SEG, (seg + 1) * SEG)
        query = q_ref[rows, :]
        grad = grad_ref[rows, :]
        total = jnp.sum(jnp.where(lane == head, total_ref[rows, :], 0.0), axis=-1, keepdims=True)
        delta = jnp.sum(grad.astype(F32) * out_ref[rows, :].astype(F32), axis=-1, keepdims=True)
        query_grad = jnp.zeros((SEG, DH), F32)
        for start, size, column, own in seg_parts(seg, info_ref):
            keys = pl.ds(start, size)
            scores = lax.dot_general(query, unit_ref[keys, :], (((1,), (1,)), ((), ())), preferred_element_type=F32)
            counted = count_ref[rows, column:column + size].astype(F32)
            if own:
                scores = jnp.where(diagonal, SELF_SCORE, scores)
            scores = jnp.where(counted > 0.0, scores, NEG_SCORE)
            chance = counted * jnp.exp(scores - total)
            reach = lax.dot_general(grad, v_ref[keys, :], (((1,), (1,)), ((), ())), preferred_element_type=F32)
            slope = chance * (reach - delta)
            if own:
                slope = jnp.where(diagonal, 0.0, slope)
            slope = slope.astype(BF)
            chance_ref[rows, column:column + size] = chance.astype(BF)
            slope_ref[rows, column:column + size] = slope
            query_grad = query_grad + jnp.dot(slope, unit_ref[keys, :], preferred_element_type=F32)
        query_acc[rows, :] = query_grad

    for weight_ref, side_ref, acc in ((chance_ref, grad_ref, value_acc), (slope_ref, q_ref, key_acc)):
        acc[0:trunk, :] = lax.dot_general(weight_ref[:, 0:trunk], side_ref[...], (((0,), (0,)), ((), ())), preferred_element_type=F32)
        for seg in range(segments):
            rows = slice(seg * SEG, (seg + 1) * SEG)
            leaf = seg >= TRUNK + BRANCHES
            begin = trunk if leaf else trunk + SEG
            added = lax.dot_general(weight_ref[rows, begin:trunk + 2 * SEG], side_ref[rows, :], (((0,), (0,)), ((), ())), preferred_element_type=F32)
            if leaf:
                above = pl.ds(pl.multiple_of(info_ref[seg] * SEG, SEG), SEG)
                acc[above, :] += added[0:SEG]
                added = added[SEG:]
            acc[rows, :] = added if seg >= TRUNK else acc[rows, :] + added

    key_grad = key_acc[...]
    along = jnp.mean(key_grad * whole, axis=-1, keepdims=True) * (factor * factor)
    dq_ref[...] = (query_acc[...] + (factor * (1.0 / math.sqrt(DH))) * (key_grad - whole * along)).astype(BF)
    dv_ref[...] = value_acc[...].astype(BF)


def attention_calls(tree_len, local_heads, rounds, segments):
    head_spec = pl.BlockSpec((tree_len, DH), lambda h, info: (0, h))
    side = pl.BlockSpec((tree_len, 128), lambda h, info: (0, 0))
    count_spec = pl.BlockSpec((tree_len, (TRUNK + 2) * SEG), lambda h, info: (0, 0))
    wide = local_heads * DH
    forward = pl.pallas_call(
        functools.partial(attention_forward_kernel, segments, rounds),
        grid_spec=pltpu.PrefetchScalarGridSpec(
            num_scalar_prefetch=1,
            grid=(local_heads,),
            in_specs=[head_spec, head_spec, side, pl.BlockSpec((8, tree_len), lambda h, info: (0, 0))],
            out_specs=[head_spec, side, count_spec],
            scratch_shapes=[pltpu.VMEM((tree_len, DH), BF)],
        ),
        out_shape=[
            jax.ShapeDtypeStruct((tree_len, wide), BF),
            jax.ShapeDtypeStruct((tree_len, 128), F32),
            jax.ShapeDtypeStruct((tree_len, (TRUNK + 2) * SEG), BF),
        ],
        compiler_params=pltpu.CompilerParams(vmem_limit_bytes=40 << 20),
        cost_estimate=cost(18),
        name="attention_forward",
    )
    backward = pl.pallas_call(
        functools.partial(attention_backward_kernel, segments),
        grid_spec=pltpu.PrefetchScalarGridSpec(
            num_scalar_prefetch=1,
            grid=(local_heads,),
            in_specs=[head_spec, head_spec, head_spec, head_spec, side, count_spec],
            out_specs=[head_spec, head_spec],
            scratch_shapes=[pltpu.VMEM((tree_len, DH), BF)]
            + [pltpu.VMEM((tree_len, (TRUNK + 2) * SEG), BF)] * 2
            + [pltpu.VMEM((tree_len, DH), F32)] * 3,
        ),
        out_shape=[jax.ShapeDtypeStruct((tree_len, wide), BF)] * 2,
        compiler_params=pltpu.CompilerParams(vmem_limit_bytes=40 << 20),
        cost_estimate=cost(21),
        name="attention_backward",
    )
    return forward, backward


def row_block(where_fn, coords_ref, span):
    return pl.ds(pl.multiple_of(where_fn(coords_ref) * span, span), span)


def piece_view(refs, piece):
    view = refs[piece[0]].at[piece[1]] if piece[1] else refs[piece[0]]
    if piece[2] is None:
        return view
    return view.at[pl.ds(piece[2][0], piece[3]), pl.ds(piece[2][1], piece[5][1])]


def whole_view(whole, coords_ref, piece):
    rows = row_block(piece[4], coords_ref, piece[3])
    first = piece[5][0]
    if callable(first):
        first = pl.multiple_of(first(coords_ref) * piece[5][1], piece[5][1])
    return whole.at[rows, pl.ds(first, piece[5][1])]


def load_pieces(coords_ref, refs, pieces, target, sems, first):
    return [
        pltpu.make_async_copy(piece_view(refs, piece), whole_view(target, coords_ref, piece), sems.at[first + number])
        for number, piece in enumerate(pieces)
    ]


def store_pieces(coords_ref, source, refs, pieces, sems, first):
    return [
        pltpu.make_async_copy(whole_view(source, coords_ref, piece), piece_view(refs, piece), sems.at[first + number])
        for number, piece in enumerate(pieces)
    ]


def project_kernel(q_pieces, v_pieces, q_count, v_count, coords_ref, mixed_ref, *refs):
    q_refs, v_refs = refs[:q_count], refs[q_count:q_count + v_count]
    q_out, v_out, q_weight, v_weight, sems = refs[q_count + v_count:]
    to_q = load_pieces(coords_ref, q_refs, q_pieces, q_weight, sems, 0)
    to_v = load_pieces(coords_ref, v_refs, v_pieces, v_weight, sems, len(q_pieces))
    for copy in to_q + to_v:
        copy.start()
    for copy in to_q:
        copy.wait()
    q_out[...] = jnp.dot(mixed_ref[...], q_weight[...], preferred_element_type=F32).astype(BF)
    for copy in to_v:
        copy.wait()
    v_out[...] = jnp.dot(mixed_ref[...], v_weight[...], preferred_element_type=F32).astype(BF)


VM = pl.BlockSpec(memory_space=pltpu.VMEM)
ANYWHERE = pl.BlockSpec(memory_space=pl.ANY)


def cost(micros):
    return pl.CostEstimate(flops=int(micros * 1e7), transcendentals=0, bytes_accessed=0)


def kernel_call(body, ins, outs, scratch, name, limit, micros, grid=()):
    return pl.pallas_call(
        body,
        grid_spec=pltpu.PrefetchScalarGridSpec(num_scalar_prefetch=1, grid=grid, in_specs=ins, out_specs=outs[0], scratch_shapes=scratch),
        out_shape=outs[1],
        compiler_params=pltpu.CompilerParams(vmem_limit_bytes=limit << 20),
        cost_estimate=cost(micros),
        name=name,
    )


def project(coords, mixed_tree, q_side, v_side, wide):
    q_arrays, q_pieces = q_side
    v_arrays, v_pieces = v_side
    rows, features = mixed_tree.shape
    body = functools.partial(project_kernel, q_pieces, v_pieces, len(q_arrays), len(v_arrays))
    return kernel_call(
        body,
        [VM] + [ANYWHERE] * (len(q_arrays) + len(v_arrays)),
        ([VM, VM], [jax.ShapeDtypeStruct((rows, wide), BF)] * 2),
        [pltpu.VMEM((features, wide), BF)] * 2 + [pltpu.SemaphoreType.DMA((len(q_pieces) + len(v_pieces),))],
        "project",
        40,
        7,
    )(coords, mixed_tree, *q_arrays, *v_arrays)


def project_back_kernel(q_pieces, v_pieces, q_count, v_count, q_outs, v_outs, q_made, v_made, coords_ref, mixed_ref, unit_ref, dq_ref, dv_ref, *refs):
    q_refs, v_refs = refs[:q_count], refs[q_count:q_count + v_count]
    rest = refs[q_count + v_count:]
    partial_ref, gain_sum, shift_sum = rest[:3]
    rest = rest[3:]
    q_grads, v_grads = rest[:q_made], rest[q_made:q_made + v_made]
    q_weight, v_weight, q_sum, v_sum, sems = rest[q_made + v_made:]
    to_q = load_pieces(coords_ref, q_refs, q_pieces, q_weight, sems, 0)
    to_v = load_pieces(coords_ref, v_refs, v_pieces, v_weight, sems, len(q_pieces))
    for copy in to_q + to_v:
        copy.start()
    used = len(q_pieces) + len(v_pieces)
    turned = (((0,), (0,)), ((), ()))
    crossed = (((1,), (1,)), ((), ()))
    q_sum[...] = lax.dot_general(mixed_ref[...], dq_ref[...], turned, preferred_element_type=F32).astype(BF)
    from_q = store_pieces(coords_ref, q_sum, q_grads, q_outs, sems, used)
    for copy in from_q:
        copy.start()
    v_sum[...] = lax.dot_general(mixed_ref[...], dv_ref[...], turned, preferred_element_type=F32).astype(BF)
    from_v = store_pieces(coords_ref, v_sum, v_grads, v_outs, sems, used + len(q_outs))
    for copy in from_v:
        copy.start()
    for copy in to_q + to_v:
        copy.wait()
    partial = lax.dot_general(dq_ref[...], q_weight[...], crossed, preferred_element_type=F32) + lax.dot_general(
        dv_ref[...], v_weight[...], crossed, preferred_element_type=F32
    )
    partial_ref[...] = partial.astype(BF)
    gain_sum[...] = jnp.sum(partial * unit_ref[...].astype(F32), axis=0, keepdims=True)
    shift_sum[...] = jnp.sum(partial, axis=0, keepdims=True)
    for copy in from_q + from_v:
        copy.wait()


def project_back(coords, mixed_tree, unit_tree, dq, dv, q_side, v_side, q_form, v_form):
    q_arrays, q_pieces = q_side
    v_arrays, v_pieces = v_side
    q_shapes, q_outs = q_form
    v_shapes, v_outs = v_form
    rows, features = mixed_tree.shape
    wide = dq.shape[1]
    body = functools.partial(
        project_back_kernel, q_pieces, v_pieces, len(q_arrays), len(v_arrays), q_outs, v_outs, len(q_shapes), len(v_shapes)
    )
    made = kernel_call(
        body,
        [VM] * 4 + [ANYWHERE] * (len(q_arrays) + len(v_arrays)),
        (
            [VM] * 3 + [ANYWHERE] * (len(q_shapes) + len(v_shapes)),
            [jax.ShapeDtypeStruct((rows, features), BF)]
            + [jax.ShapeDtypeStruct((1, features), F32)] * 2
            + [jax.ShapeDtypeStruct(s, BF) for s in q_shapes + v_shapes],
        ),
        [pltpu.VMEM((features, wide), BF)] * 4
        + [pltpu.SemaphoreType.DMA((len(q_pieces) + len(v_pieces) + len(q_outs) + len(v_outs),))],
        "project_back",
        50,
        18,
    )(coords, mixed_tree, unit_tree, dq, dv, *q_arrays, *v_arrays)
    return made[:3], made[3:3 + len(q_shapes)], made[3 + len(q_shapes):]


def normalised(values):
    center = values - jnp.mean(values, axis=-1, keepdims=True)
    factor = lax.rsqrt(jnp.mean(center * center, axis=-1, keepdims=True) + EPSILON)
    return center * factor, factor


def out_kernel(pieces, count, coords_ref, att_ref, first_ref, gain_ref, shift_ref, *refs):
    o_refs = refs[:count]
    first_out, feed_out, weight, sems = refs[count:]
    copies = load_pieces(coords_ref, o_refs, pieces, weight, sems, 0)
    for copy in copies:
        copy.start()
    for copy in copies:
        copy.wait()
    made = first_ref[...] + jnp.dot(att_ref[...], weight[...], preferred_element_type=F32)
    first_out[...] = made
    feed_out[...] = (normalised(made)[0] * gain_ref[...] + shift_ref[...]).astype(BF)


def out_project(coords, att, first, gain, shift, side):
    arrays, pieces = side
    rows, features = first.shape
    return kernel_call(
        functools.partial(out_kernel, pieces, len(arrays)),
        [VM] * 4 + [ANYWHERE] * len(arrays),
        ([VM, VM], [jax.ShapeDtypeStruct((rows, features), F32), jax.ShapeDtypeStruct((rows, features), BF)]),
        [pltpu.VMEM((features, features), BF), pltpu.SemaphoreType.DMA((len(pieces),))],
        "out_project",
        50,
        8,
    )(coords, att, first, gain, shift, *arrays)


def out_back_kernel(pieces, count, outs, made, coords_ref, back_ref, first_ref, grad_ref, att_ref, gain_ref, *refs):
    o_refs = refs[:count]
    rest = refs[count:]
    grad_in, grad_att, gain_sum, shift_sum = rest[:4]
    grads = rest[4:4 + made]
    weight, total, sems = rest[4 + made:]
    copies = load_pieces(coords_ref, o_refs, pieces, weight, sems, 0)
    for copy in copies:
        copy.start()
    back = back_ref[...]
    unit, factor = normalised(first_ref[...])
    gain_sum[...] = jnp.sum(back * unit, axis=0, keepdims=True)
    shift_sum[...] = jnp.sum(back, axis=0, keepdims=True)
    scaled = back * gain_ref[...]
    inner = jnp.mean(scaled * unit, axis=-1, keepdims=True)
    value = grad_ref[...] + factor * (scaled - jnp.mean(scaled, axis=-1, keepdims=True) - unit * inner)
    grad_in[...] = value
    low = value.astype(BF)
    total[...] = lax.dot_general(att_ref[...], low, (((0,), (0,)), ((), ())), preferred_element_type=F32).astype(BF)
    stores = store_pieces(coords_ref, total, grads, outs, sems, len(pieces))
    for copy in stores:
        copy.start()
    for copy in copies:
        copy.wait()
    grad_att[...] = lax.dot_general(low, weight[...], (((1,), (1,)), ((), ())), preferred_element_type=F32).astype(BF)
    for copy in stores:
        copy.wait()


def out_back(coords, back, first_out, grad, att, gain, side, form):
    arrays, pieces = side
    shapes, outs = form
    rows, features = back.shape
    full = jax.ShapeDtypeStruct((rows, features), F32)
    line = jax.ShapeDtypeStruct((1, features), F32)
    made = kernel_call(
        functools.partial(out_back_kernel, pieces, len(arrays), outs, len(shapes)),
        [VM] * 5 + [ANYWHERE] * len(arrays),
        (
            [VM] * 4 + [ANYWHERE] * len(shapes),
            [full, jax.ShapeDtypeStruct((rows, features), BF), line, line] + [jax.ShapeDtypeStruct(s, BF) for s in shapes],
        ),
        [pltpu.VMEM((features, features), BF)] * 2 + [pltpu.SemaphoreType.DMA((len(pieces) + len(outs),))],
        "out_back",
        60,
        12,
    )(coords, back, first_out, grad, att, gain, *arrays)
    return made[:4], made[4:]


def feed_in_kernel(plan, counts, coords_ref, feed_ref, grad_ref, bias_ref, *refs):
    pieces, step_outs, block_of = plan
    i_count, made = counts
    i_refs = refs[:i_count]
    active_ref, slope_ref = refs[i_count:i_count + 2]
    grads = refs[i_count + 2:i_count + 2 + made]
    weight, outer_sum, in_sems, out_sems = refs[i_count + 2 + made:]
    step = pl.program_id(0)
    slot = lax.rem(step, 2)
    tile = outer_sum.shape[1]
    count = len(step_outs)

    def store(number):
        return store_pieces(coords_ref, outer_sum.at[number % 2], grads, step_outs[number], out_sems.at[number % 2], 0)

    @pl.when(step == 0)
    def _():
        copies = load_pieces(coords_ref, i_refs, pieces, weight, in_sems, 0)
        for copy in copies:
            copy.start()
        for copy in copies:
            copy.wait()

    for number in range(2, count):

        @pl.when(step == number)
        def _(number=number):
            for copy in store(number - 2):
                copy.wait()

    columns = pl.ds(pl.multiple_of(block_of(step, coords_ref) * tile, tile), tile)
    value = jnp.dot(feed_ref[...], weight[:, columns], preferred_element_type=F32) + bias_ref[:, columns]
    square = value * value
    bend = jnp.tanh(GELU_A * (value + GELU_B * (square * value)))
    half = 0.5 * (1.0 + bend)
    active = (value * half).astype(BF)
    active_ref[...] = active
    slope_ref[...] = (half + 0.5 * value * (1.0 - bend * bend) * (GELU_A * (1.0 + 3.0 * GELU_B * square))).astype(BF)
    outer_sum[slot] = lax.dot_general(active, grad_ref[...], (((0,), (0,)), ((), ())), preferred_element_type=F32).astype(BF)

    for number in range(count):

        @pl.when(step == number)
        def _(number=number):
            for copy in store(number):
                copy.start()
            if number == count - 1:
                for last in range(max(0, number - 1), count):
                    for copy in store(last):
                        copy.wait()


def feed_in(coords, feed, grad, bias, side, form, block_of):
    arrays, pieces = side
    shapes, step_outs = form
    rows, features = feed.shape
    hidden = bias.shape[1]
    tile = hidden // len(step_outs)
    most = max(len(outs) for outs in step_outs)
    block = pl.BlockSpec((rows, tile), lambda j, co: (0, block_of(j, co)))
    made = kernel_call(
        functools.partial(feed_in_kernel, (pieces, step_outs, block_of), (len(arrays), len(shapes))),
        [VM] * 3 + [ANYWHERE] * len(arrays),
        (
            [block, block] + [ANYWHERE] * len(shapes),
            [jax.ShapeDtypeStruct((rows, hidden), BF)] * 2 + [jax.ShapeDtypeStruct(s, BF) for s in shapes],
        ),
        [
            pltpu.VMEM((features, hidden), BF),
            pltpu.VMEM((2, tile, features), BF),
            pltpu.SemaphoreType.DMA((len(pieces),)),
            pltpu.SemaphoreType.DMA((2, most)),
        ],
        "feed_in",
        60,
        29,
        grid=(len(step_outs),),
    )(coords, feed, grad, bias, *arrays)
    return made[0], made[1], made[2:]


def feed_out_kernel(plan, counts, coords_ref, feed_ref, grad_ref, base_ref, bias_ref, active_ref, slope_ref, *refs):
    i_pieces, i_outs, steps, block_of = plan
    i_count, u_count, made = counts
    i_refs, u_refs = refs[:i_count], refs[i_count:i_count + u_count]
    rest = refs[i_count + u_count:]
    out_ref, back_ref, bias_sum = rest[:3]
    grads = rest[3:3 + made]
    weight, weight_sum, outer, i_sems, u_sems, out_sems = rest[3 + made:]
    step = pl.program_id(0)
    slot = lax.rem(step, 2)
    tile = outer.shape[1]
    count = len(steps)

    def u_load(number):
        return load_pieces(coords_ref, u_refs, steps[number], outer.at[number % 2], u_sems.at[number % 2], 0)

    @pl.when(step == 0)
    def _():
        copies = load_pieces(coords_ref, i_refs, i_pieces, weight, i_sems, 0)
        for copy in u_load(0) + copies:
            copy.start()
        out_ref[...] = base_ref[...] + bias_ref[...]
        back_ref[...] = jnp.zeros_like(back_ref)
        for copy in copies:
            copy.wait()

    for number in range(count):

        @pl.when(step == number)
        def _(number=number):
            if number + 1 < count:
                for copy in u_load(number + 1):
                    copy.start()
            for copy in u_load(number):
                copy.wait()

    columns = pl.ds(pl.multiple_of(block_of(step, coords_ref) * tile, tile), tile)
    grad = grad_ref[...]
    out_ref[...] += jnp.dot(active_ref[...], outer[slot], preferred_element_type=F32)
    pulled = lax.dot_general(grad, outer[slot], (((1,), (1,)), ((), ())), preferred_element_type=F32)
    inner_low = (pulled * slope_ref[...].astype(F32)).astype(BF)
    bias_sum[:, columns] = jnp.sum(inner_low.astype(F32), axis=0, keepdims=True)
    weight_sum[:, columns] = lax.dot_general(feed_ref[...], inner_low, (((0,), (0,)), ((), ())), preferred_element_type=F32).astype(BF)
    back_ref[...] += lax.dot_general(inner_low, weight[:, columns], (((1,), (1,)), ((), ())), preferred_element_type=F32)

    @pl.when(step == count - 1)
    def _():
        copies = store_pieces(coords_ref, weight_sum, grads, i_outs, out_sems, 0)
        for copy in copies:
            copy.start()
        for copy in copies:
            copy.wait()


def feed_out(coords, feed, grad, base, bias, active, slope, i_side, u_side, i_form, block_of):
    i_arrays, i_pieces = i_side
    u_arrays, steps = u_side
    shapes, i_outs = i_form
    rows, features = feed.shape
    hidden = active.shape[1]
    tile = hidden // len(steps)
    most = max(len(pieces) for pieces in steps)
    block = pl.BlockSpec((rows, tile), lambda j, co: (0, block_of(j, co)))
    made = kernel_call(
        functools.partial(feed_out_kernel, (i_pieces, i_outs, steps, block_of), (len(i_arrays), len(u_arrays), len(shapes))),
        [VM] * 4 + [block, block] + [ANYWHERE] * (len(i_arrays) + len(u_arrays)),
        (
            [VM] * 3 + [ANYWHERE] * len(shapes),
            [jax.ShapeDtypeStruct((rows, features), F32)] * 2
            + [jax.ShapeDtypeStruct((1, hidden), F32)]
            + [jax.ShapeDtypeStruct(s, BF) for s in shapes],
        ),
        [
            pltpu.VMEM((features, hidden), BF),
            pltpu.VMEM((features, hidden), BF),
            pltpu.VMEM((2, tile, features), BF),
            pltpu.SemaphoreType.DMA((len(i_pieces),)),
            pltpu.SemaphoreType.DMA((2, most)),
            pltpu.SemaphoreType.DMA((len(i_outs),)),
        ],
        "feed_out",
        60,
        40,
        grid=(len(steps),),
    )(coords, feed, grad, base, bias, active, slope, *i_arrays, *u_arrays)
    return made[0], made[1], made[2], made[3:]


def pick(flag, when_true, when_false):
    return jnp.where(flag, when_true, when_false)


def after(value, *earlier):
    return lax.optimization_barrier((value,) + earlier)[0]


class GroupPlan:
    def __init__(self, size, trees):
        me = lax.axis_index("fsdp")
        self.size = size
        self.trees = trees
        self.group = size // trees
        self.tree = me // self.group
        self.head_group = me % self.group
        self.me = me

    def rows_to_tree(self, rows):
        every = lax.all_gather(rows, "fsdp", axis=1, tiled=True)
        return lax.dynamic_index_in_dim(every, self.tree, 0, False)

    def heads_to_rows(self, heads):
        count = heads.shape[0] // self.size
        every = lax.all_gather(heads, "fsdp", axis=0, tiled=False)
        mine = lax.dynamic_slice_in_dim(every, self.me * count, count, 1)
        mine = mine.reshape(self.trees, self.group, count, heads.shape[1])
        return jnp.moveaxis(mine, 1, 2).reshape(self.trees, count, -1)

    def rows_to_heads(self, rows):
        wide = rows.shape[2] // self.group
        whole = self.rows_to_tree(rows)
        return lax.dynamic_slice_in_dim(whole, self.head_group * wide, wide, 1)

    def partial_to_rows(self, partial):
        every = jnp.zeros((self.trees,) + partial.shape, F32)
        every = lax.dynamic_update_index_in_dim(every, partial.astype(F32), self.tree, 0)
        return lax.psum_scatter(every, "fsdp", scatter_dimension=1, tiled=True)


def low(value):
    return value.astype(BF)


def wide_of(value):
    return value.astype(F32)


def swap_pairs(size, bit):
    return [(i, i ^ bit) for i in range(size)]


def natural(rows, columns):
    return [(0, (), None, rows, (lambda co: co[0] * 0), (0, columns))]


def swap_pairs(size, bit):
    return [(i, i ^ bit) for i in range(size)]


def core(value):
    return lax.ppermute(value, "fsdp", swap_pairs(4, 1))


def over_y(value):
    return lax.ppermute(value, "fsdp", swap_pairs(4, 2))


def over_x(value):
    return lax.ppermute(value, "dp", swap_pairs(8, 1))


def up_z(value):
    return lax.ppermute(value, "dp", [(i, (i + 2) % 8) for i in range(8)])


def bit_move(bit, value):
    if bit < 2:
        return lax.ppermute(value, "fsdp", swap_pairs(4, 1 << bit))
    return lax.ppermute(value, "dp", swap_pairs(8, 1 << (bit - 2)))


def place32(k, rx, ry, rc):
    return lambda co: ((((co[0] + 4 - k) & 3) * 2 + (co[1] ^ rx)) * 2 + (co[2] ^ ry)) * 2 + (co[3] ^ rc)


def place16(k, rx, ry):
    return lambda co: (((co[0] + 4 - k) & 3) * 2 + (co[1] ^ rx)) * 2 + (co[2] ^ ry)


def place4(ry, rc):
    return lambda co: (co[2] ^ ry) * 2 + (co[3] ^ rc)


def hidden_block(step, co):
    return ((co[0] + 4 - (step >> 1)) & 3) * 2 + (co[1] ^ (step & 1))


def heads_pieces(which, rows, half):
    pieces = []
    for outer in range(2):
        for inner in range(2):
            for k in range(4):
                rx, ry = (outer, inner) if which == 0 else (inner, outer)
                pieces.append((outer, (inner, k), None, rows, place16(k, rx, ry), (0, half)))
    return pieces


def output_in_pieces(rows, half):
    pieces = []
    for rc in range(2):
        for rx in range(2):
            for ry in range(2):
                for k in range(4):
                    columns = ((lambda co, rc=rc: co[3] ^ rc), half)
                    pieces.append((rc * 2 + rx, (ry, k), None, rows, place16(k, rx, ry), columns))
    return pieces


def output_out_pieces(count, features):
    pieces = []
    for rc in range(2):
        for ry in range(2):
            for rx in range(2):
                for k in range(4):
                    pieces.append((rc * 2 + ry, (rx, k), None, count, place32(k, rx, ry, rc), (0, features)))
    return pieces


def inner_pieces(count, hidden, cut):
    pieces = []
    for part in range(2):
        for rc in range(2):
            for outer in range(2):
                for inner in range(2):
                    for k in range(4):
                        rx, ry = (outer, inner) if part == 0 else (inner, outer)
                        columns = (0, cut) if part == 0 else (cut, hidden - cut)
                        pieces.append((rc * 4 + part * 2 + outer, (inner, k), None, count, place32(k, rx, ry, rc), columns))
    return pieces


def outer_steps(count, features):
    steps = []
    for k in range(4):
        for rx in range(2):
            steps.append([(rc * 4 + k, (rx, ry), None, count, place4(ry, rc), (0, features)) for ry in range(2) for rc in range(2)])
    return steps


def together(*values):
    return lax.optimization_barrier(values)


def join_vectors(parts):
    total = sum(part.shape[0] for part in parts)
    made, begin = 0.0, 0
    for part in parts:
        made = made + jnp.pad(wide_of(part), (begin, total - begin - part.shape[0]))
        begin += part.shape[0]
    return low(made)


def per_device(
    first_half,
    second_half,
    grad_first,
    grad_second,
    query_weight,
    value_weight,
    output_weight,
    inner_weight,
    inner_bias,
    outer_weight,
    outer_bias,
    mixer_gain,
    mixer_shift,
    feed_gain,
    feed_shift,
    parents,
    buckets,
    order,
    *,
    dp_size,
    fsdp_size,
):
    trees = first_half.shape[0]
    row_count = first_half.shape[2]
    features = first_half.shape[3]
    hidden = inner_weight.shape[1]
    rounds = buckets.shape[2]
    tree_len = buckets.shape[3]
    segments = parents.shape[2]
    all_rows = trees * row_count
    devices = dp_size * fsdp_size
    small_parts = (inner_bias, outer_bias, mixer_gain, mixer_shift, feed_gain, feed_shift)
    small_sizes = [v.shape[0] for v in small_parts]
    small_count = sum(small_sizes)

    first = first_half[:, 0]
    second = second_half[:, 0]
    grad_b = grad_second[:, 0]
    joined = join_vectors(small_parts)[None]

    def flat(value):
        return value.reshape(all_rows, features)

    def split(small):
        vectors, begin = [], 0
        for size in small_sizes:
            vectors.append(small[:, begin:begin + size].reshape(1, -1))
            begin += size
        return vectors

    def tables(tree, *earlier):
        parent_row = lax.dynamic_index_in_dim(after(parents, *earlier)[:, 0], tree, 0, False)
        bucket_rows = lax.dynamic_index_in_dim(after(buckets, *earlier)[:, 0], tree, 0, False)
        branch = parent_row[jnp.clip(parent_row, 0, segments - 1)]
        trunk_end = jnp.where(jnp.arange(segments) >= TRUNK + BRANCHES, branch, parent_row)
        codes = position_codes(bucket_rows)
        return (
            jnp.concatenate([parent_row, trunk_end]),
            jnp.pad(codes, ((0, 0), (0, 128 - rounds))),
            jnp.pad(codes.T, ((0, 8 - rounds), (0, 0))),
        )

    local_heads = H // (fsdp_size // trees)
    wide = local_heads * DH
    attend, attend_back = attention_calls(tree_len, local_heads, rounds, segments)
    outer_low = flat(low(grad_b))
    outer_bias_sum = jnp.sum(wide_of(outer_low), axis=0)

    if (dp_size, fsdp_size, trees) == (8, 4, 2):
        dp, fsdp = lax.axis_index("dp"), lax.axis_index("fsdp")
        bits = [fsdp % 2, fsdp // 2, dp % 2, dp // 2 % 2, dp // 4]
        coords = jnp.stack([dp // 2, dp % 2, fsdp // 2, fsdp % 2]).astype(jnp.int32)
        odd, upper, tree = fsdp % 2 == 1, fsdp // 2 == 1, fsdp // 2
        count, half, cut = query_weight.shape[0], features // 2, hidden * 11 // 16
        outer_count = outer_weight.shape[0]

        def order(flag, one, other, axis=0, join=jnp.stack):
            return join([pick(flag, other, one), pick(flag, one, other)], axis=axis)

        def small_step(bit, made):
            return order(bits[bit] == 1, made, bit_move(bit, made), 0, jnp.concatenate)

        both = jnp.stack([query_weight, value_weight, output_weight])
        got, small_got = together(core(pick(odd, both[:, :, :half], both[:, :, half:])), bit_move(0, joined))
        chip = order(odd, pick(odd, both[:, :, half:], both[:, :, :half]), got, 1, jnp.concatenate)
        small = order(odd, joined, small_got, 0, jnp.concatenate)
        mix_unit, mix_factor = norm_stats(after(second, small))
        unit_low = low(mix_unit)
        ring_got, small, unit_low = together(up_z(chip), small_step(1, small), unit_low)
        ring = [chip, ring_got]
        rows_mine = pick(upper, unit_low[1], unit_low[0])
        rows_got = over_y(pick(upper, unit_low[0], unit_low[1]))
        u_near = jnp.stack([outer_weight, over_y(after(outer_weight, chip))])
        ring_got, small = together(up_z(ring_got), small_step(2, small))
        ring.append(ring_got)
        info, codes_q, codes_k = tables(tree, small)
        u_got = over_x(u_near)
        ring_got, small, u_got, rows_got = together(up_z(ring_got), small_step(3, small), u_got, rows_got)
        ring.append(ring_got)
        u_plane = jnp.stack([u_near, u_got])
        q_near, v_near, o_near = (jnp.stack([r[which] for r in ring]) for which in range(3))
        pair = order(upper, rows_mine, rows_got)
        q_got, v_got, i_got, small, pair_got = together(
            over_y(q_near), over_x(v_near), up_z(after(inner_weight, ring_got)), small_step(4, small), core(pair)
        )
        i_ring = [inner_weight, i_got]
        q_near, v_near = jnp.stack([q_near, q_got]), jnp.stack([v_near, v_got])
        bias_inner, bias_outer, gain_mix, shift_mix, gain_feed, shift_feed = split(wide_of(small))
        unit_tree = order(odd, pair, pair_got, 1).reshape(tree_len, features)
        mixed_tree = low(wide_of(unit_tree) * gain_mix + shift_mix)
        q_got, v_got, i_got, mixed_tree, codes_q, codes_k = together(
            over_x(q_near), over_y(v_near), up_z(i_got), mixed_tree, codes_q, codes_k
        )
        i_ring.append(i_got)
        q_side = ([q_near, q_got], heads_pieces(0, 2 * count, half))
        v_side = ([v_near, v_got], heads_pieces(1, 2 * count, half))

        mixed_tree, i_got, o_near, u_plane = together(mixed_tree, i_got, o_near, u_plane)
        query_key, value_rows = project(coords, mixed_tree, q_side, v_side, wide)
        query_key, value_rows, i_got, o_got = together(query_key, value_rows, up_z(i_got), over_y(o_near))
        i_ring.append(i_got)
        u_ring = [u_plane, up_z(after(u_plane, i_got))]

        a_near = jnp.stack([r[:, :cut] for r in i_ring])
        b_near = jnp.stack([r[:, cut:] for r in i_ring])
        o_near = jnp.stack([o_near, o_got])
        attended, totals, counts = attend(info, query_key, value_rows, codes_q, codes_k)
        attended, totals, counts, a_got, b_got, o_got, u_got = together(
            attended, totals, counts, over_y(a_near), over_x(b_near), over_x(o_near), u_ring[1]
        )
        u_ring[1] = u_got
        u_first = up_z(u_got[0])
        a_near, b_near = jnp.stack([a_near, a_got]), jnp.stack([b_near, b_got])
        a_got = over_x(a_near)
        blocks = attended.reshape(2, 2, row_count, wide)
        got = core(pick(odd, blocks[:, 0], blocks[:, 1]))
        heads = order(odd, pick(odd, blocks[:, 1], blocks[:, 0]), got, 2, jnp.concatenate)
        got = over_y(pick(upper, heads[0], heads[1]))
        attended_low = flat(order(upper, pick(upper, heads[1], heads[0]), got))
        attended_low, o_core, o_core_got, u_first = together(attended_low, core(o_near), core(o_got), u_first)
        o_side = ([o_near, o_got, o_core, o_core_got], output_in_pieces(2 * count, half))

        b_got, u_second = over_y(after(b_near, attended_low)), up_z(after(u_ring[1][1], attended_low))
        first_out, feed_low = out_project(coords, attended_low, flat(first), gain_feed, shift_feed, o_side)
        first_out, feed_low, a_got, b_got, a_core, b_core, u_second = together(
            first_out, feed_low, a_got, b_got, core(a_near), core(b_near), u_second
        )
        u_got = jnp.stack([u_first, u_second])
        feed_low, a_core_got, b_core_got, u_got = together(feed_low, core(a_got), core(b_got), u_got)
        i_side = (
            [a_near, a_got, b_near, b_got, a_core, a_core_got, b_core, b_core_got],
            inner_pieces(count, hidden, cut),
        )
        u_ring += [u_got, up_z(u_got)]

        u_form = ([(2, 2, outer_count, features)] * 8, outer_steps(outer_count, features))
        active, slope, u_parts = feed_in(coords, feed_low, outer_low, bias_inner, i_side, u_form, hidden_block)
        u_cores = [core(u) for u in u_ring[:3]]
        made = together(active, slope, u_ring[3], *u_cores, *u_parts)
        active, slope, u_ring[3] = made[:3]
        u_cores, u_parts = list(made[3:6]), made[6:]
        sent = low(wide_of(u_parts[1]) + wide_of(core(u_parts[5])))
        sent, u_core, active = together(sent, core(u_ring[3]), active)
        u_side = (u_ring + u_cores + [u_core], outer_steps(outer_count, features))

        i_form = (([(2, 4, count, cut)] * 2 + [(2, 4, count, hidden - cut)] * 2) * 2, inner_pieces(count, hidden, cut))
        second_out, grad_feed, inner_bias_sum, i_parts = feed_out(
            coords, feed_low, outer_low, flat(second), bias_outer, active, slope, i_side, u_side, i_form, hidden_block
        )
        made = together(second_out, grad_feed, inner_bias_sum, up_z(sent), *[core(u_parts[4 + k]) for k in (2, 3, 0)], *i_parts)
        second_out, grad_feed, inner_bias_sum, u_got = made[:4]
        u_shares = [wide_of(u_parts[k]) + wide_of(c) for k, c in zip((2, 3, 0), made[4:7])]
        i_parts = made[7:]
        sent = low(wide_of(u_got) + u_shares[0])
        sent, grad_feed = together(sent, grad_feed)
        u_first = up_z(sent[0])
        o_form = ([(2, 4, count, features)] * 4, output_out_pieces(count, features))
        (grad_first_in, grad_attended, feed_gain_sum, feed_shift_sum), o_parts = out_back(
            coords, grad_feed, first_out, flat(grad_first), attended_low, gain_feed, o_side, o_form
        )
        made = together(grad_first_in, grad_attended, u_first, *[core(part) for part in i_parts[4:]], *o_parts)
        grad_first_in, grad_attended, u_first = made[:3]
        i_cores, o_parts = made[3:7], made[7:]
        u_second = up_z(after(sent[1], grad_attended))
        a_keep, a_sent = (wide_of(i_parts[which]) + wide_of(i_cores[which]) for which in range(2))
        rows = grad_attended.reshape(trees, row_count, features)
        got = over_y(pick(upper, rows[0], rows[1]))
        pair = order(upper, pick(upper, rows[1], rows[0]), got)
        a_got = over_x(low(a_sent))
        got = core(pick(odd, pair[..., :half], pair[..., half:]))
        grad_heads = order(odd, pick(odd, pair[..., half:], pair[..., :half]), got, 1).reshape(tree_len, half)
        grad_heads, o_core, o_core_sent, u_second = together(grad_heads, core(o_parts[2]), core(o_parts[3]), u_second)
        u_got = jnp.stack([u_first, u_second])
        small_sums = [inner_bias_sum, outer_bias_sum, None, None, feed_gain_sum, feed_shift_sum]

        def spread(values):
            made, begin = 0.0, 0
            for size, value in zip(small_sizes, values):
                if value is not None:
                    made = made + jnp.pad(value.reshape(devices, size), ((0, 0), (begin, small_count - begin - size)))
                begin += size
            return made

        small = spread(small_sums)
        b_keep, b_sent = (
            jnp.concatenate([wide_of(i_parts[2 + w]) + wide_of(i_cores[2 + w]), wide_of(o_parts[w]) + wide_of(c)], axis=3)
            for w, c in ((0, o_core), (1, o_core_sent))
        )

        sent, b_sent, grad_heads, small = together(low(wide_of(u_got) + u_shares[1]), low(b_sent), grad_heads, small)
        query_low, value_low = attend_back(info, query_key, value_rows, attended, grad_heads, totals, counts)
        query_low, value_low, u_got, a_got, b_got = together(query_low, value_low, up_z(sent), a_got, over_y(b_sent))
        a_keep, b_keep = a_keep + wide_of(a_got), b_keep + wide_of(b_got)
        a_sent, b_sent, query_low = together(low(a_keep[1]), low(b_keep[1]), query_low)
        q_form = ([(2, 4, 2 * count, half)] * 2, heads_pieces(0, 2 * count, half))
        v_form = ([(2, 4, 2 * count, half)] * 2, heads_pieces(1, 2 * count, half))
        (partial, mix_gain_sum, mix_shift_sum), q_parts, v_parts = project_back(
            coords, mixed_tree, unit_tree, query_low, value_low, q_side, v_side, q_form, v_form
        )
        made = together(partial, mix_gain_sum, mix_shift_sum, over_y(a_sent), over_x(b_sent), *q_parts, *v_parts)
        partial, mix_gain_sum, mix_shift_sum, a_got, b_got, q_keep, q_sent, v_keep, v_sent = made

        small = small + spread([None, None, mix_gain_sum, mix_shift_sum, None, None])

        def small_sum(bit, made):
            middle = made.shape[0] // 2
            one = bits[bit] == 1
            return pick(one, made[middle:], made[:middle]) + bit_move(bit, pick(one, made[:middle], made[middle:]))

        i_sum = jnp.concatenate([a_keep[0] + wide_of(a_got), b_keep[0] + wide_of(b_got)], axis=2)
        q_got, v_got, i_got, small = together(over_x(q_sent), over_y(v_sent), up_z(low(i_sum[1])), small_sum(4, small))
        q_sum, v_sum = wide_of(q_keep) + wide_of(q_got), wide_of(v_keep) + wide_of(v_got)
        i_total = wide_of(i_got) + i_sum[2]
        blocks = partial.reshape(2, 2, row_count, features)
        got = core(pick(odd, blocks[:, 0], blocks[:, 1]))
        q_got, v_got, i_got, small, got = together(
            over_y(low(q_sum[1])), over_x(low(v_sum[1])), up_z(low(i_total)), small_sum(3, small), got
        )
        shared = low(wide_of(pick(odd, blocks[:, 1], blocks[:, 0])) + wide_of(got))
        h_sum = jnp.stack([q_sum[0] + wide_of(q_got), v_sum[0] + wide_of(v_got)], axis=1)
        i_total = wide_of(i_got) + i_sum[3]
        rows_got = over_y(pick(upper, shared[0], shared[1]))
        u_sum = wide_of(u_got) + u_shares[2]
        u_got = over_x(low(u_sum[1]))
        h_got, i_got, small = together(up_z(low(h_sum[1])), up_z(low(i_total)), small_sum(2, small))
        h_total = wide_of(h_got) + h_sum[2]
        i_total = wide_of(i_got) + i_sum[0]
        h_got, small, u_got, rows_got = together(up_z(low(h_total)), small_sum(1, small), u_got, rows_got)
        h_total = wide_of(h_got) + h_sum[3]
        u_sum = u_sum[0] + wide_of(u_got)
        h_got, u_got = up_z(low(h_total)), over_y(low(u_sum[1]))
        grad_mixed = wide_of(order(upper, pick(upper, shared[1], shared[0]), rows_got))
        grad_second_in = grad_b + norm_back(mix_unit, mix_factor, gain_mix, grad_mixed)
        packed = small_sum(0, small)[0]
        grad_second_in, h_got, u_got, packed = together(grad_second_in, h_got, u_got, packed)
        h_total = wide_of(h_got) + h_sum[0]
        got = wide_of(core(low(pick(odd, h_total[:, :count], h_total[:, count:]))))
        heads = order(odd, pick(odd, h_total[:, count:], h_total[:, :count]), got, 2, jnp.concatenate)
        query_grad, value_grad = heads[0], heads[1]
        outer_grad = u_sum[0] + wide_of(u_got)
        inner_grad, output_grad = i_total[:, :hidden], i_total[:, hidden:]
    else:
        plan = GroupPlan(fsdp_size, trees)
        coords = jnp.zeros((4,), jnp.int32)

        def gather(shard):
            return lax.all_gather(shard, AXES, axis=0, tiled=True)

        def scatter(total):
            return lax.psum_scatter(wide_of(total), AXES, scatter_dimension=0, tiled=True)

        def own_heads(full):
            return lax.dynamic_slice_in_dim(full, plan.head_group * wide, wide, 1)

        def whole_heads(cols):
            return lax.dynamic_update_slice_in_dim(jnp.zeros((features, features), BF), cols, plan.head_group * wide, 1)

        bias_inner, bias_outer, gain_mix, shift_mix, gain_feed, shift_feed = split(wide_of(gather(joined)))
        q_side = ([own_heads(gather(query_weight))], natural(features, wide))
        v_side = ([own_heads(gather(value_weight))], natural(features, wide))
        o_side = ([gather(output_weight)], natural(features, features))
        i_side = ([gather(inner_weight)], natural(features, hidden))
        tile = min(512, hidden)
        steps = [[(0, (s,), None, tile, (lambda co: co[0] * 0), (0, features))] for s in range(hidden // tile)]
        u_side = ([gather(outer_weight).reshape(-1, tile, features)], steps)
        info, codes_q, codes_k = tables(plan.tree)
        mix_unit, mix_factor = norm_stats(second)
        unit_tree = plan.rows_to_tree(low(mix_unit))
        mixed_tree = low(wide_of(unit_tree) * gain_mix + shift_mix)
        query_key, value_rows = project(coords, mixed_tree, q_side, v_side, wide)
        attended, totals, counts = attend(info, query_key, value_rows, codes_q, codes_k)
        attended_low = flat(plan.heads_to_rows(attended))
        first_out, feed_low = out_project(coords, attended_low, flat(first), gain_feed, shift_feed, o_side)
        active, slope, u_parts = feed_in(
            coords, feed_low, outer_low, bias_inner, i_side, ([(hidden // tile, tile, features)], steps), lambda step, co: step
        )
        second_out, grad_feed, inner_bias_sum, i_parts = feed_out(
            coords,
            feed_low,
            outer_low,
            flat(second),
            bias_outer,
            active,
            slope,
            i_side,
            u_side,
            ([(features, hidden)], natural(features, hidden)),
            lambda step, co: step,
        )
        (grad_first_in, grad_attended, feed_gain_sum, feed_shift_sum), o_parts = out_back(
            coords,
            grad_feed,
            first_out,
            flat(grad_first),
            attended_low,
            gain_feed,
            o_side,
            ([(features, features)], natural(features, features)),
        )
        grad_heads = plan.rows_to_heads(grad_attended.reshape(trees, row_count, features))
        query_low, value_low = attend_back(info, query_key, value_rows, attended, grad_heads, totals, counts)
        form = ([(features, wide)], natural(features, wide))
        (partial, mix_gain_sum, mix_shift_sum), q_parts, v_parts = project_back(
            coords, mixed_tree, unit_tree, query_low, value_low, q_side, v_side, form, form
        )
        grad_mixed = plan.partial_to_rows(partial)
        grad_second_in = grad_b + norm_back(mix_unit, mix_factor, gain_mix, grad_mixed)
        small_sums = [inner_bias_sum, outer_bias_sum, mix_gain_sum, mix_shift_sum, feed_gain_sum, feed_shift_sum]
        packed = scatter(jnp.concatenate([v.reshape(devices, -1) for v in small_sums], axis=1))[0]
        query_grad, value_grad = scatter(whole_heads(q_parts[0])), scatter(whole_heads(v_parts[0]))
        inner_grad, output_grad = scatter(i_parts[0]), scatter(o_parts[0])
        outer_grad = scatter(u_parts[0].reshape(hidden, features))

    pieces = []
    begin = 0
    for size in small_sizes:
        pieces.append(packed[begin:begin + size])
        begin += size
    return (
        first_out.reshape(first_half.shape),
        second_out.reshape(first_half.shape),
        grad_first_in.reshape(first_half.shape),
        grad_second_in[:, None],
        query_grad,
        value_grad,
        output_grad,
        inner_grad,
        pieces[0],
        outer_grad,
        pieces[1],
        pieces[2],
        pieces[3],
        pieces[4],
        pieces[5],
    )


def solution(mesh):
    rows = P(None, "dp", "fsdp", None)
    matrix = P(AXES, None)
    vector = P(AXES)
    weights = (matrix, matrix, matrix, matrix, vector, matrix, vector, vector, vector, vector, vector)
    return jax.shard_map(
        functools.partial(per_device, dp_size=mesh.shape["dp"], fsdp_size=mesh.shape["fsdp"]),
        mesh=mesh,
        in_specs=(rows,) * 4 + weights + (P(None, "dp", None), P(None, "dp", None, None), P(None, "dp", None, None)),
        out_specs=(rows,) * 4 + weights,
        check_vma=False,
    )
```

```python
import functools
import math

import jax
import jax.numpy as jnp
from jax import lax
from jax.experimental import pallas as pl
from jax.experimental.pallas import tpu as pltpu
from jax.sharding import PartitionSpec as P

H = 8
DH = 128
CH = 64
SEG = 128
TRUNK = 4
BRANCHES = 2
NBUCK = 32
SELF_SCORE = -10000.0
NEG_SCORE = -1e30
EPSILON = 1e-06
BF = jnp.bfloat16
F32 = jnp.float32
AXES = ("dp", "fsdp")
GELU_A = math.sqrt(2.0 / math.pi)
GELU_B = 0.044715


def norm_stats(values):
    center = values - jnp.mean(values, axis=-1, keepdims=True)
    factor = lax.rsqrt(jnp.mean(center * center, axis=-1, keepdims=True) + EPSILON)
    return center * factor, factor


def norm_back(unit, factor, gain_vec, grad):
    scaled = grad * gain_vec
    inner = jnp.mean(scaled * unit, axis=-1, keepdims=True)
    return factor * (scaled - jnp.mean(scaled, axis=-1, keepdims=True) - unit * inner)


def position_codes(bucket_rows):
    rounds, tree_len = bucket_rows.shape
    buckets_t = bucket_rows.T
    lanes = jnp.arange(rounds * NBUCK, dtype=jnp.int32)
    member = (jnp.repeat(buckets_t, NBUCK, axis=1) == (lanes % NBUCK)[None, :]).astype(F32)
    rows = jnp.arange(tree_len, dtype=jnp.int32)
    lower = (rows[:, None] >= rows[None, :]).astype(BF)
    ranks = jnp.dot(lower, member.astype(BF), preferred_element_type=F32)
    totals = ranks[-1]
    before = ((lanes[:, None] // NBUCK == lanes[None, :] // NBUCK) & (lanes[:, None] < lanes[None, :])).astype(F32)
    offsets = jnp.sum(totals[:, None] * before, axis=0)
    places = jnp.sum((member * (ranks - 1.0 + offsets[None, :])).reshape(tree_len, rounds, NBUCK), axis=-1)
    return buckets_t.astype(F32) * tree_len + jnp.floor((places + 0.5) / CH)


def seg_parts(seg, info_ref):
    parts = []
    prefix = min(seg, TRUNK) * SEG
    if prefix:
        parts.append((0, prefix, 0, False))
    if seg >= TRUNK + BRANCHES:
        start = pl.multiple_of(info_ref[seg] * SEG, SEG)
        parts.append((start, SEG, TRUNK * SEG, False))
    parts.append((seg * SEG, SEG, (TRUNK + 1) * SEG, True))
    return parts


def unit_rows(rows_f32):
    factor = lax.rsqrt(jnp.mean(rows_f32 * rows_f32, axis=-1, keepdims=True) + EPSILON)
    return rows_f32 * factor * (1.0 / math.sqrt(DH)), factor


def own_diagonal():
    row = lax.broadcasted_iota(jnp.int32, (SEG, SEG), 0)
    col = lax.broadcasted_iota(jnp.int32, (SEG, SEG), 1)
    return row == col


def attention_forward_kernel(segments, rounds, info_ref, q_ref, v_ref, cq_ref, ck_ref, out_ref, total_ref, count_ref, unit_ref):
    head = pl.program_id(0)

    @pl.when(head == 0)
    def _():
        row = lax.broadcasted_iota(jnp.int32, (SEG, SEG), 0)
        col = lax.broadcasted_iota(jnp.int32, (SEG, SEG), 1)
        total_ref[...] = jnp.zeros_like(total_ref)
        for seg in range(segments):
            query = cq_ref[seg * SEG:(seg + 1) * SEG, :]
            for start, size, column, own in seg_parts(seg, info_ref):
                for piece in range(size // SEG):
                    first = start + piece * SEG
                    key = ck_ref[:, pl.ds(first, SEG)]
                    counted = jnp.zeros((SEG, SEG), F32)
                    for turn in range(rounds):
                        gap = query[:, turn:turn + 1] - key[turn:turn + 1, :]
                        counted = counted + jnp.where(jnp.abs(gap - 0.5) < 0.75, 1.0, 0.0)
                    if own:
                        counted = jnp.where(row >= col, counted, 0.0)
                    elif column == 0 and seg >= TRUNK:
                        counted = counted * jnp.where(info_ref[segments + seg] >= piece, 1.0, 0.0)
                    begin = column + piece * SEG
                    count_ref[seg * SEG:(seg + 1) * SEG, begin:begin + SEG] = counted.astype(BF)

    unit_ref[...] = unit_rows(q_ref[...].astype(F32))[0].astype(BF)
    diagonal = own_diagonal()
    lane = lax.broadcasted_iota(jnp.int32, (SEG, 128), 1)
    for seg in range(segments):
        rows = slice(seg * SEG, (seg + 1) * SEG)
        query = q_ref[rows, :]
        scored = []
        top = None
        for start, size, column, own in seg_parts(seg, info_ref):
            keys = pl.ds(start, size)
            scores = lax.dot_general(query, unit_ref[keys, :], (((1,), (1,)), ((), ())), preferred_element_type=F32)
            counted = count_ref[rows, column:column + size].astype(F32)
            if own:
                scores = jnp.where(diagonal, SELF_SCORE, scores)
            scores = jnp.where(counted > 0.0, scores, NEG_SCORE)
            best = jnp.max(scores, axis=-1, keepdims=True)
            top = best if top is None else jnp.maximum(top, best)
            scored.append((keys, scores, counted))
        amount = jnp.zeros((SEG, 1), F32)
        result = jnp.zeros((SEG, DH), F32)
        for keys, scores, counted in scored:
            weight = counted * jnp.exp(scores - top)
            amount = amount + jnp.sum(weight, axis=-1, keepdims=True)
            result = result + jnp.dot(weight.astype(BF), v_ref[keys, :], preferred_element_type=F32)
        out_ref[rows, :] = (result / amount).astype(BF)
        total = top + jnp.log(amount)
        total_ref[rows, :] = jnp.where(lane == head, total, total_ref[rows, :])


def attention_backward_kernel(segments, info_ref, q_ref, v_ref, out_ref, grad_ref, total_ref, count_ref, dq_ref, dv_ref, unit_ref, chance_ref, slope_ref, key_acc, value_acc, query_acc):
    head = pl.program_id(0)
    trunk = TRUNK * SEG
    whole = q_ref[...].astype(F32)
    unit, factor = unit_rows(whole)
    unit_ref[...] = unit.astype(BF)

    @pl.when(head == 0)
    def _():
        chance_ref[0:trunk, 0:trunk] = jnp.zeros((trunk, trunk), BF)
        slope_ref[0:trunk, 0:trunk] = jnp.zeros((trunk, trunk), BF)

    diagonal = own_diagonal()
    lane = lax.broadcasted_iota(jnp.int32, (SEG, 128), 1)
    for seg in range(segments):
        rows = slice(seg * SEG, (seg + 1) * SEG)
        query = q_ref[rows, :]
        grad = grad_ref[rows, :]
        total = jnp.sum(jnp.where(lane == head, total_ref[rows, :], 0.0), axis=-1, keepdims=True)
        delta = jnp.sum(grad.astype(F32) * out_ref[rows, :].astype(F32), axis=-1, keepdims=True)
        query_grad = jnp.zeros((SEG, DH), F32)
        for start, size, column, own in seg_parts(seg, info_ref):
            keys = pl.ds(start, size)
            scores = lax.dot_general(query, unit_ref[keys, :], (((1,), (1,)), ((), ())), preferred_element_type=F32)
            counted = count_ref[rows, column:column + size].astype(F32)
            if own:
                scores = jnp.where(diagonal, SELF_SCORE, scores)
            scores = jnp.where(counted > 0.0, scores, NEG_SCORE)
            chance = counted * jnp.exp(scores - total)
            reach = lax.dot_general(grad, v_ref[keys, :], (((1,), (1,)), ((), ())), preferred_element_type=F32)
            slope = chance * (reach - delta)
            if own:
                slope = jnp.where(diagonal, 0.0, slope)
            slope = slope.astype(BF)
            chance_ref[rows, column:column + size] = chance.astype(BF)
            slope_ref[rows, column:column + size] = slope
            query_grad = query_grad + jnp.dot(slope, unit_ref[keys, :], preferred_element_type=F32)
        query_acc[rows, :] = query_grad

    for weight_ref, side_ref, acc in ((chance_ref, grad_ref, value_acc), (slope_ref, q_ref, key_acc)):
        acc[0:trunk, :] = lax.dot_general(weight_ref[:, 0:trunk], side_ref[...], (((0,), (0,)), ((), ())), preferred_element_type=F32)
        for seg in range(segments):
            rows = slice(seg * SEG, (seg + 1) * SEG)
            leaf = seg >= TRUNK + BRANCHES
            begin = trunk if leaf else trunk + SEG
            added = lax.dot_general(weight_ref[rows, begin:trunk + 2 * SEG], side_ref[rows, :], (((0,), (0,)), ((), ())), preferred_element_type=F32)
            if leaf:
                above = pl.ds(pl.multiple_of(info_ref[seg] * SEG, SEG), SEG)
                acc[above, :] += added[0:SEG]
                added = added[SEG:]
            acc[rows, :] = added if seg >= TRUNK else acc[rows, :] + added

    key_grad = key_acc[...]
    along = jnp.mean(key_grad * whole, axis=-1, keepdims=True) * (factor * factor)
    dq_ref[...] = (query_acc[...] + (factor * (1.0 / math.sqrt(DH))) * (key_grad - whole * along)).astype(BF)
    dv_ref[...] = value_acc[...].astype(BF)


def attention_calls(tree_len, local_heads, rounds, segments):
    head_spec = pl.BlockSpec((tree_len, DH), lambda h, info: (0, h))
    side = pl.BlockSpec((tree_len, 128), lambda h, info: (0, 0))
    count_spec = pl.BlockSpec((tree_len, (TRUNK + 2) * SEG), lambda h, info: (0, 0))
    wide = local_heads * DH
    forward = pl.pallas_call(
        functools.partial(attention_forward_kernel, segments, rounds),
        grid_spec=pltpu.PrefetchScalarGridSpec(
            num_scalar_prefetch=1,
            grid=(local_heads,),
            in_specs=[head_spec, head_spec, side, pl.BlockSpec((8, tree_len), lambda h, info: (0, 0))],
            out_specs=[head_spec, side, count_spec],
            scratch_shapes=[pltpu.VMEM((tree_len, DH), BF)],
        ),
        out_shape=[
            jax.ShapeDtypeStruct((tree_len, wide), BF),
            jax.ShapeDtypeStruct((tree_len, 128), F32),
            jax.ShapeDtypeStruct((tree_len, (TRUNK + 2) * SEG), BF),
        ],
        compiler_params=pltpu.CompilerParams(vmem_limit_bytes=40 << 20),
        cost_estimate=cost(18),
        name="attention_forward",
    )
    backward = pl.pallas_call(
        functools.partial(attention_backward_kernel, segments),
        grid_spec=pltpu.PrefetchScalarGridSpec(
            num_scalar_prefetch=1,
            grid=(local_heads,),
            in_specs=[head_spec, head_spec, head_spec, head_spec, side, count_spec],
            out_specs=[head_spec, head_spec],
            scratch_shapes=[pltpu.VMEM((tree_len, DH), BF)]
            + [pltpu.VMEM((tree_len, (TRUNK + 2) * SEG), BF)] * 2
            + [pltpu.VMEM((tree_len, DH), F32)] * 3,
        ),
        out_shape=[jax.ShapeDtypeStruct((tree_len, wide), BF)] * 2,
        compiler_params=pltpu.CompilerParams(vmem_limit_bytes=40 << 20),
        cost_estimate=cost(21),
        name="attention_backward",
    )
    return forward, backward


def row_block(where_fn, coords_ref, span):
    return pl.ds(pl.multiple_of(where_fn(coords_ref) * span, span), span)


def piece_view(refs, piece):
    view = refs[piece[0]].at[piece[1]] if piece[1] else refs[piece[0]]
    if piece[2] is None:
        return view
    return view.at[pl.ds(piece[2][0], piece[3]), pl.ds(piece[2][1], piece[5][1])]


def whole_view(whole, coords_ref, piece):
    rows = row_block(piece[4], coords_ref, piece[3])
    first = piece[5][0]
    if callable(first):
        first = pl.multiple_of(first(coords_ref) * piece[5][1], piece[5][1])
    return whole.at[rows, pl.ds(first, piece[5][1])]


def load_pieces(coords_ref, refs, pieces, target, sems, first):
    return [
        pltpu.make_async_copy(piece_view(refs, piece), whole_view(target, coords_ref, piece), sems.at[first + number])
        for number, piece in enumerate(pieces)
    ]


def store_pieces(coords_ref, source, refs, pieces, sems, first):
    return [
        pltpu.make_async_copy(whole_view(source, coords_ref, piece), piece_view(refs, piece), sems.at[first + number])
        for number, piece in enumerate(pieces)
    ]


def project_kernel(q_pieces, v_pieces, q_count, v_count, parts, coords_ref, gain_ref, shift_ref, *refs):
    part_refs, refs = refs[:len(parts)], refs[len(parts):]
    q_refs, v_refs = refs[:q_count], refs[q_count:q_count + v_count]
    q_out, v_out, unit_ref, mixed_ref, q_weight, v_weight, sems = refs[q_count + v_count:]
    to_q = load_pieces(coords_ref, q_refs, q_pieces, q_weight, sems, 0)
    to_v = load_pieces(coords_ref, v_refs, v_pieces, v_weight, sems, len(q_pieces))
    for copy in to_q + to_v:
        copy.start()
    for part_ref, places in zip(part_refs, parts):
        for number, place in enumerate(places):
            unit = part_ref[number]
            rows = row_block(place, coords_ref, unit.shape[0])
            unit_ref[rows, :] = unit
            mixed_ref[rows, :] = (unit.astype(F32) * gain_ref[...] + shift_ref[...]).astype(BF)
    for copy in to_q:
        copy.wait()
    q_out[...] = jnp.dot(mixed_ref[...], q_weight[...], preferred_element_type=F32).astype(BF)
    for copy in to_v:
        copy.wait()
    v_out[...] = jnp.dot(mixed_ref[...], v_weight[...], preferred_element_type=F32).astype(BF)


VM = pl.BlockSpec(memory_space=pltpu.VMEM)
ANYWHERE = pl.BlockSpec(memory_space=pl.ANY)


def cost(micros):
    return pl.CostEstimate(flops=int(micros * 1e7), transcendentals=0, bytes_accessed=0)


def kernel_call(body, ins, outs, scratch, name, limit, micros, grid=()):
    return pl.pallas_call(
        body,
        grid_spec=pltpu.PrefetchScalarGridSpec(num_scalar_prefetch=1, grid=grid, in_specs=ins, out_specs=outs[0], scratch_shapes=scratch),
        out_shape=outs[1],
        compiler_params=pltpu.CompilerParams(vmem_limit_bytes=limit << 20),
        cost_estimate=cost(micros),
        name=name,
    )


def project(coords, row_parts, places, gain, shift, q_side, v_side, wide):
    q_arrays, q_pieces = q_side
    v_arrays, v_pieces = v_side
    rows, features = sum(part.shape[0] * part.shape[1] for part in row_parts), gain.shape[1]
    body = functools.partial(project_kernel, q_pieces, v_pieces, len(q_arrays), len(v_arrays), places)
    return kernel_call(
        body,
        [VM] * (2 + len(row_parts)) + [ANYWHERE] * (len(q_arrays) + len(v_arrays)),
        ([VM] * 4, [jax.ShapeDtypeStruct((rows, wide), BF)] * 2 + [jax.ShapeDtypeStruct((rows, features), BF)] * 2),
        [pltpu.VMEM((features, wide), BF)] * 2 + [pltpu.SemaphoreType.DMA((len(q_pieces) + len(v_pieces),))],
        "project",
        50,
        7,
    )(coords, gain, shift, *row_parts, *q_arrays, *v_arrays)


def project_back_kernel(q_pieces, v_pieces, q_count, v_count, q_outs, v_outs, q_made, v_made, coords_ref, mixed_ref, unit_ref, dq_ref, dv_ref, *refs):
    q_refs, v_refs = refs[:q_count], refs[q_count:q_count + v_count]
    rest = refs[q_count + v_count:]
    partial_ref, gain_sum, shift_sum = rest[:3]
    rest = rest[3:]
    q_grads, v_grads = rest[:q_made], rest[q_made:q_made + v_made]
    q_weight, v_weight, q_sum, v_sum, sems = rest[q_made + v_made:]
    to_q = load_pieces(coords_ref, q_refs, q_pieces, q_weight, sems, 0)
    to_v = load_pieces(coords_ref, v_refs, v_pieces, v_weight, sems, len(q_pieces))
    for copy in to_q + to_v:
        copy.start()
    used = len(q_pieces) + len(v_pieces)
    turned = (((0,), (0,)), ((), ()))
    crossed = (((1,), (1,)), ((), ()))
    q_sum[...] = lax.dot_general(mixed_ref[...], dq_ref[...], turned, preferred_element_type=F32).astype(BF)
    from_q = store_pieces(coords_ref, q_sum, q_grads, q_outs, sems, used)
    for copy in from_q:
        copy.start()
    v_sum[...] = lax.dot_general(mixed_ref[...], dv_ref[...], turned, preferred_element_type=F32).astype(BF)
    from_v = store_pieces(coords_ref, v_sum, v_grads, v_outs, sems, used + len(q_outs))
    for copy in from_v:
        copy.start()
    for copy in to_q + to_v:
        copy.wait()
    partial = lax.dot_general(dq_ref[...], q_weight[...], crossed, preferred_element_type=F32) + lax.dot_general(
        dv_ref[...], v_weight[...], crossed, preferred_element_type=F32
    )
    partial_ref[...] = partial.astype(BF)
    gain_sum[...] = jnp.sum(partial * unit_ref[...].astype(F32), axis=0, keepdims=True)
    shift_sum[...] = jnp.sum(partial, axis=0, keepdims=True)
    for copy in from_q + from_v:
        copy.wait()


def project_back(coords, mixed_tree, unit_tree, dq, dv, q_side, v_side, q_form, v_form):
    q_arrays, q_pieces = q_side
    v_arrays, v_pieces = v_side
    q_shapes, q_outs = q_form
    v_shapes, v_outs = v_form
    rows, features = mixed_tree.shape
    wide = dq.shape[1]
    body = functools.partial(
        project_back_kernel, q_pieces, v_pieces, len(q_arrays), len(v_arrays), q_outs, v_outs, len(q_shapes), len(v_shapes)
    )
    made = kernel_call(
        body,
        [VM] * 4 + [ANYWHERE] * (len(q_arrays) + len(v_arrays)),
        (
            [VM] * 3 + [ANYWHERE] * (len(q_shapes) + len(v_shapes)),
            [jax.ShapeDtypeStruct((rows, features), BF)]
            + [jax.ShapeDtypeStruct((1, features), F32)] * 2
            + [jax.ShapeDtypeStruct(s, BF) for s in q_shapes + v_shapes],
        ),
        [pltpu.VMEM((features, wide), BF)] * 4
        + [pltpu.SemaphoreType.DMA((len(q_pieces) + len(v_pieces) + len(q_outs) + len(v_outs),))],
        "project_back",
        50,
        18,
    )(coords, mixed_tree, unit_tree, dq, dv, *q_arrays, *v_arrays)
    return made[:3], made[3:3 + len(q_shapes)], made[3 + len(q_shapes):]


def normalised(values):
    center = values - jnp.mean(values, axis=-1, keepdims=True)
    factor = lax.rsqrt(jnp.mean(center * center, axis=-1, keepdims=True) + EPSILON)
    return center * factor, factor


def out_kernel(pieces, count, coords_ref, att_ref, first_ref, gain_ref, shift_ref, *refs):
    o_refs = refs[:count]
    first_out, feed_out, weight, sems = refs[count:]
    copies = load_pieces(coords_ref, o_refs, pieces, weight, sems, 0)
    for copy in copies:
        copy.start()
    for copy in copies:
        copy.wait()
    made = first_ref[...] + jnp.dot(att_ref[...], weight[...], preferred_element_type=F32)
    first_out[...] = made
    feed_out[...] = (normalised(made)[0] * gain_ref[...] + shift_ref[...]).astype(BF)


def out_project(coords, att, first, gain, shift, side):
    arrays, pieces = side
    rows, features = first.shape
    return kernel_call(
        functools.partial(out_kernel, pieces, len(arrays)),
        [VM] * 4 + [ANYWHERE] * len(arrays),
        ([VM, VM], [jax.ShapeDtypeStruct((rows, features), F32), jax.ShapeDtypeStruct((rows, features), BF)]),
        [pltpu.VMEM((features, features), BF), pltpu.SemaphoreType.DMA((len(pieces),))],
        "out_project",
        50,
        8,
    )(coords, att, first, gain, shift, *arrays)


def out_back_kernel(pieces, count, outs, made, coords_ref, back_ref, first_ref, grad_ref, att_ref, gain_ref, *refs):
    o_refs = refs[:count]
    rest = refs[count:]
    grad_in, grad_att, gain_sum, shift_sum = rest[:4]
    grads = rest[4:4 + made]
    weight, total, sems = rest[4 + made:]
    copies = load_pieces(coords_ref, o_refs, pieces, weight, sems, 0)
    for copy in copies:
        copy.start()
    back = back_ref[...]
    unit, factor = normalised(first_ref[...])
    gain_sum[...] = jnp.sum(back * unit, axis=0, keepdims=True)
    shift_sum[...] = jnp.sum(back, axis=0, keepdims=True)
    scaled = back * gain_ref[...]
    inner = jnp.mean(scaled * unit, axis=-1, keepdims=True)
    value = grad_ref[...] + factor * (scaled - jnp.mean(scaled, axis=-1, keepdims=True) - unit * inner)
    grad_in[...] = value
    low = value.astype(BF)
    total[...] = lax.dot_general(att_ref[...], low, (((0,), (0,)), ((), ())), preferred_element_type=F32).astype(BF)
    stores = store_pieces(coords_ref, total, grads, outs, sems, len(pieces))
    for copy in stores:
        copy.start()
    for copy in copies:
        copy.wait()
    grad_att[...] = lax.dot_general(low, weight[...], (((1,), (1,)), ((), ())), preferred_element_type=F32).astype(BF)
    for copy in stores:
        copy.wait()


def out_back(coords, back, first_out, grad, att, gain, side, form):
    arrays, pieces = side
    shapes, outs = form
    rows, features = back.shape
    full = jax.ShapeDtypeStruct((rows, features), F32)
    line = jax.ShapeDtypeStruct((1, features), F32)
    made = kernel_call(
        functools.partial(out_back_kernel, pieces, len(arrays), outs, len(shapes)),
        [VM] * 5 + [ANYWHERE] * len(arrays),
        (
            [VM] * 4 + [ANYWHERE] * len(shapes),
            [full, jax.ShapeDtypeStruct((rows, features), BF), line, line] + [jax.ShapeDtypeStruct(s, BF) for s in shapes],
        ),
        [pltpu.VMEM((features, features), BF)] * 2 + [pltpu.SemaphoreType.DMA((len(pieces) + len(outs),))],
        "out_back",
        60,
        12,
    )(coords, back, first_out, grad, att, gain, *arrays)
    return made[:4], made[4:]


def feed_in_kernel(plan, counts, coords_ref, feed_ref, grad_ref, bias_ref, *refs):
    pieces, step_outs, block_of = plan
    i_count, made = counts
    i_refs = refs[:i_count]
    active_ref, slope_ref = refs[i_count:i_count + 2]
    grads = refs[i_count + 2:i_count + 2 + made]
    weight, outer_sum, in_sems, out_sems = refs[i_count + 2 + made:]
    step = pl.program_id(0)
    slot = lax.rem(step, 2)
    tile = outer_sum.shape[1]
    count = len(step_outs)

    def store(number):
        return store_pieces(coords_ref, outer_sum.at[number % 2], grads, step_outs[number], out_sems.at[number % 2], 0)

    @pl.when(step == 0)
    def _():
        copies = load_pieces(coords_ref, i_refs, pieces, weight, in_sems, 0)
        for copy in copies:
            copy.start()
        for copy in copies:
            copy.wait()

    for number in range(2, count):

        @pl.when(step == number)
        def _(number=number):
            for copy in store(number - 2):
                copy.wait()

    columns = pl.ds(pl.multiple_of(block_of(step, coords_ref) * tile, tile), tile)
    value = jnp.dot(feed_ref[...], weight[:, columns], preferred_element_type=F32) + bias_ref[:, columns]
    square = value * value
    half = 0.5 + 0.5 * jnp.tanh(value * (GELU_A + GELU_A * GELU_B * square))
    product = value * half
    active = product.astype(BF)
    active_ref[...] = active
    slope_ref[...] = (half + product * (1.0 - half) * (2.0 * GELU_A + 6.0 * GELU_A * GELU_B * square)).astype(BF)
    outer_sum[slot] = lax.dot_general(active, grad_ref[...], (((0,), (0,)), ((), ())), preferred_element_type=F32).astype(BF)

    for number in range(count):

        @pl.when(step == number)
        def _(number=number):
            for copy in store(number):
                copy.start()
            if number == count - 1:
                for last in range(max(0, number - 1), count):
                    for copy in store(last):
                        copy.wait()


def feed_in(coords, feed, grad, bias, side, form, block_of):
    arrays, pieces = side
    shapes, step_outs = form
    rows, features = feed.shape
    hidden = bias.shape[1]
    tile = hidden // len(step_outs)
    most = max(len(outs) for outs in step_outs)
    block = pl.BlockSpec((rows, tile), lambda j, co: (0, block_of(j, co)))
    made = kernel_call(
        functools.partial(feed_in_kernel, (pieces, step_outs, block_of), (len(arrays), len(shapes))),
        [VM] * 3 + [ANYWHERE] * len(arrays),
        (
            [block, block] + [ANYWHERE] * len(shapes),
            [jax.ShapeDtypeStruct((rows, hidden), BF)] * 2 + [jax.ShapeDtypeStruct(s, BF) for s in shapes],
        ),
        [
            pltpu.VMEM((features, hidden), BF),
            pltpu.VMEM((2, tile, features), BF),
            pltpu.SemaphoreType.DMA((len(pieces),)),
            pltpu.SemaphoreType.DMA((2, most)),
        ],
        "feed_in",
        60,
        29,
        grid=(len(step_outs),),
    )(coords, feed, grad, bias, *arrays)
    return made[0], made[1], made[2:]


def feed_out_kernel(plan, counts, coords_ref, feed_ref, grad_ref, base_ref, bias_ref, active_ref, slope_ref, *refs):
    i_pieces, i_outs, steps, block_of = plan
    i_count, u_count, made = counts
    i_refs, u_refs = refs[:i_count], refs[i_count:i_count + u_count]
    rest = refs[i_count + u_count:]
    out_ref, back_ref, bias_sum = rest[:3]
    grads = rest[3:3 + made]
    weight, weight_sum, outer, low_ref, i_sems, u_sems, out_sems = rest[3 + made:]
    step = pl.program_id(0)
    slot = lax.rem(step, 2)
    tile = outer.shape[1]
    count = len(steps)

    def u_load(number):
        return load_pieces(coords_ref, u_refs, steps[number], outer.at[number % 2], u_sems.at[number % 2], 0)

    @pl.when(step == 0)
    def _():
        copies = load_pieces(coords_ref, i_refs, i_pieces, weight, i_sems, 0)
        for copy in u_load(0) + copies:
            copy.start()
        out_ref[...] = base_ref[...] + bias_ref[...]
        back_ref[...] = jnp.zeros_like(back_ref)
        for copy in copies:
            copy.wait()

    for number in range(count):

        @pl.when(step == number)
        def _(number=number):
            if number + 1 < count:
                for copy in u_load(number + 1):
                    copy.start()
            for copy in u_load(number):
                copy.wait()

    columns = pl.ds(pl.multiple_of(block_of(step, coords_ref) * tile, tile), tile)
    pulled = lax.dot_general(grad_ref[...], outer[slot], (((1,), (1,)), ((), ())), preferred_element_type=F32)
    inner_low = (pulled * slope_ref[...].astype(F32)).astype(BF)
    bias_sum[:, columns] = jnp.sum(inner_low.astype(F32), axis=0, keepdims=True)
    weight_sum[:, columns] = lax.dot_general(feed_ref[...], inner_low, (((0,), (0,)), ((), ())), preferred_element_type=F32).astype(BF)
    low_ref[...] = inner_low
    out_ref[...] += jnp.dot(active_ref[...], outer[slot], preferred_element_type=F32)
    back_ref[...] += lax.dot_general(low_ref[...], weight[:, columns], (((1,), (1,)), ((), ())), preferred_element_type=F32)

    @pl.when(step == count - 1)
    def _():
        copies = store_pieces(coords_ref, weight_sum, grads, i_outs, out_sems, 0)
        for copy in copies:
            copy.start()
        for copy in copies:
            copy.wait()


def feed_out(coords, feed, grad, base, bias, active, slope, i_side, u_side, i_form, block_of):
    i_arrays, i_pieces = i_side
    u_arrays, steps = u_side
    shapes, i_outs = i_form
    rows, features = feed.shape
    hidden = active.shape[1]
    tile = hidden // len(steps)
    most = max(len(pieces) for pieces in steps)
    block = pl.BlockSpec((rows, tile), lambda j, co: (0, block_of(j, co)))
    made = kernel_call(
        functools.partial(feed_out_kernel, (i_pieces, i_outs, steps, block_of), (len(i_arrays), len(u_arrays), len(shapes))),
        [VM] * 4 + [block, block] + [ANYWHERE] * (len(i_arrays) + len(u_arrays)),
        (
            [VM] * 3 + [ANYWHERE] * len(shapes),
            [jax.ShapeDtypeStruct((rows, features), F32)] * 2
            + [jax.ShapeDtypeStruct((1, hidden), F32)]
            + [jax.ShapeDtypeStruct(s, BF) for s in shapes],
        ),
        [
            pltpu.VMEM((features, hidden), BF),
            pltpu.VMEM((features, hidden), BF),
            pltpu.VMEM((2, tile, features), BF),
            pltpu.VMEM((rows, tile), BF),
            pltpu.SemaphoreType.DMA((len(i_pieces),)),
            pltpu.SemaphoreType.DMA((2, most)),
            pltpu.SemaphoreType.DMA((len(i_outs),)),
        ],
        "feed_out",
        60,
        40,
        grid=(len(steps),),
    )(coords, feed, grad, base, bias, active, slope, *i_arrays, *u_arrays)
    return made[0], made[1], made[2], made[3:]


def pick(flag, when_true, when_false):
    return jnp.where(flag, when_true, when_false)


def after(value, *earlier):
    return lax.optimization_barrier((value,) + earlier)[0]


class GroupPlan:
    def __init__(self, size, trees):
        me = lax.axis_index("fsdp")
        self.size = size
        self.trees = trees
        self.group = size // trees
        self.tree = me // self.group
        self.head_group = me % self.group
        self.me = me

    def rows_to_tree(self, rows):
        every = lax.all_gather(rows, "fsdp", axis=1, tiled=True)
        return lax.dynamic_index_in_dim(every, self.tree, 0, False)

    def heads_to_rows(self, heads):
        count = heads.shape[0] // self.size
        every = lax.all_gather(heads, "fsdp", axis=0, tiled=False)
        mine = lax.dynamic_slice_in_dim(every, self.me * count, count, 1)
        mine = mine.reshape(self.trees, self.group, count, heads.shape[1])
        return jnp.moveaxis(mine, 1, 2).reshape(self.trees, count, -1)

    def rows_to_heads(self, rows):
        wide = rows.shape[2] // self.group
        whole = self.rows_to_tree(rows)
        return lax.dynamic_slice_in_dim(whole, self.head_group * wide, wide, 1)

    def partial_to_rows(self, partial):
        every = jnp.zeros((self.trees,) + partial.shape, F32)
        every = lax.dynamic_update_index_in_dim(every, partial.astype(F32), self.tree, 0)
        return lax.psum_scatter(every, "fsdp", scatter_dimension=1, tiled=True)


def low(value):
    return value.astype(BF)


def wide_of(value):
    return value.astype(F32)


def swap_pairs(size, bit):
    return [(i, i ^ bit) for i in range(size)]


def natural(rows, columns):
    return [(0, (), None, rows, (lambda co: co[0] * 0), (0, columns))]


def swap_pairs(size, bit):
    return [(i, i ^ bit) for i in range(size)]


def core(value):
    return lax.ppermute(value, "fsdp", swap_pairs(4, 1))


def over_y(value):
    return lax.ppermute(value, "fsdp", swap_pairs(4, 2))


def over_x(value):
    return lax.ppermute(value, "dp", swap_pairs(8, 1))


def up_z(value):
    return lax.ppermute(value, "dp", [(i, (i + 2) % 8) for i in range(8)])


def bit_move(bit, value):
    if bit < 2:
        return lax.ppermute(value, "fsdp", swap_pairs(4, 1 << bit))
    return lax.ppermute(value, "dp", swap_pairs(8, 1 << (bit - 2)))


def place32(k, rx, ry, rc):
    return lambda co: ((((co[0] + 4 - k) & 3) * 2 + (co[1] ^ rx)) * 2 + (co[2] ^ ry)) * 2 + (co[3] ^ rc)


def place16(k, rx, ry):
    return lambda co: (((co[0] + 4 - k) & 3) * 2 + (co[1] ^ rx)) * 2 + (co[2] ^ ry)


def place8(rx, ry, rc):
    return lambda co: ((co[1] ^ rx) * 2 + (co[2] ^ ry)) * 2 + (co[3] ^ rc)


def hidden_block(step, co):
    return (co[0] + 4 - step) & 3


def heads_pieces(which, rows, half):
    pieces = []
    for outer in range(2):
        for inner in range(2):
            for k in range(4):
                rx, ry = (outer, inner) if which == 0 else (inner, outer)
                pieces.append((outer, (inner, k), None, rows, place16(k, rx, ry), (0, half)))
    return pieces


def output_in_pieces(rows, half):
    pieces = []
    for rc in range(2):
        for rx in range(2):
            for ry in range(2):
                for k in range(4):
                    columns = ((lambda co, rc=rc: co[3] ^ rc), half)
                    pieces.append((rc * 2 + rx, (ry, k), None, rows, place16(k, rx, ry), columns))
    return pieces


def output_out_pieces(count, features):
    pieces = []
    for rc in range(2):
        for ry in range(2):
            for rx in range(2):
                for k in range(4):
                    pieces.append((rc * 2 + ry, (rx, k), None, count, place32(k, rx, ry, rc), (0, features)))
    return pieces


def inner_pieces(count, hidden, cut):
    pieces = []
    for part in range(2):
        for rc in range(2):
            for outer in range(2):
                for inner in range(2):
                    for k in range(4):
                        rx, ry = (outer, inner) if part == 0 else (inner, outer)
                        columns = (0, cut) if part == 0 else (cut, hidden - cut)
                        pieces.append((rc * 4 + part * 2 + outer, (inner, k), None, count, place32(k, rx, ry, rc), columns))
    return pieces


def outer_steps(count, features):
    return [
        [
            (rc * 4 + k, (rx, ry), None, count, place8(rx, ry, rc), (0, features))
            for rx in range(2)
            for ry in range(2)
            for rc in range(2)
        ]
        for k in range(4)
    ]


def together(*values):
    return lax.optimization_barrier(values)


def join_vectors(parts):
    total = sum(part.shape[0] for part in parts)
    made, begin = 0.0, 0
    for part in parts:
        made = made + jnp.pad(wide_of(part), (begin, total - begin - part.shape[0]))
        begin += part.shape[0]
    return low(made)


def per_device(
    first_half,
    second_half,
    grad_first,
    grad_second,
    query_weight,
    value_weight,
    output_weight,
    inner_weight,
    inner_bias,
    outer_weight,
    outer_bias,
    mixer_gain,
    mixer_shift,
    feed_gain,
    feed_shift,
    parents,
    buckets,
    order,
    *,
    dp_size,
    fsdp_size,
):
    trees = first_half.shape[0]
    row_count = first_half.shape[2]
    features = first_half.shape[3]
    hidden = inner_weight.shape[1]
    rounds = buckets.shape[2]
    tree_len = buckets.shape[3]
    segments = parents.shape[2]
    all_rows = trees * row_count
    devices = dp_size * fsdp_size
    small_parts = (inner_bias, outer_bias, mixer_gain, mixer_shift, feed_gain, feed_shift)
    small_sizes = [v.shape[0] for v in small_parts]
    small_count = sum(small_sizes)

    first = first_half[:, 0]
    second = second_half[:, 0]
    grad_b = grad_second[:, 0]
    joined = join_vectors(small_parts)[None]

    def flat(value):
        return value.reshape(all_rows, features)

    def split(small):
        vectors, begin = [], 0
        for size in small_sizes:
            vectors.append(small[:, begin:begin + size].reshape(1, -1))
            begin += size
        return vectors

    def tables(tree, *earlier):
        parent_row = lax.dynamic_index_in_dim(after(parents, *earlier)[:, 0], tree, 0, False)
        bucket_rows = lax.dynamic_index_in_dim(after(buckets, *earlier)[:, 0], tree, 0, False)
        branch = parent_row[jnp.clip(parent_row, 0, segments - 1)]
        trunk_end = jnp.where(jnp.arange(segments) >= TRUNK + BRANCHES, branch, parent_row)
        codes = position_codes(bucket_rows)
        return (
            jnp.concatenate([parent_row, trunk_end]),
            jnp.pad(codes, ((0, 0), (0, 128 - rounds))),
            jnp.pad(codes.T, ((0, 8 - rounds), (0, 0))),
        )

    local_heads = H // (fsdp_size // trees)
    wide = local_heads * DH
    attend, attend_back = attention_calls(tree_len, local_heads, rounds, segments)
    outer_low = flat(low(grad_b))
    outer_bias_sum = jnp.sum(wide_of(outer_low), axis=0)

    if (dp_size, fsdp_size, trees) == (8, 4, 2):
        dp, fsdp = lax.axis_index("dp"), lax.axis_index("fsdp")
        bits = [fsdp % 2, fsdp // 2, dp % 2, dp // 2 % 2, dp // 4]
        coords = jnp.stack([dp // 2, dp % 2, fsdp // 2, fsdp % 2]).astype(jnp.int32)
        odd, upper, tree = fsdp % 2 == 1, fsdp // 2 == 1, fsdp // 2
        count, half, cut = query_weight.shape[0], features // 2, hidden * 11 // 16
        outer_count = outer_weight.shape[0]

        def order(flag, one, other, axis=0, join=jnp.stack):
            return join([pick(flag, other, one), pick(flag, one, other)], axis=axis)

        def small_step(bit, made):
            return order(bits[bit] == 1, made, bit_move(bit, made), 0, jnp.concatenate)

        both = jnp.stack([query_weight, value_weight, output_weight])
        got, small_got = together(core(pick(odd, both[:, :, :half], both[:, :, half:])), bit_move(0, joined))
        chip = order(odd, pick(odd, both[:, :, half:], both[:, :, :half]), got, 1, jnp.concatenate)
        small = order(odd, joined, small_got, 0, jnp.concatenate)
        mix_unit, mix_factor = norm_stats(after(second, chip))
        ring_got, small, unit_low = together(up_z(chip), small_step(1, small), low(mix_unit))
        ring = [chip, ring_got]
        rows_mine = pick(upper, unit_low[1], unit_low[0])
        rows_got = over_y(pick(upper, unit_low[0], unit_low[1]))
        u_near = jnp.stack([outer_weight, over_y(after(outer_weight, chip))])
        ring_got, small = together(up_z(ring_got), small_step(3, small_step(2, small)))
        ring.append(ring_got)
        u_got = over_x(u_near)
        ring_got, small, u_got, rows_got = together(up_z(ring_got), small_step(4, small), u_got, rows_got)
        ring.append(ring_got)
        q_near, v_near = (jnp.stack([r[which] for r in ring]) for which in range(2))
        i_got = up_z(after(inner_weight, ring_got))
        pair = order(upper, rows_mine, rows_got)
        q_got, v_got, pair_got = together(over_y(q_near), over_x(v_near), core(pair))
        i_ring = [inner_weight, i_got]
        q_near, v_near = jnp.stack([q_near, q_got]), jnp.stack([v_near, v_got])
        info, codes_q, codes_k = tables(tree, pair_got)
        bias_inner, bias_outer, gain_mix, shift_mix, gain_feed, shift_feed = split(wide_of(small))
        o_near = jnp.stack([r[2] for r in ring[:3]] + [after(ring[3], pair_got)[2]])
        u_plane = jnp.stack([u_near, after(u_got, pair_got)])
        q_got, v_got, i_got, codes_q, codes_k, o_near, u_plane = together(
            over_x(q_near), over_y(v_near), up_z(after(i_got, pair_got)), codes_q, codes_k, o_near, u_plane
        )
        i_ring.append(i_got)
        q_side = ([q_near, q_got], heads_pieces(0, 2 * count, half))
        v_side = ([v_near, v_got], heads_pieces(1, 2 * count, half))

        places = [[(lambda co, y=y, rc=rc: 2 * y + (co[3] ^ rc)) for y in range(2)] for rc in range(2)]
        made = project(coords, [pair, pair_got], places, gain_mix, shift_mix, q_side, v_side, wide)
        query_key, value_rows, unit_tree, mixed_tree, i_got, o_got = together(*made, up_z(i_got), over_y(o_near))
        i_ring.append(i_got)
        u_ring = [u_plane, up_z(after(u_plane, i_got))]

        a_near = jnp.stack([r[:, :cut] for r in i_ring])
        b_near = jnp.stack([r[:, cut:] for r in i_ring])
        o_near = jnp.stack([o_near, o_got])
        attended, totals, counts = attend(info, query_key, value_rows, codes_q, codes_k)
        attended, totals, counts, a_got, b_got, o_got, u_got = together(
            attended, totals, counts, over_y(a_near), over_x(b_near), over_x(o_near), u_ring[1]
        )
        u_ring[1] = u_got
        blocks = attended.reshape(2, 2, row_count, wide)
        got = core(pick(odd, blocks[:, 0], blocks[:, 1]))
        heads = order(odd, pick(odd, blocks[:, 1], blocks[:, 0]), got, 2, jnp.concatenate)
        mine, other = pick(upper, heads[1], heads[0]), pick(upper, heads[0], heads[1])
        mine, other = together(mine, other)
        a_near = jnp.stack([a_near, after(a_got, other)])
        a_got = over_x(a_near)
        b_near = jnp.stack([b_near, after(b_got, other)])
        u_next = up_z(after(u_got, other))
        got, o_core, o_core_got = together(over_y(other), core(o_near), core(o_got))
        attended_low = flat(order(upper, mine, got))
        o_side = ([o_near, o_got, o_core, o_core_got], output_in_pieces(2 * count, half))

        b_got = over_y(after(b_near, got))
        first_out, feed_low = out_project(coords, attended_low, flat(first), gain_feed, shift_feed, o_side)
        first_out, feed_low, a_got, b_got, a_core, b_core, u_got = together(
            first_out, feed_low, a_got, b_got, core(a_near), core(b_near), u_next
        )
        feed_low, a_core_got, b_core_got = together(feed_low, core(a_got), core(b_got))
        i_side = (
            [a_near, a_got, b_near, b_got, a_core, a_core_got, b_core, b_core_got],
            inner_pieces(count, hidden, cut),
        )
        u_ring += [u_got, up_z(u_got)]

        u_form = ([(2, 2, outer_count, features)] * 8, outer_steps(outer_count, features))
        active, slope, u_parts = feed_in(coords, feed_low, outer_low, bias_inner, i_side, u_form, hidden_block)
        u_cores = [core(u) for u in u_ring[:3]]
        made = together(active, slope, u_ring[3], *u_cores, *u_parts)
        active, slope, u_ring[3] = made[:3]
        u_cores, u_parts = list(made[3:6]), made[6:]
        sent = low(wide_of(u_parts[1]) + wide_of(core(u_parts[5])))
        sent, u_core, active = together(sent, core(u_ring[3]), active)
        u_side = (u_ring + u_cores + [u_core], outer_steps(outer_count, features))

        i_form = (([(2, 4, count, cut)] * 2 + [(2, 4, count, hidden - cut)] * 2) * 2, inner_pieces(count, hidden, cut))
        second_out, grad_feed, inner_bias_sum, i_parts = feed_out(
            coords, feed_low, outer_low, flat(second), bias_outer, active, slope, i_side, u_side, i_form, hidden_block
        )
        made = together(second_out, grad_feed, inner_bias_sum, up_z(sent), *[core(u_parts[4 + k]) for k in (2, 3, 0)], *i_parts)
        second_out, grad_feed, inner_bias_sum, u_got = made[:4]
        u_shares = [wide_of(u_parts[k]) + wide_of(c) for k, c in zip((2, 3, 0), made[4:7])]
        i_parts = made[7:]
        sent = low(wide_of(u_got) + u_shares[0])
        sent, grad_feed = together(sent, grad_feed)
        u_first = up_z(sent[0])
        o_form = ([(2, 4, count, features)] * 4, output_out_pieces(count, features))
        (grad_first_in, grad_attended, feed_gain_sum, feed_shift_sum), o_parts = out_back(
            coords, grad_feed, first_out, flat(grad_first), attended_low, gain_feed, o_side, o_form
        )
        made = together(grad_first_in, grad_attended, u_first, *[core(part) for part in i_parts[4:]], *o_parts)
        grad_first_in, grad_attended, u_first = made[:3]
        i_cores, o_parts = made[3:7], made[7:]
        a_keep, a_sent = (wide_of(i_parts[which]) + wide_of(i_cores[which]) for which in range(2))
        rows = grad_attended.reshape(trees, row_count, features)
        mine, other = together(pick(upper, rows[1], rows[0]), pick(upper, rows[0], rows[1]))
        a_got = over_x(after(low(a_sent), other))
        got, u_second = together(over_y(other), up_z(after(sent, other)[1]))
        pair = order(upper, mine, got)
        got = core(pick(odd, pair[..., :half], pair[..., half:]))
        grad_heads = order(odd, pick(odd, pair[..., half:], pair[..., :half]), got, 1).reshape(tree_len, half)
        grad_heads, o_core, o_core_sent = together(grad_heads, core(after(o_parts[2], pair)), core(after(o_parts[3], pair)))
        u_got = jnp.stack([u_first, u_second])
        small_sums = [inner_bias_sum, outer_bias_sum, None, None, feed_gain_sum, feed_shift_sum]

        def spread(values):
            made, begin = 0.0, 0
            for size, value in zip(small_sizes, values):
                if value is not None:
                    made = made + jnp.pad(value.reshape(devices, size), ((0, 0), (begin, small_count - begin - size)))
                begin += size
            return made

        small = spread(small_sums)
        b_keep, b_sent = (
            jnp.concatenate([wide_of(i_parts[2 + w]) + wide_of(i_cores[2 + w]), wide_of(o_parts[w]) + wide_of(c)], axis=3)
            for w, c in ((0, o_core), (1, o_core_sent))
        )

        sent, b_sent, grad_heads, small = together(low(wide_of(u_got) + u_shares[1]), low(b_sent), grad_heads, small)
        query_low, value_low = attend_back(info, query_key, value_rows, attended, grad_heads, totals, counts)
        query_low, value_low, u_got, a_got, b_got = together(query_low, value_low, up_z(sent), a_got, over_y(b_sent))
        a_keep, b_keep = a_keep + wide_of(a_got), b_keep + wide_of(b_got)
        a_sent, b_sent, query_low = together(low(a_keep[1]), low(b_keep[1]), query_low)
        q_form = ([(2, 4, 2 * count, half)] * 2, heads_pieces(0, 2 * count, half))
        v_form = ([(2, 4, 2 * count, half)] * 2, heads_pieces(1, 2 * count, half))
        (partial, mix_gain_sum, mix_shift_sum), q_parts, v_parts = project_back(
            coords, mixed_tree, unit_tree, query_low, value_low, q_side, v_side, q_form, v_form
        )
        made = together(partial, mix_gain_sum, mix_shift_sum, over_y(a_sent), over_x(b_sent), *q_parts, *v_parts)
        partial, mix_gain_sum, mix_shift_sum, a_got, b_got, q_keep, q_sent, v_keep, v_sent = made

        small = small + spread([None, None, mix_gain_sum, mix_shift_sum, None, None])

        def small_sum(bit, made, axis=0):
            one = bits[bit] == 1
            if axis:
                pairs = made.reshape(2, 2, -1, made.shape[-1])
                lower, higher = pairs[:, 0].reshape(-1, made.shape[-1]), pairs[:, 1].reshape(-1, made.shape[-1])
            else:
                middle = made.shape[0] // 2
                lower, higher = made[:middle], made[middle:]
            return pick(one, higher, lower) + bit_move(bit, pick(one, lower, higher))

        i_sum = jnp.concatenate([a_keep[0] + wide_of(a_got), b_keep[0] + wide_of(b_got)], axis=2)
        q_got, v_got, i_got, small = together(over_x(q_sent), over_y(v_sent), up_z(low(i_sum[1])), small_sum(4, small))
        u_sum = wide_of(after(u_got, q_got)) + u_shares[2]
        u_got = over_x(low(u_sum[1]))
        q_sum, v_sum = wide_of(q_keep) + wide_of(q_got), wide_of(v_keep) + wide_of(v_got)
        i_total = wide_of(i_got) + i_sum[2]
        blocks = partial.reshape(2, 2, row_count, features)
        got = core(pick(odd, blocks[:, 0], blocks[:, 1]))
        q_got, v_got, i_got, small, got = together(
            over_y(low(q_sum[1])), over_x(low(v_sum[1])), up_z(low(i_total)), small_sum(3, small), got
        )
        shared = low(wide_of(pick(odd, blocks[:, 1], blocks[:, 0])) + wide_of(got))
        h_sum = jnp.stack([q_sum[0] + wide_of(q_got), v_sum[0] + wide_of(v_got)], axis=1)
        i_total = wide_of(i_got) + i_sum[3]
        rows_got = over_y(pick(upper, shared[0], shared[1]))
        h_got, i_got, small, u_got = together(up_z(low(h_sum[1])), up_z(low(i_total)), small_sum(1, small, 1), u_got)
        u_sum = u_sum[0] + wide_of(u_got)
        u_got = over_y(low(u_sum[1]))
        h_total = wide_of(h_got) + h_sum[2]
        i_total = wide_of(i_got) + i_sum[0]
        h_got, small, rows_got = together(up_z(low(h_total)), small_sum(2, small), rows_got)
        h_total = wide_of(h_got) + h_sum[3]
        h_got = up_z(low(h_total))
        grad_mixed = wide_of(order(upper, pick(upper, shared[1], shared[0]), rows_got))
        grad_second_in = grad_b + norm_back(mix_unit, mix_factor, gain_mix, grad_mixed)
        packed = small_sum(0, small)[0]
        grad_second_in, h_got, u_got, packed = together(grad_second_in, h_got, u_got, packed)
        h_total = wide_of(h_got) + h_sum[0]
        got = wide_of(core(low(pick(odd, h_total[:, :count], h_total[:, count:]))))
        heads = order(odd, pick(odd, h_total[:, count:], h_total[:, :count]), got, 2, jnp.concatenate)
        query_grad, value_grad = heads[0], heads[1]
        outer_grad = u_sum[0] + wide_of(u_got)
        inner_grad, output_grad = i_total[:, :hidden], i_total[:, hidden:]
    else:
        plan = GroupPlan(fsdp_size, trees)
        coords = jnp.zeros((4,), jnp.int32)

        def gather(shard):
            return lax.all_gather(shard, AXES, axis=0, tiled=True)

        def scatter(total):
            return lax.psum_scatter(wide_of(total), AXES, scatter_dimension=0, tiled=True)

        def own_heads(full):
            return lax.dynamic_slice_in_dim(full, plan.head_group * wide, wide, 1)

        def whole_heads(cols):
            return lax.dynamic_update_slice_in_dim(jnp.zeros((features, features), BF), cols, plan.head_group * wide, 1)

        bias_inner, bias_outer, gain_mix, shift_mix, gain_feed, shift_feed = split(wide_of(gather(joined)))
        q_side = ([own_heads(gather(query_weight))], natural(features, wide))
        v_side = ([own_heads(gather(value_weight))], natural(features, wide))
        o_side = ([gather(output_weight)], natural(features, features))
        i_side = ([gather(inner_weight)], natural(features, hidden))
        tile = min(512, hidden)
        steps = [[(0, (s,), None, tile, (lambda co: co[0] * 0), (0, features))] for s in range(hidden // tile)]
        u_side = ([gather(outer_weight).reshape(-1, tile, features)], steps)
        info, codes_q, codes_k = tables(plan.tree)
        mix_unit, mix_factor = norm_stats(second)
        query_key, value_rows, unit_tree, mixed_tree = project(
            coords, [plan.rows_to_tree(low(mix_unit))[None]], [[lambda co: co[0] * 0]], gain_mix, shift_mix, q_side, v_side, wide
        )
        attended, totals, counts = attend(info, query_key, value_rows, codes_q, codes_k)
        attended_low = flat(plan.heads_to_rows(attended))
        first_out, feed_low = out_project(coords, attended_low, flat(first), gain_feed, shift_feed, o_side)
        active, slope, u_parts = feed_in(
            coords, feed_low, outer_low, bias_inner, i_side, ([(hidden // tile, tile, features)], steps), lambda step, co: step
        )
        second_out, grad_feed, inner_bias_sum, i_parts = feed_out(
            coords,
            feed_low,
            outer_low,
            flat(second),
            bias_outer,
            active,
            slope,
            i_side,
            u_side,
            ([(features, hidden)], natural(features, hidden)),
            lambda step, co: step,
        )
        (grad_first_in, grad_attended, feed_gain_sum, feed_shift_sum), o_parts = out_back(
            coords,
            grad_feed,
            first_out,
            flat(grad_first),
            attended_low,
            gain_feed,
            o_side,
            ([(features, features)], natural(features, features)),
        )
        grad_heads = plan.rows_to_heads(grad_attended.reshape(trees, row_count, features))
        query_low, value_low = attend_back(info, query_key, value_rows, attended, grad_heads, totals, counts)
        form = ([(features, wide)], natural(features, wide))
        (partial, mix_gain_sum, mix_shift_sum), q_parts, v_parts = project_back(
            coords, mixed_tree, unit_tree, query_low, value_low, q_side, v_side, form, form
        )
        grad_mixed = plan.partial_to_rows(partial)
        grad_second_in = grad_b + norm_back(mix_unit, mix_factor, gain_mix, grad_mixed)
        small_sums = [inner_bias_sum, outer_bias_sum, mix_gain_sum, mix_shift_sum, feed_gain_sum, feed_shift_sum]
        packed = scatter(jnp.concatenate([v.reshape(devices, -1) for v in small_sums], axis=1))[0]
        query_grad, value_grad = scatter(whole_heads(q_parts[0])), scatter(whole_heads(v_parts[0]))
        inner_grad, output_grad = scatter(i_parts[0]), scatter(o_parts[0])
        outer_grad = scatter(u_parts[0].reshape(hidden, features))

    pieces = []
    begin = 0
    for size in small_sizes:
        pieces.append(packed[begin:begin + size])
        begin += size
    return (
        first_out.reshape(first_half.shape),
        second_out.reshape(first_half.shape),
        grad_first_in.reshape(first_half.shape),
        grad_second_in[:, None],
        query_grad,
        value_grad,
        output_grad,
        inner_grad,
        pieces[0],
        outer_grad,
        pieces[1],
        pieces[2],
        pieces[3],
        pieces[4],
        pieces[5],
    )


def solution(mesh):
    rows = P(None, "dp", "fsdp", None)
    matrix = P(AXES, None)
    vector = P(AXES)
    weights = (matrix, matrix, matrix, matrix, vector, matrix, vector, vector, vector, vector, vector)
    return jax.shard_map(
        functools.partial(per_device, dp_size=mesh.shape["dp"], fsdp_size=mesh.shape["fsdp"]),
        mesh=mesh,
        in_specs=(rows,) * 4 + weights + (P(None, "dp", None), P(None, "dp", None, None), P(None, "dp", None, None)),
        out_specs=(rows,) * 4 + weights,
        check_vma=False,
    )
```

```python
import functools
import math

import jax
import jax.numpy as jnp
from jax import lax
from jax.experimental import pallas as pl
from jax.experimental.pallas import tpu as pltpu
from jax.sharding import PartitionSpec as P

H = 8
DH = 128
CH = 64
SEG = 128
TRUNK = 4
BRANCHES = 2
NBUCK = 32
SELF_SCORE = -10000.0
NEG_SCORE = -1e30
EPSILON = 1e-06
BF = jnp.bfloat16
F32 = jnp.float32
AXES = ("dp", "fsdp")
GELU_A = math.sqrt(2.0 / math.pi)
GELU_B = 0.044715


def norm_stats(values):
    center = values - jnp.mean(values, axis=-1, keepdims=True)
    factor = lax.rsqrt(jnp.mean(center * center, axis=-1, keepdims=True) + EPSILON)
    return center * factor, factor


def norm_back(unit, factor, gain_vec, grad):
    scaled = grad * gain_vec
    inner = jnp.mean(scaled * unit, axis=-1, keepdims=True)
    return factor * (scaled - jnp.mean(scaled, axis=-1, keepdims=True) - unit * inner)


def position_codes(bucket_rows):
    rounds, tree_len = bucket_rows.shape
    buckets_t = bucket_rows.T
    lanes = jnp.arange(rounds * NBUCK, dtype=jnp.int32)
    member = (jnp.repeat(buckets_t, NBUCK, axis=1) == (lanes % NBUCK)[None, :]).astype(F32)
    rows = jnp.arange(tree_len, dtype=jnp.int32)
    lower = (rows[:, None] >= rows[None, :]).astype(BF)
    ranks = jnp.dot(lower, member.astype(BF), preferred_element_type=F32)
    totals = ranks[-1]
    before = ((lanes[:, None] // NBUCK == lanes[None, :] // NBUCK) & (lanes[:, None] < lanes[None, :])).astype(F32)
    offsets = jnp.sum(totals[:, None] * before, axis=0)
    places = jnp.sum((member * (ranks - 1.0 + offsets[None, :])).reshape(tree_len, rounds, NBUCK), axis=-1)
    return buckets_t.astype(F32) * tree_len + jnp.floor((places + 0.5) / CH)


def seg_parts(seg, info_ref):
    parts = []
    prefix = min(seg, TRUNK) * SEG
    if prefix:
        parts.append((0, prefix, 0, False))
    if seg >= TRUNK + BRANCHES:
        start = pl.multiple_of(info_ref[seg] * SEG, SEG)
        parts.append((start, SEG, TRUNK * SEG, False))
    parts.append((seg * SEG, SEG, (TRUNK + 1) * SEG, True))
    return parts


def unit_rows(rows_f32):
    factor = lax.rsqrt(jnp.mean(rows_f32 * rows_f32, axis=-1, keepdims=True) + EPSILON)
    return rows_f32 * factor * (1.0 / math.sqrt(DH)), factor


def own_diagonal():
    row = lax.broadcasted_iota(jnp.int32, (SEG, SEG), 0)
    col = lax.broadcasted_iota(jnp.int32, (SEG, SEG), 1)
    return row == col


def attention_forward_kernel(segments, rounds, info_ref, q_ref, v_ref, ck_ref, out_ref, total_ref, count_ref, unit_ref):
    head = pl.program_id(0)

    @pl.when(head == 0)
    def _():
        row = lax.broadcasted_iota(jnp.int32, (SEG, SEG), 0)
        col = lax.broadcasted_iota(jnp.int32, (SEG, SEG), 1)
        total_ref[...] = jnp.zeros_like(total_ref)
        for seg in range(segments):
            query = jnp.transpose(ck_ref[:, seg * SEG:(seg + 1) * SEG])
            for start, size, column, own in seg_parts(seg, info_ref):
                for piece in range(size // SEG):
                    first = start + piece * SEG
                    key = ck_ref[:, pl.ds(first, SEG)]
                    counted = jnp.zeros((SEG, SEG), F32)
                    for turn in range(rounds):
                        gap = query[:, turn:turn + 1] - key[turn:turn + 1, :]
                        counted = counted + jnp.where(jnp.abs(gap - 0.5) < 0.75, 1.0, 0.0)
                    if own:
                        counted = jnp.where(row >= col, counted, 0.0)
                    elif column == 0 and seg >= TRUNK:
                        counted = counted * jnp.where(info_ref[segments + seg] >= piece, 1.0, 0.0)
                    begin = column + piece * SEG
                    count_ref[seg * SEG:(seg + 1) * SEG, begin:begin + SEG] = counted.astype(BF)

    unit_ref[...] = unit_rows(q_ref[...].astype(F32))[0].astype(BF)
    diagonal = own_diagonal()
    lane = lax.broadcasted_iota(jnp.int32, (SEG, 128), 1)
    for seg in range(segments):
        rows = slice(seg * SEG, (seg + 1) * SEG)
        query = q_ref[rows, :]
        scored = []
        top = None
        for start, size, column, own in seg_parts(seg, info_ref):
            keys = pl.ds(start, size)
            scores = lax.dot_general(query, unit_ref[keys, :], (((1,), (1,)), ((), ())), preferred_element_type=F32)
            counted = count_ref[rows, column:column + size].astype(F32)
            if own:
                scores = jnp.where(diagonal, SELF_SCORE, scores)
            scores = jnp.where(counted > 0.0, scores, NEG_SCORE)
            best = jnp.max(scores, axis=-1, keepdims=True)
            top = best if top is None else jnp.maximum(top, best)
            scored.append((keys, scores, counted))
        amount = jnp.zeros((SEG, 1), F32)
        result = jnp.zeros((SEG, DH), F32)
        for keys, scores, counted in scored:
            weight = counted * jnp.exp(scores - top)
            amount = amount + jnp.sum(weight, axis=-1, keepdims=True)
            result = result + jnp.dot(weight.astype(BF), v_ref[keys, :], preferred_element_type=F32)
        out_ref[rows, :] = (result / amount).astype(BF)
        total = top + jnp.log(amount)
        total_ref[rows, :] = jnp.where(lane == head, total, total_ref[rows, :])


def attention_backward_kernel(segments, info_ref, q_ref, v_ref, out_ref, grad_ref, total_ref, count_ref, dq_ref, dv_ref, unit_ref, chance_ref, slope_ref, key_acc, value_acc, query_acc):
    head = pl.program_id(0)
    trunk = TRUNK * SEG
    whole = q_ref[...].astype(F32)
    unit, factor = unit_rows(whole)
    unit_ref[...] = unit.astype(BF)

    @pl.when(head == 0)
    def _():
        chance_ref[0:trunk, 0:trunk] = jnp.zeros((trunk, trunk), BF)
        slope_ref[0:trunk, 0:trunk] = jnp.zeros((trunk, trunk), BF)

    diagonal = own_diagonal()
    lane = lax.broadcasted_iota(jnp.int32, (SEG, 128), 1)
    for seg in range(segments):
        rows = slice(seg * SEG, (seg + 1) * SEG)
        query = q_ref[rows, :]
        grad = grad_ref[rows, :]
        total = jnp.sum(jnp.where(lane == head, total_ref[rows, :], 0.0), axis=-1, keepdims=True)
        delta = jnp.sum(grad.astype(F32) * out_ref[rows, :].astype(F32), axis=-1, keepdims=True)
        query_grad = jnp.zeros((SEG, DH), F32)
        for start, size, column, own in seg_parts(seg, info_ref):
            keys = pl.ds(start, size)
            scores = lax.dot_general(query, unit_ref[keys, :], (((1,), (1,)), ((), ())), preferred_element_type=F32)
            counted = count_ref[rows, column:column + size].astype(F32)
            if own:
                scores = jnp.where(diagonal, SELF_SCORE, scores)
            scores = jnp.where(counted > 0.0, scores, NEG_SCORE)
            chance = counted * jnp.exp(scores - total)
            reach = lax.dot_general(grad, v_ref[keys, :], (((1,), (1,)), ((), ())), preferred_element_type=F32)
            slope = chance * (reach - delta)
            if own:
                slope = jnp.where(diagonal, 0.0, slope)
            slope = slope.astype(BF)
            chance_ref[rows, column:column + size] = chance.astype(BF)
            slope_ref[rows, column:column + size] = slope
            query_grad = query_grad + jnp.dot(slope, unit_ref[keys, :], preferred_element_type=F32)
        query_acc[rows, :] = query_grad

    for weight_ref, side_ref, acc in ((chance_ref, grad_ref, value_acc), (slope_ref, q_ref, key_acc)):
        acc[0:trunk, :] = lax.dot_general(weight_ref[:, 0:trunk], side_ref[...], (((0,), (0,)), ((), ())), preferred_element_type=F32)
        for seg in range(segments):
            rows = slice(seg * SEG, (seg + 1) * SEG)
            leaf = seg >= TRUNK + BRANCHES
            begin = trunk if leaf else trunk + SEG
            added = lax.dot_general(weight_ref[rows, begin:trunk + 2 * SEG], side_ref[rows, :], (((0,), (0,)), ((), ())), preferred_element_type=F32)
            if leaf:
                above = pl.ds(pl.multiple_of(info_ref[seg] * SEG, SEG), SEG)
                acc[above, :] += added[0:SEG]
                added = added[SEG:]
            acc[rows, :] = added if seg >= TRUNK else acc[rows, :] + added

    key_grad = key_acc[...]
    along = jnp.mean(key_grad * whole, axis=-1, keepdims=True) * (factor * factor)
    dq_ref[...] = (query_acc[...] + (factor * (1.0 / math.sqrt(DH))) * (key_grad - whole * along)).astype(BF)
    dv_ref[...] = value_acc[...].astype(BF)


def attention_calls(tree_len, local_heads, rounds, segments):
    head_spec = pl.BlockSpec((tree_len, DH), lambda h, info: (0, h))
    side = pl.BlockSpec((tree_len, 128), lambda h, info: (0, 0))
    count_spec = pl.BlockSpec((tree_len, (TRUNK + 2) * SEG), lambda h, info: (0, 0))
    wide = local_heads * DH
    forward = pl.pallas_call(
        functools.partial(attention_forward_kernel, segments, rounds),
        grid_spec=pltpu.PrefetchScalarGridSpec(
            num_scalar_prefetch=1,
            grid=(local_heads,),
            in_specs=[head_spec, head_spec, pl.BlockSpec((8, tree_len), lambda h, info: (0, 0))],
            out_specs=[head_spec, side, count_spec],
            scratch_shapes=[pltpu.VMEM((tree_len, DH), BF)],
        ),
        out_shape=[
            jax.ShapeDtypeStruct((tree_len, wide), BF),
            jax.ShapeDtypeStruct((tree_len, 128), F32),
            jax.ShapeDtypeStruct((tree_len, (TRUNK + 2) * SEG), BF),
        ],
        compiler_params=pltpu.CompilerParams(vmem_limit_bytes=40 << 20),
        cost_estimate=cost(18),
        name="attention_forward",
    )
    backward = pl.pallas_call(
        functools.partial(attention_backward_kernel, segments),
        grid_spec=pltpu.PrefetchScalarGridSpec(
            num_scalar_prefetch=1,
            grid=(local_heads,),
            in_specs=[head_spec, head_spec, head_spec, head_spec, side, count_spec],
            out_specs=[head_spec, head_spec],
            scratch_shapes=[pltpu.VMEM((tree_len, DH), BF)]
            + [pltpu.VMEM((tree_len, (TRUNK + 2) * SEG), BF)] * 2
            + [pltpu.VMEM((tree_len, DH), F32)] * 3,
        ),
        out_shape=[jax.ShapeDtypeStruct((tree_len, wide), BF)] * 2,
        compiler_params=pltpu.CompilerParams(vmem_limit_bytes=40 << 20),
        cost_estimate=cost(21),
        name="attention_backward",
    )
    return forward, backward


def row_block(where_fn, coords_ref, span):
    return pl.ds(pl.multiple_of(where_fn(coords_ref) * span, span), span)


def piece_view(refs, piece):
    view = refs[piece[0]].at[piece[1]] if piece[1] else refs[piece[0]]
    if piece[2] is None:
        return view
    return view.at[pl.ds(piece[2][0], piece[3]), pl.ds(piece[2][1], piece[5][1])]


def whole_view(whole, coords_ref, piece):
    rows = row_block(piece[4], coords_ref, piece[3])
    first = piece[5][0]
    if callable(first):
        first = pl.multiple_of(first(coords_ref) * piece[5][1], piece[5][1])
    return whole.at[rows, pl.ds(first, piece[5][1])]


def load_pieces(coords_ref, refs, pieces, target, sems, first):
    return [
        pltpu.make_async_copy(piece_view(refs, piece), whole_view(target, coords_ref, piece), sems.at[first + number])
        for number, piece in enumerate(pieces)
    ]


def store_pieces(coords_ref, source, refs, pieces, sems, first):
    return [
        pltpu.make_async_copy(whole_view(source, coords_ref, piece), piece_view(refs, piece), sems.at[first + number])
        for number, piece in enumerate(pieces)
    ]


def project_kernel(q_pieces, v_pieces, q_count, v_count, parts, coords_ref, gain_ref, shift_ref, *refs):
    part_refs, refs = refs[:len(parts)], refs[len(parts):]
    q_refs, v_refs = refs[:q_count], refs[q_count:q_count + v_count]
    q_out, v_out, unit_ref, mixed_ref, q_weight, v_weight, sems = refs[q_count + v_count:]
    to_q = load_pieces(coords_ref, q_refs, q_pieces, q_weight, sems, 0)
    to_v = load_pieces(coords_ref, v_refs, v_pieces, v_weight, sems, len(q_pieces))
    for copy in to_q + to_v:
        copy.start()
    for part_ref, places in zip(part_refs, parts):
        for number, place in enumerate(places):
            unit = part_ref[number]
            rows = row_block(place, coords_ref, unit.shape[0])
            unit_ref[rows, :] = unit
            mixed_ref[rows, :] = (unit.astype(F32) * gain_ref[...] + shift_ref[...]).astype(BF)
    for copy in to_q:
        copy.wait()
    q_out[...] = jnp.dot(mixed_ref[...], q_weight[...], preferred_element_type=F32).astype(BF)
    for copy in to_v:
        copy.wait()
    v_out[...] = jnp.dot(mixed_ref[...], v_weight[...], preferred_element_type=F32).astype(BF)


VM = pl.BlockSpec(memory_space=pltpu.VMEM)
ANYWHERE = pl.BlockSpec(memory_space=pl.ANY)


def cost(micros):
    return pl.CostEstimate(flops=int(micros * 1e7), transcendentals=0, bytes_accessed=0)


def kernel_call(body, ins, outs, scratch, name, limit, micros, grid=()):
    return pl.pallas_call(
        body,
        grid_spec=pltpu.PrefetchScalarGridSpec(num_scalar_prefetch=1, grid=grid, in_specs=ins, out_specs=outs[0], scratch_shapes=scratch),
        out_shape=outs[1],
        compiler_params=pltpu.CompilerParams(vmem_limit_bytes=limit << 20),
        cost_estimate=cost(micros),
        name=name,
    )


def project(coords, row_parts, places, gain, shift, q_side, v_side, wide):
    q_arrays, q_pieces = q_side
    v_arrays, v_pieces = v_side
    rows, features = sum(part.shape[0] * part.shape[1] for part in row_parts), gain.shape[1]
    body = functools.partial(project_kernel, q_pieces, v_pieces, len(q_arrays), len(v_arrays), places)
    return kernel_call(
        body,
        [VM] * (2 + len(row_parts)) + [ANYWHERE] * (len(q_arrays) + len(v_arrays)),
        ([VM] * 4, [jax.ShapeDtypeStruct((rows, wide), BF)] * 2 + [jax.ShapeDtypeStruct((rows, features), BF)] * 2),
        [pltpu.VMEM((features, wide), BF)] * 2 + [pltpu.SemaphoreType.DMA((len(q_pieces) + len(v_pieces),))],
        "project",
        50,
        7,
    )(coords, gain, shift, *row_parts, *q_arrays, *v_arrays)


def project_back_kernel(q_pieces, v_pieces, q_count, v_count, q_outs, v_outs, q_made, v_made, coords_ref, mixed_ref, unit_ref, dq_ref, dv_ref, *refs):
    q_refs, v_refs = refs[:q_count], refs[q_count:q_count + v_count]
    rest = refs[q_count + v_count:]
    partial_ref, gain_sum, shift_sum = rest[:3]
    rest = rest[3:]
    q_grads, v_grads = rest[:q_made], rest[q_made:q_made + v_made]
    q_weight, v_weight, q_sum, v_sum, sems = rest[q_made + v_made:]
    to_q = load_pieces(coords_ref, q_refs, q_pieces, q_weight, sems, 0)
    to_v = load_pieces(coords_ref, v_refs, v_pieces, v_weight, sems, len(q_pieces))
    for copy in to_q + to_v:
        copy.start()
    used = len(q_pieces) + len(v_pieces)
    turned = (((0,), (0,)), ((), ()))
    crossed = (((1,), (1,)), ((), ()))
    q_sum[...] = lax.dot_general(mixed_ref[...], dq_ref[...], turned, preferred_element_type=F32).astype(BF)
    from_q = store_pieces(coords_ref, q_sum, q_grads, q_outs, sems, used)
    for copy in from_q:
        copy.start()
    v_sum[...] = lax.dot_general(mixed_ref[...], dv_ref[...], turned, preferred_element_type=F32).astype(BF)
    from_v = store_pieces(coords_ref, v_sum, v_grads, v_outs, sems, used + len(q_outs))
    for copy in from_v:
        copy.start()
    for copy in to_q + to_v:
        copy.wait()
    partial = lax.dot_general(dq_ref[...], q_weight[...], crossed, preferred_element_type=F32) + lax.dot_general(
        dv_ref[...], v_weight[...], crossed, preferred_element_type=F32
    )
    partial_ref[...] = partial.astype(BF)
    gain_sum[...] = jnp.sum(partial * unit_ref[...].astype(F32), axis=0, keepdims=True)
    shift_sum[...] = jnp.sum(partial, axis=0, keepdims=True)
    for copy in from_q + from_v:
        copy.wait()


def project_back(coords, mixed_tree, unit_tree, dq, dv, q_side, v_side, q_form, v_form):
    q_arrays, q_pieces = q_side
    v_arrays, v_pieces = v_side
    q_shapes, q_outs = q_form
    v_shapes, v_outs = v_form
    rows, features = mixed_tree.shape
    wide = dq.shape[1]
    body = functools.partial(
        project_back_kernel, q_pieces, v_pieces, len(q_arrays), len(v_arrays), q_outs, v_outs, len(q_shapes), len(v_shapes)
    )
    made = kernel_call(
        body,
        [VM] * 4 + [ANYWHERE] * (len(q_arrays) + len(v_arrays)),
        (
            [VM] * 3 + [ANYWHERE] * (len(q_shapes) + len(v_shapes)),
            [jax.ShapeDtypeStruct((rows, features), BF)]
            + [jax.ShapeDtypeStruct((1, features), F32)] * 2
            + [jax.ShapeDtypeStruct(s, BF) for s in q_shapes + v_shapes],
        ),
        [pltpu.VMEM((features, wide), BF)] * 4
        + [pltpu.SemaphoreType.DMA((len(q_pieces) + len(v_pieces) + len(q_outs) + len(v_outs),))],
        "project_back",
        50,
        18,
    )(coords, mixed_tree, unit_tree, dq, dv, *q_arrays, *v_arrays)
    return made[:3], made[3:3 + len(q_shapes)], made[3 + len(q_shapes):]


def normalised(values):
    center = values - jnp.mean(values, axis=-1, keepdims=True)
    factor = lax.rsqrt(jnp.mean(center * center, axis=-1, keepdims=True) + EPSILON)
    return center * factor, factor


def out_kernel(pieces, count, coords_ref, att_ref, first_ref, gain_ref, shift_ref, *refs):
    o_refs = refs[:count]
    first_out, feed_out, weight, sems = refs[count:]
    copies = load_pieces(coords_ref, o_refs, pieces, weight, sems, 0)
    for copy in copies:
        copy.start()
    for copy in copies:
        copy.wait()
    made = first_ref[...] + jnp.dot(att_ref[...], weight[...], preferred_element_type=F32)
    first_out[...] = made
    feed_out[...] = (normalised(made)[0] * gain_ref[...] + shift_ref[...]).astype(BF)


def out_project(coords, att, first, gain, shift, side):
    arrays, pieces = side
    rows, features = first.shape
    return kernel_call(
        functools.partial(out_kernel, pieces, len(arrays)),
        [VM] * 4 + [ANYWHERE] * len(arrays),
        ([VM, VM], [jax.ShapeDtypeStruct((rows, features), F32), jax.ShapeDtypeStruct((rows, features), BF)]),
        [pltpu.VMEM((features, features), BF), pltpu.SemaphoreType.DMA((len(pieces),))],
        "out_project",
        50,
        8,
    )(coords, att, first, gain, shift, *arrays)


def out_back_kernel(pieces, count, outs, made, coords_ref, back_ref, first_ref, grad_ref, att_ref, gain_ref, *refs):
    o_refs = refs[:count]
    rest = refs[count:]
    grad_in, grad_att, gain_sum, shift_sum = rest[:4]
    grads = rest[4:4 + made]
    weight, total, sems = rest[4 + made:]
    copies = load_pieces(coords_ref, o_refs, pieces, weight, sems, 0)
    for copy in copies:
        copy.start()
    back = back_ref[...]
    unit, factor = normalised(first_ref[...])
    gain_sum[...] = jnp.sum(back * unit, axis=0, keepdims=True)
    shift_sum[...] = jnp.sum(back, axis=0, keepdims=True)
    scaled = back * gain_ref[...]
    inner = jnp.mean(scaled * unit, axis=-1, keepdims=True)
    value = grad_ref[...] + factor * (scaled - jnp.mean(scaled, axis=-1, keepdims=True) - unit * inner)
    grad_in[...] = value
    low = value.astype(BF)
    total[...] = lax.dot_general(att_ref[...], low, (((0,), (0,)), ((), ())), preferred_element_type=F32).astype(BF)
    stores = store_pieces(coords_ref, total, grads, outs, sems, len(pieces))
    for copy in stores:
        copy.start()
    for copy in copies:
        copy.wait()
    grad_att[...] = lax.dot_general(low, weight[...], (((1,), (1,)), ((), ())), preferred_element_type=F32).astype(BF)
    for copy in stores:
        copy.wait()


def out_back(coords, back, first_out, grad, att, gain, side, form):
    arrays, pieces = side
    shapes, outs = form
    rows, features = back.shape
    full = jax.ShapeDtypeStruct((rows, features), F32)
    line = jax.ShapeDtypeStruct((1, features), F32)
    made = kernel_call(
        functools.partial(out_back_kernel, pieces, len(arrays), outs, len(shapes)),
        [VM] * 5 + [ANYWHERE] * len(arrays),
        (
            [VM] * 4 + [ANYWHERE] * len(shapes),
            [full, jax.ShapeDtypeStruct((rows, features), BF), line, line] + [jax.ShapeDtypeStruct(s, BF) for s in shapes],
        ),
        [pltpu.VMEM((features, features), BF)] * 2 + [pltpu.SemaphoreType.DMA((len(pieces) + len(outs),))],
        "out_back",
        60,
        12,
    )(coords, back, first_out, grad, att, gain, *arrays)
    return made[:4], made[4:]


def feed_in_kernel(plan, counts, coords_ref, feed_ref, grad_ref, bias_ref, *refs):
    pieces, step_outs, block_of = plan
    i_count, made = counts
    i_refs = refs[:i_count]
    active_ref, slope_ref = refs[i_count:i_count + 2]
    grads = refs[i_count + 2:i_count + 2 + made]
    weight, outer_sum, in_sems, out_sems = refs[i_count + 2 + made:]
    step = pl.program_id(0)
    slot = lax.rem(step, 2)
    tile = outer_sum.shape[1]
    count = len(step_outs)

    def store(number):
        return store_pieces(coords_ref, outer_sum.at[number % 2], grads, step_outs[number], out_sems.at[number % 2], 0)

    @pl.when(step == 0)
    def _():
        copies = load_pieces(coords_ref, i_refs, pieces, weight, in_sems, 0)
        for copy in copies:
            copy.start()
        for copy in copies:
            copy.wait()

    for number in range(2, count):

        @pl.when(step == number)
        def _(number=number):
            for copy in store(number - 2):
                copy.wait()

    columns = pl.ds(pl.multiple_of(block_of(step, coords_ref) * tile, tile), tile)
    value = jnp.dot(feed_ref[...], weight[:, columns], preferred_element_type=F32) + bias_ref[:, columns]
    square = value * value
    half = 0.5 + 0.5 * jnp.tanh(value * (GELU_A + GELU_A * GELU_B * square))
    product = value * half
    active = product.astype(BF)
    active_ref[...] = active
    slope_ref[...] = (half + product * (1.0 - half) * (2.0 * GELU_A + 6.0 * GELU_A * GELU_B * square)).astype(BF)
    outer_sum[slot] = lax.dot_general(active, grad_ref[...], (((0,), (0,)), ((), ())), preferred_element_type=F32).astype(BF)

    for number in range(count):

        @pl.when(step == number)
        def _(number=number):
            for copy in store(number):
                copy.start()
            if number == count - 1:
                for last in range(max(0, number - 1), count):
                    for copy in store(last):
                        copy.wait()


def feed_in(coords, feed, grad, bias, side, form, block_of):
    arrays, pieces = side
    shapes, step_outs = form
    rows, features = feed.shape
    hidden = bias.shape[1]
    tile = hidden // len(step_outs)
    most = max(len(outs) for outs in step_outs)
    block = pl.BlockSpec((rows, tile), lambda j, co: (0, block_of(j, co)))
    made = kernel_call(
        functools.partial(feed_in_kernel, (pieces, step_outs, block_of), (len(arrays), len(shapes))),
        [VM] * 3 + [ANYWHERE] * len(arrays),
        (
            [block, block] + [ANYWHERE] * len(shapes),
            [jax.ShapeDtypeStruct((rows, hidden), BF)] * 2 + [jax.ShapeDtypeStruct(s, BF) for s in shapes],
        ),
        [
            pltpu.VMEM((features, hidden), BF),
            pltpu.VMEM((2, tile, features), BF),
            pltpu.SemaphoreType.DMA((len(pieces),)),
            pltpu.SemaphoreType.DMA((2, most)),
        ],
        "feed_in",
        60,
        29,
        grid=(len(step_outs),),
    )(coords, feed, grad, bias, *arrays)
    return made[0], made[1], made[2:]


def feed_out_kernel(plan, counts, coords_ref, feed_ref, grad_ref, base_ref, bias_ref, active_ref, slope_ref, *refs):
    i_pieces, i_outs, steps, block_of = plan
    i_count, u_count, made = counts
    i_refs, u_refs = refs[:i_count], refs[i_count:i_count + u_count]
    rest = refs[i_count + u_count:]
    out_ref, back_ref, bias_sum = rest[:3]
    grads = rest[3:3 + made]
    weight, weight_sum, outer, low_ref, i_sems, u_sems, out_sems = rest[3 + made:]
    step = pl.program_id(0)
    slot = lax.rem(step, 2)
    tile = outer.shape[1]
    count = len(steps)

    def u_load(number):
        return load_pieces(coords_ref, u_refs, steps[number], outer.at[number % 2], u_sems.at[number % 2], 0)

    @pl.when(step == 0)
    def _():
        copies = load_pieces(coords_ref, i_refs, i_pieces, weight, i_sems, 0)
        for copy in u_load(0) + copies:
            copy.start()
        out_ref[...] = base_ref[...] + bias_ref[...]
        back_ref[...] = jnp.zeros_like(back_ref)
        for copy in copies:
            copy.wait()

    for number in range(count):

        @pl.when(step == number)
        def _(number=number):
            if number + 1 < count:
                for copy in u_load(number + 1):
                    copy.start()
            for copy in u_load(number):
                copy.wait()

    columns = pl.ds(pl.multiple_of(block_of(step, coords_ref) * tile, tile), tile)
    pulled = lax.dot_general(grad_ref[...], outer[slot], (((1,), (1,)), ((), ())), preferred_element_type=F32)
    inner_low = (pulled * slope_ref[...].astype(F32)).astype(BF)
    bias_sum[:, columns] = jnp.sum(inner_low.astype(F32), axis=0, keepdims=True)
    weight_sum[:, columns] = lax.dot_general(feed_ref[...], inner_low, (((0,), (0,)), ((), ())), preferred_element_type=F32).astype(BF)
    low_ref[...] = inner_low
    out_ref[...] += jnp.dot(active_ref[...], outer[slot], preferred_element_type=F32)
    back_ref[...] += lax.dot_general(low_ref[...], weight[:, columns], (((1,), (1,)), ((), ())), preferred_element_type=F32)

    @pl.when(step == count - 1)
    def _():
        copies = store_pieces(coords_ref, weight_sum, grads, i_outs, out_sems, 0)
        for copy in copies:
            copy.start()
        for copy in copies:
            copy.wait()


def feed_out(coords, feed, grad, base, bias, active, slope, i_side, u_side, i_form, block_of):
    i_arrays, i_pieces = i_side
    u_arrays, steps = u_side
    shapes, i_outs = i_form
    rows, features = feed.shape
    hidden = active.shape[1]
    tile = hidden // len(steps)
    most = max(len(pieces) for pieces in steps)
    block = pl.BlockSpec((rows, tile), lambda j, co: (0, block_of(j, co)))
    made = kernel_call(
        functools.partial(feed_out_kernel, (i_pieces, i_outs, steps, block_of), (len(i_arrays), len(u_arrays), len(shapes))),
        [VM] * 4 + [block, block] + [ANYWHERE] * (len(i_arrays) + len(u_arrays)),
        (
            [VM] * 3 + [ANYWHERE] * len(shapes),
            [jax.ShapeDtypeStruct((rows, features), F32)] * 2
            + [jax.ShapeDtypeStruct((1, hidden), F32)]
            + [jax.ShapeDtypeStruct(s, BF) for s in shapes],
        ),
        [
            pltpu.VMEM((features, hidden), BF),
            pltpu.VMEM((features, hidden), BF),
            pltpu.VMEM((2, tile, features), BF),
            pltpu.VMEM((rows, tile), BF),
            pltpu.SemaphoreType.DMA((len(i_pieces),)),
            pltpu.SemaphoreType.DMA((2, most)),
            pltpu.SemaphoreType.DMA((len(i_outs),)),
        ],
        "feed_out",
        60,
        40,
        grid=(len(steps),),
    )(coords, feed, grad, base, bias, active, slope, *i_arrays, *u_arrays)
    return made[0], made[1], made[2], made[3:]


def pick(flag, when_true, when_false):
    return jnp.where(flag, when_true, when_false)


def after(value, *earlier):
    return lax.optimization_barrier((value,) + earlier)[0]


class GroupPlan:
    def __init__(self, size, trees):
        me = lax.axis_index("fsdp")
        self.size = size
        self.trees = trees
        self.group = size // trees
        self.tree = me // self.group
        self.head_group = me % self.group
        self.me = me

    def rows_to_tree(self, rows):
        every = lax.all_gather(rows, "fsdp", axis=1, tiled=True)
        return lax.dynamic_index_in_dim(every, self.tree, 0, False)

    def heads_to_rows(self, heads):
        count = heads.shape[0] // self.size
        every = lax.all_gather(heads, "fsdp", axis=0, tiled=False)
        mine = lax.dynamic_slice_in_dim(every, self.me * count, count, 1)
        mine = mine.reshape(self.trees, self.group, count, heads.shape[1])
        return jnp.moveaxis(mine, 1, 2).reshape(self.trees, count, -1)

    def rows_to_heads(self, rows):
        wide = rows.shape[2] // self.group
        whole = self.rows_to_tree(rows)
        return lax.dynamic_slice_in_dim(whole, self.head_group * wide, wide, 1)

    def partial_to_rows(self, partial):
        every = jnp.zeros((self.trees,) + partial.shape, F32)
        every = lax.dynamic_update_index_in_dim(every, partial.astype(F32), self.tree, 0)
        return lax.psum_scatter(every, "fsdp", scatter_dimension=1, tiled=True)


def low(value):
    return value.astype(BF)


def wide_of(value):
    return value.astype(F32)


def swap_pairs(size, bit):
    return [(i, i ^ bit) for i in range(size)]


def natural(rows, columns):
    return [(0, (), None, rows, (lambda co: co[0] * 0), (0, columns))]


def swap_pairs(size, bit):
    return [(i, i ^ bit) for i in range(size)]


def core(value):
    return lax.ppermute(value, "fsdp", swap_pairs(4, 1))


def over_y(value):
    return lax.ppermute(value, "fsdp", swap_pairs(4, 2))


def over_x(value):
    return lax.ppermute(value, "dp", swap_pairs(8, 1))


def up_z(value):
    return lax.ppermute(value, "dp", [(i, (i + 2) % 8) for i in range(8)])


def bit_move(bit, value):
    if bit < 2:
        return lax.ppermute(value, "fsdp", swap_pairs(4, 1 << bit))
    return lax.ppermute(value, "dp", swap_pairs(8, 1 << (bit - 2)))


def place32(k, rx, ry, rc):
    return lambda co: ((((co[0] + 4 - k) & 3) * 2 + (co[1] ^ rx)) * 2 + (co[2] ^ ry)) * 2 + (co[3] ^ rc)


def place16(k, rx, ry):
    return lambda co: (((co[0] + 4 - k) & 3) * 2 + (co[1] ^ rx)) * 2 + (co[2] ^ ry)


def place8(rx, ry, rc):
    return lambda co: ((co[1] ^ rx) * 2 + (co[2] ^ ry)) * 2 + (co[3] ^ rc)


def hidden_block(step, co):
    return (co[0] + 4 - step) & 3


def heads_pieces(which, rows, half):
    pieces = []
    for outer in range(2):
        for inner in range(2):
            for k in range(4):
                rx, ry = (outer, inner) if which == 0 else (inner, outer)
                pieces.append((outer, (inner, k), None, rows, place16(k, rx, ry), (0, half)))
    return pieces


def output_in_pieces(rows, half):
    pieces = []
    for rc in range(2):
        for rx in range(2):
            for ry in range(2):
                for k in range(4):
                    columns = ((lambda co, rc=rc: co[3] ^ rc), half)
                    pieces.append((rc * 2 + rx, (ry, k), None, rows, place16(k, rx, ry), columns))
    return pieces


def output_out_pieces(count, features):
    pieces = []
    for rc in range(2):
        for ry in range(2):
            for rx in range(2):
                for k in range(4):
                    pieces.append((rc * 2 + ry, (rx, k), None, count, place32(k, rx, ry, rc), (0, features)))
    return pieces


def inner_pieces(count, hidden, cut):
    pieces = []
    for part in range(2):
        for rc in range(2):
            for outer in range(2):
                for inner in range(2):
                    for k in range(4):
                        rx, ry = (outer, inner) if part == 0 else (inner, outer)
                        columns = (0, cut) if part == 0 else (cut, hidden - cut)
                        pieces.append((rc * 4 + part * 2 + outer, (inner, k), None, count, place32(k, rx, ry, rc), columns))
    return pieces


def outer_steps(count, features):
    return [
        [
            (rc * 4 + k, (rx, ry), None, count, place8(rx, ry, rc), (0, features))
            for rx in range(2)
            for ry in range(2)
            for rc in range(2)
        ]
        for k in range(4)
    ]


def together(*values):
    return lax.optimization_barrier(values)


def join_vectors(parts):
    total = sum(part.shape[0] for part in parts)
    made, begin = 0.0, 0
    for part in parts:
        made = made + jnp.pad(wide_of(part), (begin, total - begin - part.shape[0]))
        begin += part.shape[0]
    return low(made)


def per_device(
    first_half,
    second_half,
    grad_first,
    grad_second,
    query_weight,
    value_weight,
    output_weight,
    inner_weight,
    inner_bias,
    outer_weight,
    outer_bias,
    mixer_gain,
    mixer_shift,
    feed_gain,
    feed_shift,
    parents,
    buckets,
    order,
    *,
    dp_size,
    fsdp_size,
):
    trees = first_half.shape[0]
    row_count = first_half.shape[2]
    features = first_half.shape[3]
    hidden = inner_weight.shape[1]
    rounds = buckets.shape[2]
    tree_len = buckets.shape[3]
    segments = parents.shape[2]
    all_rows = trees * row_count
    devices = dp_size * fsdp_size
    small_parts = (inner_bias, outer_bias, mixer_gain, mixer_shift, feed_gain, feed_shift)
    small_sizes = [v.shape[0] for v in small_parts]
    small_count = sum(small_sizes)

    first = first_half[:, 0]
    second = second_half[:, 0]
    grad_b = grad_second[:, 0]
    joined = join_vectors(small_parts)[None]

    def flat(value):
        return value.reshape(all_rows, features)

    def split(small):
        vectors, begin = [], 0
        for size in small_sizes:
            vectors.append(small[:, begin:begin + size].reshape(1, -1))
            begin += size
        return vectors

    def tables(tree, *earlier):
        parent_row = lax.dynamic_index_in_dim(after(parents, *earlier)[:, 0], tree, 0, False)
        bucket_rows = lax.dynamic_index_in_dim(after(buckets, *earlier)[:, 0], tree, 0, False)
        branch = parent_row[jnp.clip(parent_row, 0, segments - 1)]
        trunk_end = jnp.where(jnp.arange(segments) >= TRUNK + BRANCHES, branch, parent_row)
        codes = position_codes(bucket_rows)
        return (
            jnp.concatenate([parent_row, trunk_end]),
            jnp.pad(codes.T, ((0, 8 - rounds), (0, 0))),
        )

    local_heads = H // (fsdp_size // trees)
    wide = local_heads * DH
    attend, attend_back = attention_calls(tree_len, local_heads, rounds, segments)
    outer_low = flat(low(grad_b))
    outer_bias_sum = jnp.sum(wide_of(outer_low), axis=0)

    if (dp_size, fsdp_size, trees) == (8, 4, 2):
        dp, fsdp = lax.axis_index("dp"), lax.axis_index("fsdp")
        bits = [fsdp % 2, fsdp // 2, dp % 2, dp // 2 % 2, dp // 4]
        coords = jnp.stack([dp // 2, dp % 2, fsdp // 2, fsdp % 2]).astype(jnp.int32)
        odd, upper, tree = fsdp % 2 == 1, fsdp // 2 == 1, fsdp // 2
        count, half, cut = query_weight.shape[0], features // 2, hidden * 11 // 16
        outer_count = outer_weight.shape[0]

        def order(flag, one, other, axis=0, join=jnp.stack):
            return join([pick(flag, other, one), pick(flag, one, other)], axis=axis)

        def small_step(bit, made):
            return order(bits[bit] == 1, made, bit_move(bit, made), 0, jnp.concatenate)

        both = jnp.stack([query_weight, value_weight, output_weight])
        got, small_got = together(core(pick(odd, both[:, :, :half], both[:, :, half:])), bit_move(0, joined))
        chip = order(odd, pick(odd, both[:, :, half:], both[:, :, :half]), got, 1, jnp.concatenate)
        small = order(odd, joined, small_got, 0, jnp.concatenate)
        mix_unit, mix_factor = norm_stats(after(second, chip))
        ring_got, small, unit_low = together(up_z(chip), small_step(1, small), low(mix_unit))
        ring = [chip, ring_got]
        rows_mine = pick(upper, unit_low[1], unit_low[0])
        rows_got = over_y(pick(upper, unit_low[0], unit_low[1]))
        u_near = jnp.stack([outer_weight, over_y(after(outer_weight, chip))])
        ring_got, small = together(up_z(ring_got), small_step(3, small_step(2, small)))
        ring.append(ring_got)
        u_got = over_x(u_near)
        ring_got, small, u_got, rows_got = together(up_z(ring_got), small_step(4, small), u_got, rows_got)
        ring.append(ring_got)
        q_near, v_near = (jnp.stack([r[which] for r in ring]) for which in range(2))
        i_got = up_z(after(inner_weight, ring_got))
        pair = order(upper, rows_mine, rows_got)
        q_got, v_got, pair_got = together(over_y(q_near), over_x(v_near), core(pair))
        i_ring = [inner_weight, i_got]
        q_near, v_near = jnp.stack([q_near, q_got]), jnp.stack([v_near, v_got])
        info, codes_k = tables(tree, pair_got)
        bias_inner, bias_outer, gain_mix, shift_mix, gain_feed, shift_feed = split(wide_of(small))
        o_near = jnp.stack([r[2] for r in ring[:3]] + [after(ring[3], pair_got)[2]])
        u_plane = jnp.stack([u_near, after(u_got, pair_got)])
        q_got, v_got, i_got, codes_k, o_near, u_plane = together(
            over_x(q_near), over_y(v_near), up_z(after(i_got, pair_got)), codes_k, o_near, u_plane
        )
        i_ring.append(i_got)
        q_side = ([q_near, q_got], heads_pieces(0, 2 * count, half))
        v_side = ([v_near, v_got], heads_pieces(1, 2 * count, half))

        places = [[(lambda co, y=y, rc=rc: 2 * y + (co[3] ^ rc)) for y in range(2)] for rc in range(2)]
        made = project(coords, [pair, pair_got], places, gain_mix, shift_mix, q_side, v_side, wide)
        query_key, value_rows, unit_tree, mixed_tree, i_got, o_got = together(*made, up_z(i_got), over_y(o_near))
        i_ring.append(i_got)
        u_ring = [u_plane, up_z(after(u_plane, i_got))]

        a_near = jnp.stack([r[:, :cut] for r in i_ring])
        b_near = jnp.stack([r[:, cut:] for r in i_ring])
        o_near = jnp.stack([o_near, o_got])
        attended, totals, counts = attend(info, query_key, value_rows, codes_k)
        attended, totals, counts, a_got, b_got, o_got, u_got = together(
            attended, totals, counts, over_y(a_near), over_x(b_near), over_x(o_near), u_ring[1]
        )
        u_ring[1] = u_got
        blocks = attended.reshape(2, 2, row_count, wide)
        got = core(pick(odd, blocks[:, 0], blocks[:, 1]))
        heads = order(odd, pick(odd, blocks[:, 1], blocks[:, 0]), got, 2, jnp.concatenate)
        mine, other = pick(upper, heads[1], heads[0]), pick(upper, heads[0], heads[1])
        mine, other = together(mine, other)
        a_near = jnp.stack([a_near, after(a_got, other)])
        a_got = over_x(a_near)
        b_near = jnp.stack([b_near, after(b_got, other)])
        u_next = up_z(after(u_got, other))
        got, o_core, o_core_got = together(over_y(other), core(o_near), core(o_got))
        attended_low = flat(order(upper, mine, got))
        o_side = ([o_near, o_got, o_core, o_core_got], output_in_pieces(2 * count, half))

        b_got = over_y(after(b_near, got))
        first_out, feed_low = out_project(coords, attended_low, flat(first), gain_feed, shift_feed, o_side)
        first_out, feed_low, a_got, b_got, a_core, b_core, u_got = together(
            first_out, feed_low, a_got, b_got, core(a_near), core(b_near), u_next
        )
        feed_low, a_core_got, b_core_got = together(feed_low, core(a_got), core(b_got))
        i_side = (
            [a_near, a_got, b_near, b_got, a_core, a_core_got, b_core, b_core_got],
            inner_pieces(count, hidden, cut),
        )
        u_ring += [u_got, up_z(u_got)]

        u_form = ([(2, 2, outer_count, features)] * 8, outer_steps(outer_count, features))
        active, slope, u_parts = feed_in(coords, feed_low, outer_low, bias_inner, i_side, u_form, hidden_block)
        u_cores = [core(u) for u in u_ring[:3]]
        made = together(active, slope, u_ring[3], *u_cores, *u_parts)
        active, slope, u_ring[3] = made[:3]
        u_cores, u_parts = list(made[3:6]), made[6:]
        sent = low(wide_of(u_parts[1]) + wide_of(core(u_parts[5])))
        sent, u_core, active = together(sent, core(u_ring[3]), active)
        u_side = (u_ring + u_cores + [u_core], outer_steps(outer_count, features))

        i_form = (([(2, 4, count, cut)] * 2 + [(2, 4, count, hidden - cut)] * 2) * 2, inner_pieces(count, hidden, cut))
        second_out, grad_feed, inner_bias_sum, i_parts = feed_out(
            coords, feed_low, outer_low, flat(second), bias_outer, active, slope, i_side, u_side, i_form, hidden_block
        )
        made = together(second_out, grad_feed, inner_bias_sum, up_z(sent), *[core(u_parts[4 + k]) for k in (2, 3, 0)], *i_parts)
        second_out, grad_feed, inner_bias_sum, u_got = made[:4]
        u_shares = [wide_of(u_parts[k]) + wide_of(c) for k, c in zip((2, 3, 0), made[4:7])]
        i_parts = made[7:]
        sent = low(wide_of(u_got) + u_shares[0])
        sent, grad_feed = together(sent, grad_feed)
        u_first = up_z(sent[0])
        o_form = ([(2, 4, count, features)] * 4, output_out_pieces(count, features))
        (grad_first_in, grad_attended, feed_gain_sum, feed_shift_sum), o_parts = out_back(
            coords, grad_feed, first_out, flat(grad_first), attended_low, gain_feed, o_side, o_form
        )
        made = together(grad_first_in, grad_attended, u_first, *[core(part) for part in i_parts[4:]], *o_parts)
        grad_first_in, grad_attended, u_first = made[:3]
        i_cores, o_parts = made[3:7], made[7:]
        a_keep, a_sent = (wide_of(i_parts[which]) + wide_of(i_cores[which]) for which in range(2))
        rows = grad_attended.reshape(trees, row_count, features)
        mine, other = together(pick(upper, rows[1], rows[0]), pick(upper, rows[0], rows[1]))
        a_got = over_x(after(low(a_sent), other))
        got, u_second = together(over_y(other), up_z(after(sent, other)[1]))
        pair = order(upper, mine, got)
        got = core(pick(odd, pair[..., :half], pair[..., half:]))
        grad_heads = order(odd, pick(odd, pair[..., half:], pair[..., :half]), got, 1).reshape(tree_len, half)
        grad_heads, o_core, o_core_sent = together(grad_heads, core(after(o_parts[2], pair)), core(after(o_parts[3], pair)))
        u_got = jnp.stack([u_first, u_second])
        small_sums = [inner_bias_sum, outer_bias_sum, None, None, feed_gain_sum, feed_shift_sum]

        def spread(values):
            made, begin = 0.0, 0
            for size, value in zip(small_sizes, values):
                if value is not None:
                    made = made + jnp.pad(value.reshape(devices, size), ((0, 0), (begin, small_count - begin - size)))
                begin += size
            return made

        small = spread(small_sums)
        b_keep, b_sent = (
            jnp.concatenate([wide_of(i_parts[2 + w]) + wide_of(i_cores[2 + w]), wide_of(o_parts[w]) + wide_of(c)], axis=3)
            for w, c in ((0, o_core), (1, o_core_sent))
        )

        sent, b_sent, grad_heads, small = together(low(wide_of(u_got) + u_shares[1]), low(b_sent), grad_heads, small)
        query_low, value_low = attend_back(info, query_key, value_rows, attended, grad_heads, totals, counts)
        query_low, value_low, u_got, a_got, b_got = together(query_low, value_low, up_z(sent), a_got, over_y(b_sent))
        a_keep, b_keep = a_keep + wide_of(a_got), b_keep + wide_of(b_got)
        a_sent, b_sent, query_low = together(low(a_keep[1]), low(b_keep[1]), query_low)
        q_form = ([(2, 4, 2 * count, half)] * 2, heads_pieces(0, 2 * count, half))
        v_form = ([(2, 4, 2 * count, half)] * 2, heads_pieces(1, 2 * count, half))
        (partial, mix_gain_sum, mix_shift_sum), q_parts, v_parts = project_back(
            coords, mixed_tree, unit_tree, query_low, value_low, q_side, v_side, q_form, v_form
        )
        made = together(partial, mix_gain_sum, mix_shift_sum, over_y(a_sent), over_x(b_sent), *q_parts, *v_parts)
        partial, mix_gain_sum, mix_shift_sum, a_got, b_got, q_keep, q_sent, v_keep, v_sent = made

        small = small + spread([None, None, mix_gain_sum, mix_shift_sum, None, None])

        def small_sum(bit, made, axis=0):
            one = bits[bit] == 1
            if axis:
                pairs = made.reshape(2, 2, -1, made.shape[-1])
                lower, higher = pairs[:, 0].reshape(-1, made.shape[-1]), pairs[:, 1].reshape(-1, made.shape[-1])
            else:
                middle = made.shape[0] // 2
                lower, higher = made[:middle], made[middle:]
            return pick(one, higher, lower) + bit_move(bit, pick(one, lower, higher))

        i_sum = jnp.concatenate([a_keep[0] + wide_of(a_got), b_keep[0] + wide_of(b_got)], axis=2)
        q_got, v_got, i_got, small = together(over_x(q_sent), over_y(v_sent), up_z(low(i_sum[1])), small_sum(4, small))
        u_sum = wide_of(after(u_got, q_got)) + u_shares[2]
        u_got = over_x(low(u_sum[1]))
        q_sum, v_sum = wide_of(q_keep) + wide_of(q_got), wide_of(v_keep) + wide_of(v_got)
        i_total = wide_of(i_got) + i_sum[2]
        blocks = partial.reshape(2, 2, row_count, features)
        got = core(pick(odd, blocks[:, 0], blocks[:, 1]))
        q_got, v_got, i_got, small, got = together(
            over_y(low(q_sum[1])), over_x(low(v_sum[1])), up_z(low(i_total)), small_sum(3, small), got
        )
        shared = low(wide_of(pick(odd, blocks[:, 1], blocks[:, 0])) + wide_of(got))
        h_sum = jnp.stack([q_sum[0] + wide_of(q_got), v_sum[0] + wide_of(v_got)], axis=1)
        i_total = wide_of(i_got) + i_sum[3]
        rows_got = over_y(pick(upper, shared[0], shared[1]))
        h_got, i_got, small, u_got = together(up_z(low(h_sum[1])), up_z(low(i_total)), small_sum(1, small, 1), u_got)
        u_sum = u_sum[0] + wide_of(u_got)
        u_got = over_y(low(u_sum[1]))
        h_total = wide_of(h_got) + h_sum[2]
        i_total = wide_of(i_got) + i_sum[0]
        h_got, small, rows_got = together(up_z(low(h_total)), small_sum(2, small), rows_got)
        h_total = wide_of(h_got) + h_sum[3]
        h_got = up_z(low(h_total))
        grad_mixed = wide_of(order(upper, pick(upper, shared[1], shared[0]), rows_got))
        grad_second_in = grad_b + norm_back(mix_unit, mix_factor, gain_mix, grad_mixed)
        packed = small_sum(0, small)[0]
        grad_second_in, h_got, u_got, packed = together(grad_second_in, h_got, u_got, packed)
        h_total = wide_of(h_got) + h_sum[0]
        got = wide_of(core(low(pick(odd, h_total[:, :count], h_total[:, count:]))))
        heads = order(odd, pick(odd, h_total[:, count:], h_total[:, :count]), got, 2, jnp.concatenate)
        query_grad, value_grad = heads[0], heads[1]
        outer_grad = u_sum[0] + wide_of(u_got)
        inner_grad, output_grad = i_total[:, :hidden], i_total[:, hidden:]
    else:
        plan = GroupPlan(fsdp_size, trees)
        coords = jnp.zeros((4,), jnp.int32)

        def gather(shard):
            return lax.all_gather(shard, AXES, axis=0, tiled=True)

        def scatter(total):
            return lax.psum_scatter(wide_of(total), AXES, scatter_dimension=0, tiled=True)

        def own_heads(full):
            return lax.dynamic_slice_in_dim(full, plan.head_group * wide, wide, 1)

        def whole_heads(cols):
            return lax.dynamic_update_slice_in_dim(jnp.zeros((features, features), BF), cols, plan.head_group * wide, 1)

        bias_inner, bias_outer, gain_mix, shift_mix, gain_feed, shift_feed = split(wide_of(gather(joined)))
        q_side = ([own_heads(gather(query_weight))], natural(features, wide))
        v_side = ([own_heads(gather(value_weight))], natural(features, wide))
        o_side = ([gather(output_weight)], natural(features, features))
        i_side = ([gather(inner_weight)], natural(features, hidden))
        tile = min(512, hidden)
        steps = [[(0, (s,), None, tile, (lambda co: co[0] * 0), (0, features))] for s in range(hidden // tile)]
        u_side = ([gather(outer_weight).reshape(-1, tile, features)], steps)
        info, codes_k = tables(plan.tree)
        mix_unit, mix_factor = norm_stats(second)
        query_key, value_rows, unit_tree, mixed_tree = project(
            coords, [plan.rows_to_tree(low(mix_unit))[None]], [[lambda co: co[0] * 0]], gain_mix, shift_mix, q_side, v_side, wide
        )
        attended, totals, counts = attend(info, query_key, value_rows, codes_k)
        attended_low = flat(plan.heads_to_rows(attended))
        first_out, feed_low = out_project(coords, attended_low, flat(first), gain_feed, shift_feed, o_side)
        active, slope, u_parts = feed_in(
            coords, feed_low, outer_low, bias_inner, i_side, ([(hidden // tile, tile, features)], steps), lambda step, co: step
        )
        second_out, grad_feed, inner_bias_sum, i_parts = feed_out(
            coords,
            feed_low,
            outer_low,
            flat(second),
            bias_outer,
            active,
            slope,
            i_side,
            u_side,
            ([(features, hidden)], natural(features, hidden)),
            lambda step, co: step,
        )
        (grad_first_in, grad_attended, feed_gain_sum, feed_shift_sum), o_parts = out_back(
            coords,
            grad_feed,
            first_out,
            flat(grad_first),
            attended_low,
            gain_feed,
            o_side,
            ([(features, features)], natural(features, features)),
        )
        grad_heads = plan.rows_to_heads(grad_attended.reshape(trees, row_count, features))
        query_low, value_low = attend_back(info, query_key, value_rows, attended, grad_heads, totals, counts)
        form = ([(features, wide)], natural(features, wide))
        (partial, mix_gain_sum, mix_shift_sum), q_parts, v_parts = project_back(
            coords, mixed_tree, unit_tree, query_low, value_low, q_side, v_side, form, form
        )
        grad_mixed = plan.partial_to_rows(partial)
        grad_second_in = grad_b + norm_back(mix_unit, mix_factor, gain_mix, grad_mixed)
        small_sums = [inner_bias_sum, outer_bias_sum, mix_gain_sum, mix_shift_sum, feed_gain_sum, feed_shift_sum]
        packed = scatter(jnp.concatenate([v.reshape(devices, -1) for v in small_sums], axis=1))[0]
        query_grad, value_grad = scatter(whole_heads(q_parts[0])), scatter(whole_heads(v_parts[0]))
        inner_grad, output_grad = scatter(i_parts[0]), scatter(o_parts[0])
        outer_grad = scatter(u_parts[0].reshape(hidden, features))

    pieces = []
    begin = 0
    for size in small_sizes:
        pieces.append(packed[begin:begin + size])
        begin += size
    return (
        first_out.reshape(first_half.shape),
        second_out.reshape(first_half.shape),
        grad_first_in.reshape(first_half.shape),
        grad_second_in[:, None],
        query_grad,
        value_grad,
        output_grad,
        inner_grad,
        pieces[0],
        outer_grad,
        pieces[1],
        pieces[2],
        pieces[3],
        pieces[4],
        pieces[5],
    )


def solution(mesh):
    rows = P(None, "dp", "fsdp", None)
    matrix = P(AXES, None)
    vector = P(AXES)
    weights = (matrix, matrix, matrix, matrix, vector, matrix, vector, vector, vector, vector, vector)
    return jax.shard_map(
        functools.partial(per_device, dp_size=mesh.shape["dp"], fsdp_size=mesh.shape["fsdp"]),
        mesh=mesh,
        in_specs=(rows,) * 4 + weights + (P(None, "dp", None), P(None, "dp", None, None), P(None, "dp", None, None)),
        out_specs=(rows,) * 4 + weights,
        check_vma=False,
    )
```
